32 devices in a mesh: dp: 16 (over z, y, x), tensor: 2 (over core).
Axes of the slice: x: 2, y: 2, z: 4, core: 2. Of those that a mesh axis runs over, the one named last changes fastest.
Arguments:
- tokens: bfloat16 [16384, 1024], P('dp'), may hold values from -6 to 6
- cotangent: bfloat16 [16384, 1024], P('dp'), may hold values from -6 to 6
- segment_ids: int32 [32, 512], P('dp'), may hold values from 0 to 5, never falling along the last dimension, each value on 1 to 200 neighbouring positions
- adapter_ids: int32 [32], P('dp'), may hold values from 0 to 7, as said below
- query_weight: bfloat16 [1024, 1024], P(None, 'tensor'), may hold values from -0.1875 to 0.1875
- key_weight: bfloat16 [1024, 1024], P(None, 'tensor'), may hold values from -0.1875 to 0.1875
- value_weight: bfloat16 [1024, 1024], P(None, 'tensor'), may hold values from -0.1875 to 0.1875
- output_weight: bfloat16 [1024, 1024], P('tensor'), may hold values from -0.75 to 0.75
- expand_weight: bfloat16 [1024, 4096], P(None, 'tensor'), may hold values from -0.1875 to 0.1875
- contract_weight: bfloat16 [4096, 1024], P('tensor'), may hold values from -0.09375 to 0.09375
- first_gain: float32 [1024], replicated, may hold values from 0.5 to 1.5
- first_shift: float32 [1024], replicated, may hold values from -3 to 3
- second_gain: float32 [1024], replicated, may hold values from 0.5 to 1.5
- second_shift: float32 [1024], replicated, may hold values from -3 to 3
- query_down: bfloat16 [8, 1024, 16], replicated, may hold values from -0.1875 to 0.1875
- query_up: bfloat16 [8, 16, 1024], P(None, None, 'tensor'), may hold values from -1.5 to 1.5
- key_down: bfloat16 [8, 1024, 16], replicated, may hold values from -0.1875 to 0.1875
- key_up: bfloat16 [8, 16, 1024], P(None, None, 'tensor'), may hold values from -1.5 to 1.5
- value_down: bfloat16 [8, 1024, 16], replicated, may hold values from -0.1875 to 0.1875
- value_up: bfloat16 [8, 16, 1024], P(None, None, 'tensor'), may hold values from -1.5 to 1.5
- output_down: bfloat16 [8, 1024, 16], P(None, 'tensor'), may hold values from -0.75 to 0.75
- output_up: bfloat16 [8, 16, 1024], replicated, may hold values from -1.5 to 1.5
- expand_down: bfloat16 [8, 1024, 16], replicated, may hold values from -0.1875 to 0.1875
- expand_up: bfloat16 [8, 16, 4096], P(None, None, 'tensor'), may hold values from -1.5 to 1.5
- contract_down: bfloat16 [8, 4096, 16], P(None, 'tensor'), may hold values from -0.09375 to 0.09375
- contract_up: bfloat16 [8, 16, 1024], replicated, may hold values from -1.5 to 1.5
Outputs:
- layer_output: bfloat16 [16384, 1024], P('dp')
- input_gradient: bfloat16 [16384, 1024], P('dp')
- gradient_query_down: float32 [8, 1024, 16], replicated
- gradient_query_up: float32 [8, 16, 1024], P(None, None, 'tensor')
- gradient_key_down: float32 [8, 1024, 16], replicated
- gradient_key_up: float32 [8, 16, 1024], P(None, None, 'tensor')
- gradient_value_down: float32 [8, 1024, 16], replicated
- gradient_value_up: float32 [8, 16, 1024], P(None, None, 'tensor')
- gradient_output_down: float32 [8, 1024, 16], P(None, 'tensor')
- gradient_output_up: float32 [8, 16, 1024], replicated
- gradient_expand_down: float32 [8, 1024, 16], replicated
- gradient_expand_up: float32 [8, 16, 4096], P(None, None, 'tensor')
- gradient_contract_down: float32 [8, 4096, 16], P(None, 'tensor')
- gradient_contract_up: float32 [8, 16, 1024], replicated
The draws below stay inside these ranges and needn't reach their ends.
Inputs may be any that keep to these rules, and one draw needn't show every extreme that they name: `adapter_ids`: each of the 8 adapters serves 32 // 8 sequences or one more. `segment_ids`: numbers never fall along a sequence; every sequence holds 6 documents of 1 to 200 tokens, one of exactly 200.
All inputs are finite; a program needn't handle non-finite values.
Results may differ from the reference program's by a relative error of at most 0.019.
Values sent between devices are 32-bit elements; how exact they have to be, the bound alone decides.
A program may use at most 192 MiB of HBM per device.

```python
import math
import jax
import jax.numpy as jnp
import numpy as np
from jax import lax

D = 1024
HEADS = 16
HEAD_WIDTH = 64
FF = 4096
RANK = 16
ADAPTERS = 8
SEQ = 512
DOCS = 6
DOC_MAX = 200
SEQS = 32
TOKENS = 16384


def draw_adapter_ids(key, part):
    spread_ids = jnp.arange(SEQS, dtype=jnp.int32) % ADAPTERS
    return jax.random.permutation(key, spread_ids).astype(jnp.int32)


def steps_of(own_key, shape, pieces, smallest, largest):
    def one(axis_at, parts):
        draws = jax.random.uniform(jax.random.fold_in(jax.random.fold_in(own_key, 6), axis_at), (parts,), jnp.float32, smallest / len(pieces), largest / len(pieces))
        return jnp.repeat(jnp.exp(draws), shape[axis_at] // parts).reshape((-1,) + (1,) * (len(shape) - axis_at - 1))

    level = one(*pieces[0])
    for cut in pieces[1:]:
        level = level * one(*cut)
    return level


def profile(count, total, bound, skew):
    loads = [(1 << 20) // math.isqrt(standing ** skew) + 1 for standing in range(2, count + 1)]
    rest, counts = total - bound - (count - 1), [1] * (count - 1)
    while rest > 0:
        free = [i for i in range(count - 1) if counts[i] < bound]
        mass, budget = sum([loads[i] for i in free]), rest
        for i in free:
            extra = min(bound - counts[i], max(1, budget * loads[i] // mass), rest)
            counts[i] = counts[i] + extra
            rest = rest - extra
    return np.array([bound] + counts)


def ragged_sizes(stream_key, count, total, most, lean):
    if count == 2:
        one = jax.random.randint(stream_key, (), max(1, total - most), min(most, total - 1) + 1)
        return jnp.stack([one, total - one])
    lengths = jnp.asarray(profile(count, total, most, lean), jnp.int32)
    couples = (count - 1) // 2
    giver, taker = lengths[1:1 + 2 * couples:2], lengths[2:2 + 2 * couples:2]
    room = jnp.minimum(giver - 1, most - taker)
    passed = jax.random.randint(jax.random.fold_in(stream_key, 1), (couples,), 0, 1 << 20) % (room + 1)
    lengths = lengths.at[1:1 + 2 * couples:2].set(giver - passed).at[2:2 + 2 * couples:2].set(taker + passed)
    return lengths[jax.random.permutation(jax.random.fold_in(stream_key, 2), count)]


def gaussian(rng, dims, width, reach, shards=(), kind=jnp.bfloat16):
    gain = steps_of(rng, dims, shards, -0.22, 0.18) if shards else 1.0
    values = jax.random.normal(rng, dims, jnp.float32) * width * gain
    return jnp.minimum(jnp.maximum(values, -reach), reach).astype(kind)


def setup_inputs(seed: int = 0) -> dict:
    arg_keys = jax.random.split(jax.random.key(seed), 27)
    return {
        "tokens": gaussian(arg_keys[0], (TOKENS, D), 1.0, 6.0, ((0, 16),)),
        "cotangent": gaussian(arg_keys[1], (TOKENS, D), 1.0, 6.0, ((0, 16),)),
        "segment_ids": jax.vmap(lambda own: jnp.searchsorted(jnp.cumsum(ragged_sizes(own, DOCS, SEQ, DOC_MAX, 0)), jnp.arange(SEQ), side="right"))(jax.random.split(arg_keys[2], SEQS)).reshape((SEQS, SEQ)).astype(jnp.int32),
        "adapter_ids": draw_adapter_ids(jax.random.fold_in(arg_keys[26], 71), 0),
        "query_weight": gaussian(arg_keys[4], (D, D), D ** -0.5, 0.1875, ((1, 2),)),
        "key_weight": gaussian(arg_keys[5], (D, D), D ** -0.5, 0.1875, ((1, 2),)),
        "value_weight": gaussian(arg_keys[6], (D, D), D ** -0.5, 0.1875, ((1, 2),)),
        "output_weight": gaussian(arg_keys[7], (D, D), (D // 16) ** -0.5, 0.75, ((0, 2),)),
        "expand_weight": gaussian(arg_keys[8], (D, FF), D ** -0.5, 0.1875, ((1, 2),)),
        "contract_weight": gaussian(arg_keys[9], (FF, D), FF ** -0.5, 0.09375, ((0, 2),)),
        "first_gain": jnp.clip(1.0 + 0.1 * jax.random.normal(arg_keys[10], (D,), jnp.float32), 0.5, 1.5),
        "first_shift": gaussian(arg_keys[11], (D,), 0.3, 3.0, (), jnp.float32),
        "second_gain": jnp.clip(1.0 + 0.1 * jax.random.normal(arg_keys[12], (D,), jnp.float32), 0.5, 1.5),
        "second_shift": gaussian(arg_keys[13], (D,), 0.3, 3.0, (), jnp.float32),
        "query_down": gaussian(arg_keys[14], (ADAPTERS, D, RANK), D ** -0.5, 0.1875),
        "query_up": gaussian(arg_keys[15], (ADAPTERS, RANK, D), RANK ** -0.5, 1.5, ((2, 2),)),
        "key_down": gaussian(arg_keys[16], (ADAPTERS, D, RANK), D ** -0.5, 0.1875),
        "key_up": gaussian(arg_keys[17], (ADAPTERS, RANK, D), RANK ** -0.5, 1.5, ((2, 2),)),
        "value_down": gaussian(arg_keys[18], (ADAPTERS, D, RANK), D ** -0.5, 0.1875),
        "value_up": gaussian(arg_keys[19], (ADAPTERS, RANK, D), RANK ** -0.5, 1.5, ((2, 2),)),
        "output_down": gaussian(arg_keys[20], (ADAPTERS, D, RANK), (D // 16) ** -0.5, 0.75, ((1, 2),)),
        "output_up": gaussian(arg_keys[21], (ADAPTERS, RANK, D), RANK ** -0.5, 1.5),
        "expand_down": gaussian(arg_keys[22], (ADAPTERS, D, RANK), D ** -0.5, 0.1875),
        "expand_up": gaussian(arg_keys[23], (ADAPTERS, RANK, FF), RANK ** -0.5, 1.5, ((2, 2),)),
        "contract_down": gaussian(arg_keys[24], (ADAPTERS, FF, RANK), FF ** -0.5, 0.09375, ((1, 2),)),
        "contract_up": gaussian(arg_keys[25], (ADAPTERS, RANK, D), RANK ** -0.5, 1.5),
    }


FULL_PRECISION = lax.Precision.HIGHEST
epsilon = 1e-05

@jax.custom_vjp
def low(v):
    return lax.optimization_barrier(v.astype(jnp.bfloat16)).astype(jnp.float32)

@jax.custom_vjp
def low_back(v):
    return v

def low_keep(v):
    return (low(v), None)

def low_pass(kept, grad):
    return (grad,)

def back_keep(v):
    return (v, None)

def back_low(kept, grad):
    return (low(grad),)
low.defvjp(low_keep, low_pass)
low_back.defvjp(back_keep, back_low)

def rounded_operands(value):
    return low_back(low(value))

def choose_adapter(adapter_selector, table):
    return jnp.einsum('se,eab->sab', adapter_selector, table, precision=FULL_PRECISION)

def project(input_activation, dense_weight, down_projection_table, up_table, adapter_selector, round_value, round_gradient):
    rank_space_rows = jnp.einsum('qxm,qmw->qxw', input_activation, choose_adapter(adapter_selector, down_projection_table), precision=FULL_PRECISION)
    if round_value:
        rank_space_rows = low(rank_space_rows)
    if round_gradient:
        rank_space_rows = low_back(rank_space_rows)
    frozen_path_rows = jnp.einsum('bhp,pz->bhz', input_activation, dense_weight, precision=FULL_PRECISION)
    return frozen_path_rows + jnp.einsum('slr,srn->sln', rank_space_rows, choose_adapter(adapter_selector, up_table), precision=FULL_PRECISION)

def layer_norm(summed, norm_gain, norm_shift):
    average = lax.optimization_barrier(jnp.mean(summed, axis=-1, keepdims=True))
    centered = summed - average
    variance = lax.optimization_barrier(jnp.mean(centered * centered, axis=-1, keepdims=True))
    return centered * lax.rsqrt(variance + epsilon) * norm_gain + norm_shift

def attend_one(bundle):
    query_matrix, key_token_rows, value_matrix, segment = bundle
    attention_logits = low_back(jnp.einsum('ayb,oyb->yao', query_matrix, key_token_rows, precision=FULL_PRECISION) * HEAD_WIDTH ** (-0.5))
    same_doc = segment[:, None] == segment[None, :]
    masked = jnp.where(same_doc[None, :, :], attention_logits, -1e+30)
    row_max = lax.optimization_barrier(jnp.max(masked, axis=-1, keepdims=True))
    exponent = jnp.exp(masked - row_max)
    attention_probabilities = exponent / lax.optimization_barrier(jnp.sum(exponent, axis=-1, keepdims=True))
    return jnp.einsum('jop,pjc->ojc', low(attention_probabilities), value_matrix, precision=FULL_PRECISION)

def reference(tokens, cotangent, segment_ids, adapter_ids, query_weight, key_weight, value_weight, output_weight, expand_weight, contract_weight, first_gain, first_shift, second_gain, second_shift, query_down, query_up, key_down, key_up, value_down, value_up, output_down, output_up, expand_down, expand_up, contract_down, contract_up):
    adapter_selector = (adapter_ids[:, None] == jnp.arange(ADAPTERS, dtype=jnp.int32)[None, :]).astype(jnp.float32)
    frozen = tuple((matrix.astype(jnp.float32) for matrix in (query_weight, key_weight, value_weight, output_weight, expand_weight, contract_weight)))
    tables = tuple((matrix.astype(jnp.float32) for matrix in (query_down, query_up, key_down, key_up, value_down, value_up, output_down, output_up, expand_down, expand_up, contract_down, contract_up)))
    token_rows = tokens.astype(jnp.float32).reshape(SEQS, SEQ, D)

    def forward(input_activation, adapters):
        shape_heads = (SEQS, SEQ, HEADS, HEAD_WIDTH)
        query_matrix = rounded_operands(project(input_activation, frozen[0], adapters[0], adapters[1], adapter_selector, True, False)).reshape(shape_heads)
        key_token_rows = rounded_operands(project(input_activation, frozen[1], adapters[2], adapters[3], adapter_selector, True, False)).reshape(shape_heads)
        value_matrix = rounded_operands(project(input_activation, frozen[2], adapters[4], adapters[5], adapter_selector, True, False)).reshape(shape_heads)
        attended = lax.map(jax.checkpoint(attend_one), (query_matrix, key_token_rows, value_matrix, segment_ids))
        heads = rounded_operands(attended.reshape(SEQS, SEQ, D))
        branch = low_back(project(heads, frozen[3], adapters[6], adapters[7], adapter_selector, False, True))
        normed = layer_norm(input_activation + branch, first_gain, first_shift)
        inner = low(normed)
        before = low_back(project(inner, frozen[4], adapters[8], adapters[9], adapter_selector, True, False))
        hidden = low(jax.nn.gelu(before, approximate=False))
        outer = low_back(project(hidden, frozen[5], adapters[10], adapters[11], adapter_selector, False, True))
        return layer_norm(normed + outer, second_gain, second_shift)
    result, pullback = jax.vjp(forward, token_rows, tables)
    back_rows, back_tables = pullback(cotangent.astype(jnp.float32).reshape(SEQS, SEQ, D))
    return (result.reshape(TOKENS, D).astype(jnp.bfloat16), back_rows.reshape(TOKENS, D).astype(jnp.bfloat16), back_tables[0], back_tables[1], back_tables[2], back_tables[3], back_tables[4], back_tables[5], back_tables[6], back_tables[7], back_tables[8], back_tables[9], back_tables[10], back_tables[11])
```

```python
import jax
import jax.numpy as jnp
from jax import lax
from jax.experimental import pallas as pl
from jax.experimental.pallas import tpu as pltpu
from jax.sharding import PartitionSpec as P

HEAD_WIDTH = 64
RANK = 16
MESH = pl.DeviceIdType.MESH
F32 = jnp.float32
BF16 = jnp.bfloat16
EPS = 1e-05
ROWS = 64


def nn(a, b):
    return jnp.dot(a, b, preferred_element_type=F32)


def nt(a, b):
    return lax.dot_general(a, b, (((1,), (1,)), ((), ())), preferred_element_type=F32)


def split(v):
    hi = v.astype(BF16)
    return hi, (v - hi.astype(F32)).astype(BF16)


def nn_wide(v, b):
    hi, lo = split(v)
    return nn(hi, b) + nn(lo, b)


def gelu_parts(v):
    z = jnp.abs(v) * 0.7071067811865476
    t = 1.0 / (1.0 + 0.3275911 * z)
    e = jnp.exp(v * v * -0.5)
    tail = t * (
        0.127414796 + t * (-0.142248368 + t * (0.7107068705 + t * (-0.7265760135 + t * 0.5307027145)))
    ) * e
    cdf = jnp.where(v >= 0, 1.0 - tail, tail)
    return v * cdf, cdf + v * (e * 0.3989422804014327)


def layer_kernel(
    ids, seg, x_hbm, cot_hbm, wq, wk, wv, wo_hbm, we_hbm, wc_hbm, g1, b1, g2, b2,
    qd, kd, vd, qu, ku, vu, od, ou, ed, eu, cd, cu,
    out_hbm, grad_hbm, t_u, t_d, t_od, t_ou, t_eu, t_cd, t_ed, t_cu,
    x, cot, wp, wo, we, wc, dtab, utab, qkv, heads, bias, lse, xhat, rstd, hidden, slope, acc, recv,
    row, work, lcol, rank_t, rank_o, rank_e, rank_c, stage_out,
    load_sem, send_sem, recv_sem, out_sem, credit,
):
    dp = lax.axis_index("dp")
    core = lax.axis_index("tensor")
    partner = (dp, 1 - core)
    first = (core == 0).astype(F32)

    def load(i, src, dst):
        cp = pltpu.make_async_copy(src, dst, load_sem.at[i])
        cp.start()
        return cp

    loads = [load(0, x_hbm, x)]
    tabs = []
    for i, (w, d, u) in enumerate(((wq, qd, qu), (wk, kd, ku), (wv, vd, vu))):
        tabs.append(load(1 + i, w, wp.at[i]))
        tabs.append(load(4 + i, d, dtab.at[i]))
        tabs.append(load(7 + i, u, utab.at[i]))
    load_wo = load(10, wo_hbm, wo)
    load_we = load(11, we_hbm, we)
    load_wc = load(12, wc_hbm, wc)
    load_cot = load(13, cot_hbm, cot)

    barrier = pltpu.get_barrier_semaphore()
    pl.semaphore_signal(barrier, inc=1, device_id=partner, device_id_type=MESH)
    pl.semaphore_wait(barrier, 1)

    def exchange(s):
        return pltpu.make_async_remote_copy(
            src_ref=acc.at[s], dst_ref=recv.at[s], send_sem=send_sem.at[s], recv_sem=recv_sem.at[s],
            device_id=partner, device_id_type=MESH,
        )

    def taken(s):
        pl.semaphore_signal(credit.at[s], inc=1, device_id=partner, device_id_type=MESH)

    def send(s):
        pl.semaphore_wait(credit.at[s], 1)
        exchange(s).start()

    n = x.shape[1]
    heads_half = heads.shape[2]
    pairs = heads_half // 128
    chunks = hidden.shape[2] // 512
    lane = lax.broadcasted_iota(jnp.int32, (n, 128), 1)
    low_half = lane < HEAD_WIDTH

    for cp in loads + tabs:
        cp.wait()

    def stage1(s, carry):
        aid = ids[s]
        xs = x.at[s]
        seg_row = seg[pl.ds(s, 1), :]
        seg_col = jnp.broadcast_to(seg_row, (128, n)).T
        for j in range(n // 128):
            same = seg_col == seg_row[:, j * 128:(j + 1) * 128]
            bias[s, :, j * 128:(j + 1) * 128] = jnp.where(same, 0.0, -1e30)

        def project(p, c):
            d_sel = dtab[p, aid]
            rank = nt(xs[...], d_sel).astype(BF16)
            rank_t[s, p] = nt(d_sel, xs[...]).astype(BF16)
            scale = jnp.where(p == 0, 0.125, 1.0)
            qkv[s, p] = ((nn(xs[...], wp[p]) + nn(rank, utab[p, aid])) * scale).astype(BF16)
            return c

        lax.fori_loop(0, 3, project, 0)

        def pair(hp, c):
            at = pl.ds(pl.multiple_of(hp * 128, 128), 128)
            k2 = qkv[s, 1, :, at]
            v2 = jnp.concatenate([qkv[s, 2, :, at], jnp.ones((n, 128), BF16)], axis=1)
            for r in range(2):
                rows = slice(r * (n // 2), (r + 1) * (n // 2))
                q2 = qkv[s, 0, rows, at]
                outs = []
                ln = lane[rows]
                for j in range(2):
                    mine = (ln < HEAD_WIDTH) if j == 0 else (ln >= HEAD_WIDTH)
                    score = nt(jnp.where(mine, q2, jnp.zeros_like(q2)), k2) + bias[s, rows, :]
                    top = jnp.max(score, axis=1, keepdims=True)
                    e = jnp.exp(score - top).astype(BF16)
                    both = nn(e, v2)
                    total = both[:, 128:]
                    outs.append(both[:, :128] / total)
                    old = lcol[rows, :]
                    lcol[rows, :] = jnp.where(ln == 2 * hp + j, top + jnp.log(total), old)
                heads[s, rows, at] = jnp.where(ln < HEAD_WIDTH, outs[0], outs[1]).astype(BF16)
            return c

        lax.fori_loop(0, pairs, pair, 0)
        lse[s] = lcol[...].T[:lse.shape[1], :]
        return carry

    def stage1_out(s, carry):
        aid = ids[s]
        od_sel = od[aid]
        hs = heads[s]
        rank_o[s] = nt(od_sel, hs)
        acc[s] = nn(hs, wo[...]) + nn_wide(nt(hs, od_sel), ou[aid])
        exchange(s).start()
        return carry

    def both1(s, carry):
        stage1(s, carry)

        @pl.when(s == 0)
        def _():
            load_wo.wait()

        stage1_out(s, carry)
        return carry

    lax.fori_loop(0, 2, both1, 0)

    def stage2(s, carry):
        aid = ids[s]
        exchange(s).wait()

        def norm(i, c):
            rows = pl.ds(pl.multiple_of(i * ROWS, ROWS), ROWS)
            h = x[s, rows, :].astype(F32) + (acc[s, rows, :] + recv[s, rows, :])
            mean = jnp.mean(h, axis=1, keepdims=True)
            h = h - mean
            inv = lax.rsqrt(jnp.mean(h * h, axis=1, keepdims=True) + EPS)
            h = h * inv
            xhat[s, rows, :] = h
            rstd[s, rows, :] = jnp.broadcast_to(inv, (ROWS, 128))
            row[rows, :] = (h * g1[...] + b1[...]).astype(BF16)
            return c

        lax.fori_loop(0, n // ROWS, norm, 0)
        taken(s)
        ed_sel = ed[aid]
        inner = row[...]
        rank = nt(inner, ed_sel).astype(BF16)
        rank_e[s] = nt(ed_sel, inner).astype(BF16)

        def chunk(c, ranks):
            rc, rct = ranks
            at = pl.ds(pl.multiple_of(c * 512, 512), 512)
            before = nn(row[...], we[:, at]) + nn(rank, eu[aid, :, at])
            hid, sl = gelu_parts(before)
            hid = hid.astype(BF16)
            hidden[s, :, at] = hid
            slope[s, :, at] = sl.astype(BF16)
            cd_sel = cd[aid, :, at]
            part = nn(hid, wc[at, :])

            @pl.when(c == 0)
            def _():
                acc[s] = part

            @pl.when(c > 0)
            def _():
                acc[s] += part

            return rc + nt(hid, cd_sel), rct + nt(cd_sel, hid)

        rc, rct = lax.fori_loop(
            0, chunks, chunk, (jnp.zeros((n, RANK), F32), jnp.zeros((RANK, n), F32))
        )
        rank_c[s] = rct
        acc[s] += nn_wide(rc, cu[aid])
        send(s)
        return carry

    load_we.wait()
    load_wc.wait()
    lax.fori_loop(0, 2, stage2, 0)

    def put_out(s):
        return pltpu.make_async_copy(stage_out.at[s], out_hbm.at[s], out_sem.at[s])

    def put_grad(s):
        return pltpu.make_async_copy(stage_out.at[s], grad_hbm.at[s], out_sem.at[s])

    def stage3(s, carry):
        aid = ids[s]
        exchange(s).wait()

        def norm(i, c):
            rows = pl.ds(pl.multiple_of(i * ROWS, ROWS), ROWS)
            normed = xhat[s, rows, :] * g1[...] + b1[...]
            h = normed + (acc[s, rows, :] + recv[s, rows, :])
            mean = jnp.mean(h, axis=1, keepdims=True)
            h = h - mean
            inv = lax.rsqrt(jnp.mean(h * h, axis=1, keepdims=True) + EPS)
            h = h * inv
            stage_out[s, rows, :] = (h * g2[...] + b2[...]).astype(BF16)
            u = cot[s, rows, :].astype(F32) * g2[...]
            back = inv * (
                u - jnp.mean(u, axis=1, keepdims=True) - h * jnp.mean(u * h, axis=1, keepdims=True)
            )
            acc[s, rows, :] = back * first
            row[rows, :] = back.astype(BF16)
            return c

        lax.fori_loop(0, n // ROWS, norm, 0)
        taken(s)
        put_out(s).start()
        cu_sel = cu[aid]
        back_outer = row[...]
        brc = nt(back_outer, cu_sel).astype(BF16)
        brc_t = nt(cu_sel, back_outer).astype(BF16)
        t_cu[s] = nn_wide(rank_c[s], back_outer)
        re_t = rank_e[s]

        def chunk(c, ranks):
            br, brt = ranks
            at = pl.ds(pl.multiple_of(c * 512, 512), 512)
            t_cd[s, :, at] = nn(brc_t, hidden[s, :, at])
            bh = nt(row[...], wc[at, :]) + nn(brc, cd[aid, :, at])
            bb = (bh * slope[s, :, at].astype(F32)).astype(BF16)
            t_eu[s, :, at] = nn(re_t, bb)
            acc[s] += nt(bb, we[:, at])
            eu_sel = eu[aid, :, at]
            return br + nt(bb, eu_sel), brt + nt(eu_sel, bb)

        br, brt = lax.fori_loop(
            0, chunks, chunk, (jnp.zeros((n, RANK), F32), jnp.zeros((RANK, n), F32))
        )
        acc[s] += nn_wide(br, ed[aid])
        send(s)
        inner = (xhat[s] * g1[...] + b1[...]).astype(BF16)
        t_ed[s] = nn_wide(brt, inner)
        return carry

    load_cot.wait()
    lax.fori_loop(0, 2, stage3, 0)

    d_out, d_q, d_k, d_v, dq_t = 0, 1, 2, 3, 4

    def stage4(s, carry):
        aid = ids[s]
        exchange(s).wait()

        def norm(i, c):
            rows = pl.ds(pl.multiple_of(i * ROWS, ROWS), ROWS)
            u = (acc[s, rows, :] + recv[s, rows, :]) * g1[...]
            h = xhat[s, rows, :]
            back = rstd[s, rows, 0:1] * (
                u - jnp.mean(u, axis=1, keepdims=True) - h * jnp.mean(u * h, axis=1, keepdims=True)
            )
            acc[s, rows, :] = back * first
            row[rows, :] = back.astype(BF16)
            return c

        lax.fori_loop(0, n // ROWS, norm, 0)
        taken(s)
        ou_sel = ou[aid]
        od_sel = od[aid]
        back_branch = row[...]
        bro = nt(back_branch, ou_sel).astype(BF16)
        bro_t = nt(ou_sel, back_branch).astype(BF16)
        t_ou[s] = nn_wide(rank_o[s], back_branch)
        hs = heads[s]
        t_od[s] = nn(bro_t, hs)
        d_heads = (nt(back_branch, wo[...]) + nn(bro, od_sel)).astype(BF16)
        work[d_out] = d_heads
        pick = (
            lax.broadcasted_iota(jnp.int32, (RANK, heads_half), 1) // HEAD_WIDTH
            == lax.broadcasted_iota(jnp.int32, (RANK, heads_half), 0)
        ).astype(BF16)
        hi, lo = split(d_heads.astype(F32) * hs.astype(F32))
        lcol[0:RANK, 0:128] = jnp.zeros((RANK, 128), F32)
        dots = nt(pick, hi) + nt(pick, lo)
        drow = rank_o.at[s]
        drow[...] = dots

        def pair(hp, c):
            at = pl.ds(pl.multiple_of(hp * 128, 128), 128)
            q2 = qkv[s, 0, :, at]
            k2 = qkv[s, 1, :, at]
            v2 = qkv[s, 2, :, at]
            do2 = work[d_out, :, at]
            k2t = k2.T
            zero = jnp.zeros_like(k2)
            dk, dv = [], []
            for j in range(2):
                mine = low_half if j == 0 else jnp.logical_not(low_half)
                h = 2 * hp + j
                st = nt(jnp.where(mine, k2, zero), q2) + bias[s]
                pt = jnp.exp(st - lse[s, pl.ds(h, 1), :])
                dpt = nt(jnp.where(mine, v2, zero), do2)
                dst = (pt * (dpt - drow[pl.ds(h, 1), :])).astype(BF16)
                dv.append(nn(pt.astype(BF16), do2))
                dk.append(nn(dst, q2))
                dqt = nn(k2t[j * HEAD_WIDTH:(j + 1) * HEAD_WIDTH, :], dst) * 0.125
                work[dq_t, pl.ds(pl.multiple_of(h * HEAD_WIDTH, HEAD_WIDTH), HEAD_WIDTH), :] = dqt.astype(BF16)
            work[d_k, :, at] = jnp.where(low_half, dk[0], dk[1]).astype(BF16)
            work[d_v, :, at] = jnp.where(low_half, dv[0], dv[1]).astype(BF16)
            return c

        lax.fori_loop(0, pairs, pair, 0)
        work[d_q] = work[dq_t].T

        def project(p, c):
            dp_ = work[1 + p]
            u_sel = utab[p, aid]
            d_sel = dtab[p, aid]
            t_u[s, p] = nn(rank_t[s, p], dp_)
            t_d[s, p] = nn_wide(nt(u_sel, dp_), x[s])
            acc[s] += nt(dp_, wp[p]) + nn_wide(nt(dp_, u_sel), d_sel)
            return c

        lax.fori_loop(0, 3, project, 0)
        send(s)
        return carry

    lax.fori_loop(0, 2, stage4, 0)

    def stage5(s, carry):
        exchange(s).wait()
        put_out(s).wait()

        def add(i, c):
            rows = pl.ds(pl.multiple_of(i * ROWS, ROWS), ROWS)
            stage_out[s, rows, :] = (acc[s, rows, :] + recv[s, rows, :]).astype(BF16)
            return c

        lax.fori_loop(0, n // ROWS, add, 0)
        put_grad(s).start()
        return carry

    lax.fori_loop(0, 2, stage5, 0)
    put_grad(0).wait()
    put_grad(1).wait()


def layer(ids, seg, x, cot, wq, wk, wv, wo, we, wc, g1, b1, g2, b2, *tables):
    s, n, d = x.shape
    hw = wq.shape[1]
    f = we.shape[1]
    hbm = pl.BlockSpec(memory_space=pl.ANY)
    vm = pl.BlockSpec(memory_space=pltpu.VMEM)
    sm = pl.BlockSpec(memory_space=pltpu.SMEM)
    sds = jax.ShapeDtypeStruct
    return pl.pallas_call(
        layer_kernel,
        out_shape=(
            sds((s, n, d), BF16), sds((s, n, d), BF16),
            sds((s, 3, RANK, hw), F32), sds((s, 3, RANK, d), F32), sds((s, RANK, hw), F32),
            sds((s, RANK, d), F32), sds((s, RANK, f), F32), sds((s, RANK, f), F32),
            sds((s, RANK, d), F32), sds((s, RANK, d), F32),
        ),
        in_specs=[sm, vm, hbm, hbm, hbm, hbm, hbm, hbm, hbm, hbm, vm, vm, vm, vm]
        + [hbm] * 6 + [vm] * 6,
        out_specs=(hbm, hbm) + (vm,) * 8,
        scratch_shapes=[
            pltpu.VMEM((s, n, d), BF16),
            pltpu.VMEM((s, n, d), BF16),
            pltpu.VMEM((3, d, hw), BF16),
            pltpu.VMEM((hw, d), BF16),
            pltpu.VMEM((d, f), BF16),
            pltpu.VMEM((f, d), BF16),
            pltpu.VMEM((3, 8, RANK, d), BF16),
            pltpu.VMEM((3, 8, RANK, hw), BF16),
            pltpu.VMEM((s, 3, n, hw), BF16),
            pltpu.VMEM((s, n, hw), BF16),
            pltpu.VMEM((s, n, n), F32),
            pltpu.VMEM((s, RANK, n), F32),
            pltpu.VMEM((s, n, d), F32),
            pltpu.VMEM((s, n, 128), F32),
            pltpu.VMEM((s, n, f), BF16),
            pltpu.VMEM((s, n, f), BF16),
            pltpu.VMEM((s, n, d), F32),
            pltpu.VMEM((s, n, d), F32),
            pltpu.VMEM((n, d), BF16),
            pltpu.VMEM((5, n, hw), BF16),
            pltpu.VMEM((n, 128), F32),
            pltpu.VMEM((s, 3, RANK, n), BF16),
            pltpu.VMEM((s, RANK, n), F32),
            pltpu.VMEM((s, RANK, n), BF16),
            pltpu.VMEM((s, RANK, n), F32),
            pltpu.VMEM((s, n, d), BF16),
            pltpu.SemaphoreType.DMA((14,)),
            pltpu.SemaphoreType.DMA((2,)),
            pltpu.SemaphoreType.DMA((2,)),
            pltpu.SemaphoreType.DMA((2,)),
            pltpu.SemaphoreType.REGULAR((2,)),
        ],
        compiler_params=pltpu.CompilerParams(
            collective_id=0, has_side_effects=True, vmem_limit_bytes=63 * 1024 * 1024
        ),
    )(ids, seg, x, cot, wq, wk, wv, wo, we, wc, g1, b1, g2, b2, *tables)


def on_device(
    tokens, cotangent, segment_ids, adapter_ids, query_weight, key_weight, value_weight, output_weight,
    expand_weight, contract_weight, first_gain, first_shift, second_gain, second_shift,
    query_down, query_up, key_down, key_up, value_down, value_up, output_down, output_up,
    expand_down, expand_up, contract_down, contract_up,
):
    seqs, length = segment_ids.shape
    width = tokens.shape[1]
    turn = lambda t: jnp.swapaxes(t, 1, 2)
    line = lambda v: v.reshape(1, -1)
    out, grad, t_u, t_d, t_od, t_ou, t_eu, t_cd, t_ed, t_cu = layer(
        adapter_ids, segment_ids.astype(F32),
        tokens.reshape(seqs, length, width), cotangent.reshape(seqs, length, width),
        query_weight, key_weight, value_weight, output_weight, expand_weight, contract_weight,
        line(first_gain), line(first_shift), line(second_gain), line(second_shift),
        turn(query_down), turn(key_down), turn(value_down), query_up, key_up, value_up,
        turn(output_down), output_up, turn(expand_down), expand_up, turn(contract_down), contract_up,
    )
    selector = (
        adapter_ids[:, None] == jnp.arange(query_down.shape[0], dtype=jnp.int32)[None, :]
    ).astype(F32)
    spread = lambda t: jnp.einsum("se,s...->e...", selector, t, precision=lax.Precision.HIGHEST)
    both = lax.psum((spread(t_d), spread(t_ou), spread(t_ed), spread(t_cu)), ("dp", "tensor"))
    one = lax.psum((spread(t_u), spread(t_od), spread(t_eu), spread(t_cd)), "dp")
    g_d, g_ou, g_ed, g_cu = both
    g_u, g_od, g_eu, g_cd = one
    return (
        out.reshape(tokens.shape), grad.reshape(tokens.shape),
        turn(g_d[:, 0]), g_u[:, 0], turn(g_d[:, 1]), g_u[:, 1], turn(g_d[:, 2]), g_u[:, 2],
        turn(g_od), g_ou, turn(g_ed), g_eu, turn(g_cd), g_cu,
    )


def solution(mesh):
    cols = P(None, None, "tensor")
    mid = P(None, "tensor", None)
    return jax.shard_map(
        on_device,
        mesh=mesh,
        in_specs=(
            P("dp", None), P("dp", None), P("dp", None), P("dp"),
            P(None, "tensor"), P(None, "tensor"), P(None, "tensor"), P("tensor", None),
            P(None, "tensor"), P("tensor", None), P(), P(), P(), P(),
            P(), cols, P(), cols, P(), cols, mid, P(), P(), cols, mid, P(),
        ),
        out_specs=(
            P("dp", None), P("dp", None), P(), cols, P(), cols, P(), cols, mid, P(), P(), cols, mid, P(),
        ),
        check_vma=False,
    )
```

```python
import jax
import jax.numpy as jnp
from jax import lax
from jax.experimental import pallas as pl
from jax.experimental.pallas import tpu as pltpu
from jax.sharding import PartitionSpec as P

HEAD_WIDTH = 64
RANK = 16
MESH = pl.DeviceIdType.MESH
F32 = jnp.float32
BF16 = jnp.bfloat16
EPS = 1e-05
ROWS = 64
GROUP = 16
EARLY, LATE = 640, 512


def nn(a, b):
    return jnp.dot(a, b, preferred_element_type=F32)


def nt(a, b):
    return lax.dot_general(a, b, (((1,), (1,)), ((), ())), preferred_element_type=F32)


def split(v):
    hi = v.astype(BF16)
    return hi, (v - hi.astype(F32)).astype(BF16)


def nn_wide(v, b):
    hi, lo = split(v)
    return nn(hi, b) + nn(lo, b)


def gelu_parts(v):
    z = jnp.abs(v) * 0.7071067811865476
    t = 1.0 / (1.0 + 0.3275911 * z)
    e = jnp.exp(v * v * -0.5)
    tail = t * (
        0.127414796 + t * (-0.142248368 + t * (0.7107068705 + t * (-0.7265760135 + t * 0.5307027145)))
    ) * e
    cdf = jnp.where(v >= 0, 1.0 - tail, tail)
    return v * cdf, cdf + v * (e * 0.3989422804014327)


def layer_kernel(
    ids, seg, x_hbm, cot_hbm, wq, wk, wv, wo_hbm, we_hbm, wc_hbm, g1, b1, g2, b2,
    qd, kd, vd, qu, ku, vu, od, ou, ed, eu, cd, cu,
    out_hbm, grad_hbm, geu, ger, glu, glr, her, hlr,
    x, cot, wp, wo, we, wc, dtab, utab, qkv, heads, bias, lse, xhat, rstd, hidden, slope, acc, recv,
    row, work, lcol, rank_t, rank_e, drow, mine_rk, their_rk, stage_out,
    pick_mine, picks, pack_e, pack_l, rs_e, rs_l, dense_eu, dense_er, dense_lu, dense_lr,
    load_sem, send_sem, recv_sem, out_sem, credit, rk_send, rk_recv, pick_send, pick_recv,
    rs_send_sem, rs_recv_sem, z_send, z_recv, plane_send, plane_recv, own_sem, swap_send, swap_recv,
):
    dp = lax.axis_index("dp")
    core = lax.axis_index("tensor")
    partner = (dp, 1 - core)
    first = (core == 0).astype(F32)
    me = lax.rem(dp, GROUP)
    base = dp - me
    half = pl.ds(pl.multiple_of(core * 512, 512), 512)

    def load(i, src, dst):
        cp = pltpu.make_async_copy(src, dst, load_sem.at[i])
        cp.start()
        return cp

    loads = [load(0, x_hbm, x)]
    tabs = []
    for i, (w, d, u) in enumerate(((wq, qd, qu), (wk, kd, ku), (wv, vd, vu))):
        tabs.append(load(1 + i, w, wp.at[i]))
        tabs.append(load(4 + i, d, dtab.at[i]))
        tabs.append(load(7 + i, u, utab.at[i]))
    load_wo = load(10, wo_hbm, wo)
    load_we = load(11, we_hbm, we)
    load_wc = load(12, wc_hbm, wc)
    load_cot = load(13, cot_hbm, cot)

    def peer(k):
        return (base + lax.bitwise_xor(me, k), core)

    barrier = pltpu.get_barrier_semaphore()
    pl.semaphore_signal(barrier, inc=1, device_id=partner, device_id_type=MESH)

    def greet(k, c):
        pl.semaphore_signal(barrier, inc=1, device_id=peer(k), device_id_type=MESH)
        return c

    lax.fori_loop(1, GROUP, greet, 0)
    pl.semaphore_wait(barrier, GROUP)

    def remote(src, dst, ss, rs, to):
        return pltpu.make_async_remote_copy(
            src_ref=src, dst_ref=dst, send_sem=ss, recv_sem=rs, device_id=to, device_id_type=MESH
        )

    def pick_copy(k):
        return remote(pick_mine, picks.at[me], pick_send.at[k], pick_recv.at[k], peer(k))

    table_id = lax.broadcasted_iota(jnp.int32, (8, 128), 0)
    for s in range(2):
        pick_mine[s] = (table_id == ids[s]).astype(F32)
    picks[me] = pick_mine[...]

    def send_pick(k, c):
        pick_copy(k).start()
        return c

    lax.fori_loop(1, GROUP, send_pick, 0)

    def rk_copy(s, i):
        rows = pl.ds(i * RANK, RANK if i < 3 else 3 * RANK)
        return remote(
            mine_rk.at[s, rows], their_rk.at[s, rows], rk_send.at[s, i], rk_recv.at[s, i], partner
        )

    def rank_sum(s, i, rows):
        rk_copy(s, i).wait()
        at = slice(i * RANK, i * RANK + rows)
        return mine_rk[s, at, :] + their_rk[s, at, :]

    packs, parts, swapped = (pack_e, pack_l), (rs_e, rs_l), (her, hlr)
    denses, gathered = ((dense_eu, dense_er), (dense_lu, dense_lr)), ((geu, ger), (glu, glr))

    def shard_copy(g, s, k):
        to = lax.bitwise_xor(me, k)
        return remote(
            packs[g].at[s, to], parts[g].at[me, s], rs_send_sem.at[g, s, k], rs_recv_sem.at[g, s, k], peer(k)
        )

    def scatter(g, s):
        parts[g][me, s] = packs[g][s, me]

        def go(k, c):
            shard_copy(g, s, k).start()
            return c

        lax.fori_loop(1, GROUP, go, 0)

    def combine(g):
        def wait(k, c):
            for s in range(2):
                shard_copy(g, s, k).wait()
            return c

        lax.fori_loop(1, GROUP, wait, 0)

        def add(m, total):
            for s in range(2):
                part = parts[g][m, s]
                total = tuple(
                    t + part * jnp.broadcast_to(picks[m, s, a:a + 1, 0:1], part.shape)
                    for a, t in enumerate(total)
                )
            return total

        zero = jnp.zeros(parts[g].shape[2:], F32)
        for a, t in enumerate(lax.fori_loop(0, GROUP, add, (zero,) * 8)):
            w = denses[g][0].shape[2]
            denses[g][0][a] = t[:, :w]
            denses[g][1][a] = t[:, w:]

    def own_copy(g, i):
        return pltpu.make_async_copy(denses[g][i], gathered[g][i].at[me], own_sem.at[g, i])

    def z_copy(g, i, u):
        return remote(
            denses[g][i], gathered[g][i].at[me], z_send.at[g, i, u], z_recv.at[g, i, u], peer(4 * u)
        )

    def slot(u, k):
        return lax.bitwise_xor(me, 4 * u + k)

    def plane_copy(g, i, u, way):
        to = gathered[g][i].at[slot(u, 0)]
        return remote(
            denses[g][i] if u == 0 else to, to, plane_send.at[g, i, u, way], plane_recv.at[g, i, u, way],
            peer(way + 1),
        )

    def onward_copy(g, i, u, way):
        at = gathered[g][i].at[slot(u, way + 1), pl.ds(4 * way, 4)]
        return remote(
            at, at, plane_send.at[g, i, u, 2 + way], plane_recv.at[g, i, u, 2 + way], peer(2 - way)
        )

    def swap_copy(g, u):
        plane = pl.ds(slot(u, 0) // 4 * 4, 4)
        return remote(
            gathered[g][1].at[plane], swapped[g].at[plane], swap_send.at[g, u], swap_recv.at[g, u], partner
        )

    both = [(i, way) for i in range(2) for way in range(2)]

    def gather_first(g):
        for i in range(2):
            own_copy(g, i).start()
            for u in (1, 2, 3):
                z_copy(g, i, u).start()
        for i, way in both:
            plane_copy(g, i, 0, way).start()

    def gather_unit(g, u):
        for i in range(2):
            z_copy(g, i, u).wait_recv()
        for i, way in both:
            plane_copy(g, i, u, way).start()

    def gather_onward(g, u):
        for i, way in both:
            plane_copy(g, i, u, way).wait_recv()
            onward_copy(g, i, u, way).start()

    def gather_swap(g, u):
        if u == 0:
            for i in range(2):
                own_copy(g, i).wait()
        for i, way in both:
            onward_copy(g, i, u, way).wait_recv()
        swap_copy(g, u).start()

    def gather_end(g):
        for u in (1, 2, 3):
            for i in range(2):
                z_copy(g, i, u).wait_send()
        for u in range(4):
            for i, way in both:
                plane_copy(g, i, u, way).wait_send()
                onward_copy(g, i, u, way).wait_send()
            swap_copy(g, u).wait()

    def exchange(s):
        return pltpu.make_async_remote_copy(
            src_ref=acc.at[s], dst_ref=recv.at[s], send_sem=send_sem.at[s], recv_sem=recv_sem.at[s],
            device_id=partner, device_id_type=MESH,
        )

    def taken(s):
        pl.semaphore_signal(credit.at[s], inc=1, device_id=partner, device_id_type=MESH)

    def send(s):
        pl.semaphore_wait(credit.at[s], 1)
        exchange(s).start()

    n = x.shape[1]
    heads_half = heads.shape[2]
    pairs = heads_half // 128
    chunks = hidden.shape[2] // 512
    lane = lax.broadcasted_iota(jnp.int32, (n, 128), 1)
    low_half = lane < HEAD_WIDTH

    for cp in loads + tabs:
        cp.wait()

    def stage1(s, carry):
        aid = ids[s]
        xs = x.at[s]
        seg_row = seg[pl.ds(s, 1), :]
        seg_col = jnp.broadcast_to(seg_row, (128, n)).T
        for j in range(n // 128):
            same = seg_col == seg_row[:, j * 128:(j + 1) * 128]
            bias[s, :, j * 128:(j + 1) * 128] = jnp.where(same, 0.0, -1e30)

        def project(p, c):
            d_sel = dtab[p, aid]
            rank = nt(xs[...], d_sel).astype(BF16)
            rank_t[s, p] = nt(d_sel, xs[...]).astype(BF16)
            scale = jnp.where(p == 0, 0.125, 1.0)
            qkv[s, p] = ((nn(xs[...], wp[p]) + nn(rank, utab[p, aid])) * scale).astype(BF16)
            return c

        lax.fori_loop(0, 3, project, 0)

        def pair(hp, c):
            at = pl.ds(pl.multiple_of(hp * 128, 128), 128)
            k2 = qkv[s, 1, :, at]
            v2 = jnp.concatenate([qkv[s, 2, :, at], jnp.ones((n, 128), BF16)], axis=1)
            for r in range(2):
                rows = slice(r * (n // 2), (r + 1) * (n // 2))
                q2 = qkv[s, 0, rows, at]
                outs = []
                ln = lane[rows]
                for j in range(2):
                    mine = (ln < HEAD_WIDTH) if j == 0 else (ln >= HEAD_WIDTH)
                    score = nt(jnp.where(mine, q2, jnp.zeros_like(q2)), k2) + bias[s, rows, :]
                    top = jnp.max(score, axis=1, keepdims=True)
                    e = jnp.exp(score - top).astype(BF16)
                    both = nn(e, v2)
                    total = both[:, 128:]
                    outs.append(both[:, :128] / total)
                    old = lcol[rows, :]
                    lcol[rows, :] = jnp.where(ln == 2 * hp + j, top + jnp.log(total), old)
                heads[s, rows, at] = jnp.where(ln < HEAD_WIDTH, outs[0], outs[1]).astype(BF16)
            return c

        lax.fori_loop(0, pairs, pair, 0)
        lse[s] = lcol[...].T[:lse.shape[1], :]
        return carry

    def stage1_out(s, carry):
        aid = ids[s]
        od_sel = od[aid]
        hs = heads[s]
        mine_rk[s, 0:RANK, :] = nt(od_sel, hs)
        rk_copy(s, 0).start()
        acc[s] = nn(hs, wo[...]) + nn_wide(nt(hs, od_sel), ou[aid])
        exchange(s).start()
        return carry

    def both1(s, carry):
        stage1(s, carry)

        @pl.when(s == 0)
        def _():
            load_wo.wait()

        stage1_out(s, carry)
        return carry

    lax.fori_loop(0, 2, both1, 0)

    def stage2(s, carry):
        aid = ids[s]
        exchange(s).wait()

        def norm(i, c):
            rows = pl.ds(pl.multiple_of(i * ROWS, ROWS), ROWS)
            h = x[s, rows, :].astype(F32) + (acc[s, rows, :] + recv[s, rows, :])
            mean = jnp.mean(h, axis=1, keepdims=True)
            h = h - mean
            inv = lax.rsqrt(jnp.mean(h * h, axis=1, keepdims=True) + EPS)
            h = h * inv
            xhat[s, rows, :] = h
            rstd[s, rows, :] = jnp.broadcast_to(inv, (ROWS, 128))
            row[rows, :] = (h * g1[...] + b1[...]).astype(BF16)
            return c

        lax.fori_loop(0, n // ROWS, norm, 0)
        taken(s)
        ed_sel = ed[aid]
        inner = row[...]
        rank = nt(inner, ed_sel).astype(BF16)
        rank_e[s] = nt(ed_sel, inner).astype(BF16)

        def chunk(c, ranks):
            rc, rct = ranks
            at = pl.ds(pl.multiple_of(c * 512, 512), 512)
            before = nn(row[...], we[:, at]) + nn(rank, eu[aid, :, at])
            hid, sl = gelu_parts(before)
            hid = hid.astype(BF16)
            hidden[s, :, at] = hid
            slope[s, :, at] = sl.astype(BF16)
            cd_sel = cd[aid, :, at]
            part = nn(hid, wc[at, :])

            @pl.when(c == 0)
            def _():
                acc[s] = part

            @pl.when(c > 0)
            def _():
                acc[s] += part

            return rc + nt(hid, cd_sel), rct + nt(cd_sel, hid)

        rc, rct = lax.fori_loop(
            0, chunks, chunk, (jnp.zeros((n, RANK), F32), jnp.zeros((RANK, n), F32))
        )
        mine_rk[s, RANK:2 * RANK, :] = rct
        rk_copy(s, 1).start()
        acc[s] += nn_wide(rc, cu[aid])
        send(s)
        return carry

    load_we.wait()
    load_wc.wait()
    lax.fori_loop(0, 2, stage2, 0)

    def put_out(s):
        return pltpu.make_async_copy(stage_out.at[s], out_hbm.at[s], out_sem.at[s])

    def put_grad(s):
        return pltpu.make_async_copy(stage_out.at[s], grad_hbm.at[s], out_sem.at[s])

    def stage3(s, carry):
        aid = ids[s]
        exchange(s).wait()

        def norm(i, c):
            rows = pl.ds(pl.multiple_of(i * ROWS, ROWS), ROWS)
            normed = xhat[s, rows, :] * g1[...] + b1[...]
            h = normed + (acc[s, rows, :] + recv[s, rows, :])
            mean = jnp.mean(h, axis=1, keepdims=True)
            h = h - mean
            inv = lax.rsqrt(jnp.mean(h * h, axis=1, keepdims=True) + EPS)
            h = h * inv
            stage_out[s, rows, :] = (h * g2[...] + b2[...]).astype(BF16)
            u = cot[s, rows, :].astype(F32) * g2[...]
            back = inv * (
                u - jnp.mean(u, axis=1, keepdims=True) - h * jnp.mean(u * h, axis=1, keepdims=True)
            )
            acc[s, rows, :] = back * first
            row[rows, :] = back.astype(BF16)
            return c

        lax.fori_loop(0, n // ROWS, norm, 0)
        taken(s)
        put_out(s).start()
        cu_sel = cu[aid]
        back_outer = row[...]
        brc = nt(back_outer, cu_sel).astype(BF16)
        brc_t = nt(cu_sel, back_outer).astype(BF16)
        t_cu = nn_wide(rank_sum(s, 1, RANK), row[:, half])
        for q in range(4):
            for h in range(2):
                pack_e[s, 8 + 2 * q + h, :, 512:640] = t_cu[8 * h:8 * h + 8, 128 * q:128 * q + 128]
        re_t = rank_e[s]

        def chunk(c, ranks):
            br, brt = ranks
            at = pl.ds(pl.multiple_of(c * 512, 512), 512)
            t_cd = nn(brc_t, hidden[s, :, at])
            bh = nt(row[...], wc[at, :]) + nn(brc, cd[aid, :, at])
            bb = (bh * slope[s, :, at].astype(F32)).astype(BF16)
            t_eu = nn(re_t, bb)
            for q in range(2):
                for h in range(2):
                    shard = 4 * c + 2 * q + h
                    part = slice(8 * h, 8 * h + 8), slice(256 * q, 256 * q + 256)
                    pack_e[s, shard, :, 0:256] = t_eu[part]
                    pack_e[s, shard, :, 256:512] = t_cd[part]
            acc[s] += nt(bb, we[:, at])
            eu_sel = eu[aid, :, at]
            return br + nt(bb, eu_sel), brt + nt(eu_sel, bb)

        br, brt = lax.fori_loop(
            0, chunks, chunk, (jnp.zeros((n, RANK), F32), jnp.zeros((RANK, n), F32))
        )
        mine_rk[s, 2 * RANK:3 * RANK, :] = brt
        rk_copy(s, 2).start()
        acc[s] += nn_wide(br, ed[aid])
        send(s)
        return carry

    load_cot.wait()
    lax.fori_loop(0, 2, stage3, 0)

    def early(s, carry):
        inner = (xhat[s, :, half] * g1[:, half] + b1[:, half]).astype(BF16)
        t_ed = nn_wide(rank_sum(s, 2, RANK), inner)
        for q in range(4):
            for h in range(2):
                pack_e[s, 2 * q + h, :, 512:640] = t_ed[8 * h:8 * h + 8, 128 * q:128 * q + 128]
        scatter(0, s)
        return carry

    lax.fori_loop(0, 2, early, 0)

    d_out, d_q, d_k, d_v, dq_t = 0, 1, 2, 3, 4

    def put_late(s, t, up, down):
        for q in range(2):
            for h in range(2):
                part = slice(8 * h, 8 * h + 8), slice(256 * q, 256 * q + 256)
                if up is not None:
                    pack_l[s, 4 * t + 2 * q + h, :, 0:256] = up[part]
                if down is not None:
                    pack_l[s, 4 * t + 2 * q + h, :, 256:512] = down[part]

    def between(s, hp):
        def at(s_, hp_, f):
            @pl.when(jnp.logical_and(s == s_, hp == hp_))
            def _():
                f()

        def begin():
            combine(0)
            gather_first(0)

        def step(u):
            def f():
                gather_unit(0, u)
                gather_onward(0, u - 1)
            return f

        at(0, 3, begin)
        at(1, 0, step(1))
        at(1, 1, step(2))
        at(1, 3, step(3))

    def wait_picks(k, c):
        pick_copy(k).wait()
        return c

    lax.fori_loop(1, GROUP, wait_picks, 0)

    def stage4(s, carry):
        aid = ids[s]
        exchange(s).wait()

        def norm(i, c):
            rows = pl.ds(pl.multiple_of(i * ROWS, ROWS), ROWS)
            u = (acc[s, rows, :] + recv[s, rows, :]) * g1[...]
            h = xhat[s, rows, :]
            back = rstd[s, rows, 0:1] * (
                u - jnp.mean(u, axis=1, keepdims=True) - h * jnp.mean(u * h, axis=1, keepdims=True)
            )
            acc[s, rows, :] = back * first
            row[rows, :] = back.astype(BF16)
            return c

        lax.fori_loop(0, n // ROWS, norm, 0)
        taken(s)
        ou_sel = ou[aid]
        od_sel = od[aid]
        back_branch = row[...]
        bro = nt(back_branch, ou_sel).astype(BF16)
        bro_t = nt(ou_sel, back_branch).astype(BF16)
        hs = heads[s]
        put_late(s, 3, nn(bro_t, hs), nn_wide(rank_sum(s, 0, RANK), row[:, half]))
        d_heads = (nt(back_branch, wo[...]) + nn(bro, od_sel)).astype(BF16)
        work[d_out] = d_heads
        pick = (
            lax.broadcasted_iota(jnp.int32, (RANK, heads_half), 1) // HEAD_WIDTH
            == lax.broadcasted_iota(jnp.int32, (RANK, heads_half), 0)
        ).astype(BF16)
        hi, lo = split(d_heads.astype(F32) * hs.astype(F32))
        drow[...] = nt(pick, hi) + nt(pick, lo)

        def pair(hp, c):
            at = pl.ds(pl.multiple_of(hp * 128, 128), 128)
            q2 = qkv[s, 0, :, at]
            k2 = qkv[s, 1, :, at]
            v2 = qkv[s, 2, :, at]
            do2 = work[d_out, :, at]
            k2t = k2.T
            zero = jnp.zeros_like(k2)
            dk, dv = [], []
            for j in range(2):
                mine = low_half if j == 0 else jnp.logical_not(low_half)
                h = 2 * hp + j
                st = nt(jnp.where(mine, k2, zero), q2) + bias[s]
                pt = jnp.exp(st - lse[s, pl.ds(h, 1), :])
                dpt = nt(jnp.where(mine, v2, zero), do2)
                dst = (pt * (dpt - drow[pl.ds(h, 1), :])).astype(BF16)
                dv.append(nn(pt.astype(BF16), do2))
                dk.append(nn(dst, q2))
                dqt = nn(k2t[j * HEAD_WIDTH:(j + 1) * HEAD_WIDTH, :], dst) * 0.125
                work[dq_t, pl.ds(pl.multiple_of(h * HEAD_WIDTH, HEAD_WIDTH), HEAD_WIDTH), :] = dqt.astype(BF16)
            work[d_k, :, at] = jnp.where(low_half, dk[0], dk[1]).astype(BF16)
            work[d_v, :, at] = jnp.where(low_half, dv[0], dv[1]).astype(BF16)
            between(s, hp)
            return c

        lax.fori_loop(0, pairs, pair, 0)
        work[d_q] = work[dq_t].T

        def terms(p, c):
            dp_ = work[1 + p]
            put_late(s, p, nn(rank_t[s, p], dp_), None)
            mine_rk[s, pl.ds(pl.multiple_of((3 + p) * RANK, RANK), RANK), :] = nt(utab[p, aid], dp_)
            return c

        lax.fori_loop(0, 3, terms, 0)
        rk_copy(s, 3).start()
        hi, lo = split(rank_sum(s, 3, 3 * RANK))
        xs = x[s, :, half]
        t_d = nn(hi, xs) + nn(lo, xs)
        for p in range(3):
            put_late(s, p, None, t_d[RANK * p:RANK * p + RANK, :])
        scatter(1, s)

        def project(p, c):
            dp_ = work[1 + p]
            u_sel = utab[p, aid]
            d_sel = dtab[p, aid]
            acc[s] += nt(dp_, wp[p]) + nn_wide(nt(dp_, u_sel), d_sel)
            return c

        lax.fori_loop(0, 3, project, 0)
        send(s)
        return carry

    lax.fori_loop(0, 2, stage4, 0)

    gather_onward(0, 3)

    def stage5(s, carry):
        exchange(s).wait()
        put_out(s).wait()

        def add(i, c):
            rows = pl.ds(pl.multiple_of(i * ROWS, ROWS), ROWS)
            stage_out[s, rows, :] = (acc[s, rows, :] + recv[s, rows, :]).astype(BF16)
            return c

        lax.fori_loop(0, n // ROWS, add, 0)
        put_grad(s).start()
        return carry

    lax.fori_loop(0, 2, stage5, 0)
    for u in range(4):
        gather_swap(0, u)
    combine(1)
    gather_first(1)
    for u in (1, 2, 3):
        gather_unit(1, u)
        gather_onward(1, u - 1)
    gather_onward(1, 3)
    for u in range(4):
        gather_swap(1, u)
    gather_end(0)
    gather_end(1)
    put_grad(0).wait()
    put_grad(1).wait()


def place_kernel(*refs):
    src, dst, src_v, dst_v = refs[:8], refs[8:22], refs[22:30], refs[30:42]
    in_sem, out_sem = refs[42:]
    core = lax.axis_index("tensor")
    loads = [pltpu.make_async_copy(a, b, in_sem.at[i]) for i, (a, b) in enumerate(zip(src, src_v))]
    for cp in loads:
        cp.start()
    ends = []

    def store(v, i):
        cp = pltpu.make_async_copy(v, dst[i], out_sem.at[i])
        cp.start()
        ends.append(cp)

    qd, qu, kd, ku, vd, vu, od, ou, ed, eu, cd, cu = range(12)
    up, down, low = (qu, ku, vu, od), (qd, kd, vd, ou), (ed, cu)
    geu, ger, glu, glr, her, hlr = src_v[:6]

    def lanes(side, width, i):
        return pl.ds(pl.multiple_of(side * 512 + width * i, 128), width)

    def rows(n):
        return slice(8 * (n % 2), 8 * (n % 2) + 8)

    loads[0].wait()
    for n in range(GROUP):
        at = slice(256 * (n // 2), 256 * (n // 2) + 256)
        dst_v[eu][:, rows(n), at] = geu[n, :, :, 0:256]
        dst_v[cd][:, rows(n), at] = geu[n, :, :, 256:512]
    store(dst_v[eu], 2 + eu)
    store(dst_v[cd], 2 + cd)
    for i in (1, 4):
        loads[i].wait()
    for n in range(GROUP):
        v = dst_v[low[n // 8]]
        v[:, rows(n), lanes(core, 128, n % 8 // 2)] = ger[n]
        v[:, rows(n), lanes(1 - core, 128, n % 8 // 2)] = her[n]
    store(dst_v[ed], 2 + ed)
    store(dst_v[cu], 2 + cu)
    for i in (2, 3, 5):
        loads[i].wait()
    for t in range(4):
        for n in range(4 * t, 4 * t + 4):
            q = n % 4 // 2
            dst_v[up[t]][:, rows(n), 256 * q:256 * q + 256] = glu[n]
            dst_v[down[t]][:, rows(n), lanes(core, 256, q)] = glr[n]
            dst_v[down[t]][:, rows(n), lanes(1 - core, 256, q)] = hlr[n]
        store(dst_v[up[t]], 2 + up[t])
        store(dst_v[down[t]], 2 + down[t])
    for i in range(2):
        loads[6 + i].wait()
        store(src_v[6 + i], i)
    for cp in ends:
        cp.wait()


def place(out, grad, tables, hw, f):
    s, n, d = out.shape
    hbm = pl.BlockSpec(memory_space=pl.ANY)
    widths = (d, hw, d, hw, d, hw, hw, d, d, f, f, d)
    args = (*tables, out, grad)
    return pl.pallas_call(
        place_kernel,
        out_shape=[jax.ShapeDtypeStruct((s, n, d), BF16)] * 2
        + [jax.ShapeDtypeStruct((8, RANK, w), F32) for w in widths],
        in_specs=[hbm] * 8,
        out_specs=[hbm] * 14,
        scratch_shapes=[pltpu.VMEM(a.shape, a.dtype) for a in args]
        + [pltpu.VMEM((8, RANK, w), F32) for w in widths]
        + [pltpu.SemaphoreType.DMA((8,)), pltpu.SemaphoreType.DMA((14,))],
        compiler_params=pltpu.CompilerParams(vmem_limit_bytes=40 * 1024 * 1024),
    )(*args)


def layer(ids, seg, x, cot, wq, wk, wv, wo, we, wc, g1, b1, g2, b2, *tables):
    s, n, d = x.shape
    hw = wq.shape[1]
    f = we.shape[1]
    hbm = pl.BlockSpec(memory_space=pl.ANY)
    vm = pl.BlockSpec(memory_space=pltpu.VMEM)
    sm = pl.BlockSpec(memory_space=pltpu.SMEM)
    sds = jax.ShapeDtypeStruct
    return pl.pallas_call(
        layer_kernel,
        out_shape=(
            sds((s, n, d), BF16), sds((s, n, d), BF16),
            sds((GROUP, 8, 8, 512), F32), sds((GROUP, 8, 8, 128), F32),
            sds((GROUP, 8, 8, 256), F32), sds((GROUP, 8, 8, 256), F32),
            sds((GROUP, 8, 8, 128), F32), sds((GROUP, 8, 8, 256), F32),
        ),
        in_specs=[sm, vm, hbm, hbm, hbm, hbm, hbm, hbm, hbm, hbm, vm, vm, vm, vm]
        + [hbm] * 6 + [vm] * 6,
        out_specs=(hbm,) * 8,
        scratch_shapes=[
            pltpu.VMEM((s, n, d), BF16),
            pltpu.VMEM((s, n, d), BF16),
            pltpu.VMEM((3, d, hw), BF16),
            pltpu.VMEM((hw, d), BF16),
            pltpu.VMEM((d, f), BF16),
            pltpu.VMEM((f, d), BF16),
            pltpu.VMEM((3, 8, RANK, d), BF16),
            pltpu.VMEM((3, 8, RANK, hw), BF16),
            pltpu.VMEM((s, 3, n, hw), BF16),
            pltpu.VMEM((s, n, hw), BF16),
            pltpu.VMEM((s, n, n), F32),
            pltpu.VMEM((s, RANK, n), F32),
            pltpu.VMEM((s, n, d), F32),
            pltpu.VMEM((s, n, 128), F32),
            pltpu.VMEM((s, n, f), BF16),
            pltpu.VMEM((s, n, f), BF16),
            pltpu.VMEM((s, n, d), F32),
            pltpu.VMEM((s, n, d), F32),
            pltpu.VMEM((n, d), BF16),
            pltpu.VMEM((5, n, hw), BF16),
            pltpu.VMEM((n, 128), F32),
            pltpu.VMEM((s, 3, RANK, n), BF16),
            pltpu.VMEM((s, RANK, n), BF16),
            pltpu.VMEM((RANK, n), F32),
            pltpu.VMEM((s, 6 * RANK, n), F32),
            pltpu.VMEM((s, 6 * RANK, n), F32),
            pltpu.VMEM((s, n, d), BF16),
            pltpu.VMEM((s, 8, 128), F32),
            pltpu.VMEM((GROUP, s, 8, 128), F32),
            pltpu.VMEM((s, GROUP, 8, EARLY), F32),
            pltpu.VMEM((s, GROUP, 8, LATE), F32),
            pltpu.VMEM((GROUP, s, 8, EARLY), F32),
            pltpu.VMEM((GROUP, s, 8, LATE), F32),
            pltpu.VMEM((8, 8, 512), F32),
            pltpu.VMEM((8, 8, 128), F32),
            pltpu.VMEM((8, 8, 256), F32),
            pltpu.VMEM((8, 8, 256), F32),
            pltpu.SemaphoreType.DMA((14,)),
            pltpu.SemaphoreType.DMA((2,)),
            pltpu.SemaphoreType.DMA((2,)),
            pltpu.SemaphoreType.DMA((2,)),
            pltpu.SemaphoreType.REGULAR((2,)),
            pltpu.SemaphoreType.DMA((2, 4)),
            pltpu.SemaphoreType.DMA((2, 4)),
            pltpu.SemaphoreType.DMA((GROUP,)),
            pltpu.SemaphoreType.DMA((GROUP,)),
            pltpu.SemaphoreType.DMA((2, 2, GROUP)),
            pltpu.SemaphoreType.DMA((2, 2, GROUP)),
            pltpu.SemaphoreType.DMA((2, 2, 4)),
            pltpu.SemaphoreType.DMA((2, 2, 4)),
            pltpu.SemaphoreType.DMA((2, 2, 4, 4)),
            pltpu.SemaphoreType.DMA((2, 2, 4, 4)),
            pltpu.SemaphoreType.DMA((2, 2)),
            pltpu.SemaphoreType.DMA((2, 4)),
            pltpu.SemaphoreType.DMA((2, 4)),
        ],
        compiler_params=pltpu.CompilerParams(
            collective_id=0, has_side_effects=True, vmem_limit_bytes=63 * 1024 * 1024
        ),
    )(ids, seg, x, cot, wq, wk, wv, wo, we, wc, g1, b1, g2, b2, *tables)


def on_device(
    tokens, cotangent, segment_ids, adapter_ids, query_weight, key_weight, value_weight, output_weight,
    expand_weight, contract_weight, first_gain, first_shift, second_gain, second_shift,
    query_down, query_up, key_down, key_up, value_down, value_up, output_down, output_up,
    expand_down, expand_up, contract_down, contract_up,
):
    seqs, length = segment_ids.shape
    width = tokens.shape[1]
    turn = lambda t: jnp.swapaxes(t, 1, 2)
    line = lambda v: v.reshape(1, -1)
    out, grad, *tables = layer(
        adapter_ids, segment_ids.astype(F32),
        tokens.reshape(seqs, length, width), cotangent.reshape(seqs, length, width),
        query_weight, key_weight, value_weight, output_weight, expand_weight, contract_weight,
        line(first_gain), line(first_shift), line(second_gain), line(second_shift),
        turn(query_down), turn(key_down), turn(value_down), query_up, key_up, value_up,
        turn(output_down), output_up, turn(expand_down), expand_up, turn(contract_down), contract_up,
    )
    out, grad, *tables = place(out, grad, tables, query_weight.shape[1], expand_weight.shape[1])
    count = lax.axis_size("dp")
    if count > GROUP:
        across = [list(range(i, count, GROUP)) for i in range(GROUP)]
        tables = lax.psum(tuple(tables), "dp", axis_index_groups=across)
    qd, qu, kd, ku, vd, vu, od, ou, ed, eu, cd, cu = tables
    return (
        out.reshape(tokens.shape), grad.reshape(tokens.shape),
        turn(qd), qu, turn(kd), ku, turn(vd), vu, turn(od), ou, turn(ed), eu, turn(cd), cu,
    )


def solution(mesh):
    cols = P(None, None, "tensor")
    mid = P(None, "tensor", None)
    return jax.shard_map(
        on_device,
        mesh=mesh,
        in_specs=(
            P("dp", None), P("dp", None), P("dp", None), P("dp"),
            P(None, "tensor"), P(None, "tensor"), P(None, "tensor"), P("tensor", None),
            P(None, "tensor"), P("tensor", None), P(), P(), P(), P(),
            P(), cols, P(), cols, P(), cols, mid, P(), P(), cols, mid, P(),
        ),
        out_specs=(
            P("dp", None), P("dp", None), P(), cols, P(), cols, P(), cols, mid, P(), P(), cols, mid, P(),
        ),
        check_vma=False,
    )
```

```python
import jax
import jax.numpy as jnp
from jax import lax
from jax.experimental import pallas as pl
from jax.experimental.pallas import tpu as pltpu
from jax.sharding import PartitionSpec as P

HEAD_WIDTH = 64
RANK = 16
MESH = pl.DeviceIdType.MESH
F32 = jnp.float32
BF16 = jnp.bfloat16
EPS = 1e-05
ROWS = 128
GROUP = 16
EARLY, LATE = 640, 512


def nn(a, b):
    return jnp.dot(a, b, preferred_element_type=F32)


def nt(a, b):
    return lax.dot_general(a, b, (((1,), (1,)), ((), ())), preferred_element_type=F32)


def split(v):
    hi = v.astype(BF16)
    return hi, (v - hi.astype(F32)).astype(BF16)


def nn_wide(v, b):
    hi, lo = split(v)
    return nn(hi, b) + nn(lo, b)


def gelu_parts(v):
    z = jnp.abs(v) * 0.7071067811865476
    t = 1.0 / (1.0 + 0.3275911 * z)
    e = jnp.exp(v * v * -0.5)
    tail = t * (
        0.127414796 + t * (-0.142248368 + t * (0.7107068705 + t * (-0.7265760135 + t * 0.5307027145)))
    ) * e
    cdf = jnp.where(v >= 0, 1.0 - tail, tail)
    return v * cdf, cdf + v * (e * 0.3989422804014327)


def layer_kernel(
    ids, seg, x_hbm, cot_hbm, wq, wk, wv, wo_hbm, we_hbm, wc_hbm, g1, b1, g2, b2,
    qd, kd, vd, qu, ku, vu, od, ou, ed, eu, cd, cu,
    out_hbm, grad_hbm, geu, ger, glu, glr, her, hlr,
    x, cot, wp, wo, we, wc, dtab, utab, qkv, heads, bias, lse, xhat, rstd, hidden, slope, acc, recv,
    row, d_heads, d_qkv, dq_t, u_cat, d_cat, lcol, rank_t, rank_e, drow, mine_rk, their_rk, stage_out,
    pick_mine, picks, pack_e, pack_l, rs_e, rs_l, dense_eu, dense_er, dense_lu, dense_lr,
    load_sem, send_sem, recv_sem, out_sem, credit, rk_send, rk_recv, pick_send, pick_recv,
    rs_send_sem, rs_recv_sem, z_send, z_recv, plane_send, plane_recv, own_sem, swap_send, swap_recv,
):
    dp = lax.axis_index("dp")
    core = lax.axis_index("tensor")
    partner = (dp, 1 - core)
    first = (core == 0).astype(F32)
    me = lax.rem(dp, GROUP)
    base = dp - me
    half = pl.ds(pl.multiple_of(core * 512, 512), 512)

    def load(i, src, dst):
        cp = pltpu.make_async_copy(src, dst, load_sem.at[i])
        cp.start()
        return cp

    loads = [load(0, x_hbm, x)]
    tabs = []
    for i, (w, d, u) in enumerate(((wq, qd, qu), (wk, kd, ku), (wv, vd, vu))):
        tabs.append(load(1 + i, w, wp.at[:, pl.ds(512 * i, 512)]))
        tabs.append(load(4 + i, d, dtab.at[i]))
        tabs.append(load(7 + i, u, utab.at[i]))
    load_wo = load(10, wo_hbm, wo)
    load_we = load(11, we_hbm, we)
    load_wc = load(12, wc_hbm, wc)
    load_cot = load(13, cot_hbm, cot)

    def peer(k):
        return (base + lax.bitwise_xor(me, k), core)

    barrier = pltpu.get_barrier_semaphore()
    pl.semaphore_signal(barrier, inc=1, device_id=partner, device_id_type=MESH)

    def greet(k, c):
        pl.semaphore_signal(barrier, inc=1, device_id=peer(k), device_id_type=MESH)
        return c

    lax.fori_loop(1, GROUP, greet, 0)
    pl.semaphore_wait(barrier, GROUP)

    def remote(src, dst, ss, rs, to):
        return pltpu.make_async_remote_copy(
            src_ref=src, dst_ref=dst, send_sem=ss, recv_sem=rs, device_id=to, device_id_type=MESH
        )

    def pick_copy(k):
        return remote(pick_mine, picks.at[me], pick_send.at[k], pick_recv.at[k], peer(k))

    table_id = lax.broadcasted_iota(jnp.int32, (8, 128), 0)
    for s in range(2):
        pick_mine[s] = (table_id == ids[s]).astype(F32)
    picks[me] = pick_mine[...]

    def send_pick(k, c):
        pick_copy(k).start()
        return c

    lax.fori_loop(1, GROUP, send_pick, 0)

    def rk_copy(s, i):
        rows = pl.ds(i * RANK, RANK if i < 3 else 3 * RANK)
        return remote(
            mine_rk.at[s, rows], their_rk.at[s, rows], rk_send.at[s, i], rk_recv.at[s, i], partner
        )

    def rank_sum(s, i, rows):
        rk_copy(s, i).wait()
        at = slice(i * RANK, i * RANK + rows)
        return mine_rk[s, at, :] + their_rk[s, at, :]

    packs, parts, swapped = (pack_e, pack_l), (rs_e, rs_l), (her, hlr)
    denses, gathered = ((dense_eu, dense_er), (dense_lu, dense_lr)), ((geu, ger), (glu, glr))

    def shard_copy(g, s, k):
        to = lax.bitwise_xor(me, k)
        return remote(
            packs[g].at[s, to], parts[g].at[me, s], rs_send_sem.at[g, s, k], rs_recv_sem.at[g, s, k], peer(k)
        )

    def scatter(g, s):
        parts[g][me, s] = packs[g][s, me]

        def go(k, c):
            shard_copy(g, s, k).start()
            return c

        lax.fori_loop(1, GROUP, go, 0)

    def combine(g):
        def wait(k, c):
            for s in range(2):
                shard_copy(g, s, k).wait()
            return c

        lax.fori_loop(1, GROUP, wait, 0)

        def add(m, total):
            for s in range(2):
                part = parts[g][m, s]
                total = tuple(
                    t + part * jnp.broadcast_to(picks[m, s, a:a + 1, 0:1], part.shape)
                    for a, t in enumerate(total)
                )
            return total

        zero = jnp.zeros(parts[g].shape[2:], F32)
        for a, t in enumerate(lax.fori_loop(0, GROUP, add, (zero,) * 8)):
            w = denses[g][0].shape[2]
            denses[g][0][a] = t[:, :w]
            denses[g][1][a] = t[:, w:]

    def own_copy(g, i):
        return pltpu.make_async_copy(denses[g][i], gathered[g][i].at[me], own_sem.at[g, i])

    def z_copy(g, i, u):
        return remote(
            denses[g][i], gathered[g][i].at[me], z_send.at[g, i, u], z_recv.at[g, i, u], peer(4 * u)
        )

    def slot(u, k):
        return lax.bitwise_xor(me, 4 * u + k)

    def plane_copy(g, i, u, way):
        to = gathered[g][i].at[slot(u, 0)]
        return remote(
            denses[g][i] if u == 0 else to, to, plane_send.at[g, i, u, way], plane_recv.at[g, i, u, way],
            peer(way + 1),
        )

    def onward_copy(g, i, u, way):
        at = gathered[g][i].at[slot(u, way + 1), pl.ds(4 * way, 4)]
        return remote(
            at, at, plane_send.at[g, i, u, 2 + way], plane_recv.at[g, i, u, 2 + way], peer(2 - way)
        )

    def swap_copy(g, u):
        plane = pl.ds(slot(u, 0) // 4 * 4, 4)
        return remote(
            gathered[g][1].at[plane], swapped[g].at[plane], swap_send.at[g, u], swap_recv.at[g, u], partner
        )

    both = [(i, way) for i in range(2) for way in range(2)]

    def gather_first(g):
        for i in range(2):
            own_copy(g, i).start()
            for u in (1, 2, 3):
                z_copy(g, i, u).start()
        for i, way in both:
            plane_copy(g, i, 0, way).start()

    def gather_unit(g, u):
        for i in range(2):
            z_copy(g, i, u).wait_recv()
        for i, way in both:
            plane_copy(g, i, u, way).start()

    def gather_onward(g, u):
        for i, way in both:
            plane_copy(g, i, u, way).wait_recv()
            onward_copy(g, i, u, way).start()

    def gather_swap(g, u):
        if u == 0:
            for i in range(2):
                own_copy(g, i).wait()
        for i, way in both:
            onward_copy(g, i, u, way).wait_recv()
        swap_copy(g, u).start()

    def gather_end(g):
        for u in (1, 2, 3):
            for i in range(2):
                z_copy(g, i, u).wait_send()
        for u in range(4):
            for i, way in both:
                plane_copy(g, i, u, way).wait_send()
                onward_copy(g, i, u, way).wait_send()
            swap_copy(g, u).wait()

    def exchange(s):
        return pltpu.make_async_remote_copy(
            src_ref=acc.at[s], dst_ref=recv.at[s], send_sem=send_sem.at[s], recv_sem=recv_sem.at[s],
            device_id=partner, device_id_type=MESH,
        )

    def taken(s):
        pl.semaphore_signal(credit.at[s], inc=1, device_id=partner, device_id_type=MESH)

    def send(s):
        pl.semaphore_wait(credit.at[s], 1)
        exchange(s).start()

    n = x.shape[1]
    hw = heads.shape[2]
    pairs = hw // 128
    chunks = hidden.shape[2] // 512
    lane = lax.broadcasted_iota(jnp.int32, (n, 128), 1)
    low_half = lane < HEAD_WIDTH

    for cp in loads + tabs:
        cp.wait()

    u_cat[...] = jnp.zeros_like(u_cat)
    d_cat[...] = jnp.zeros_like(d_cat)

    def stack_tables(aid):
        for p in range(3):
            for r in (0, 64):
                rows = slice(r + RANK * p, r + RANK * p + RANK)
                d_cat[rows, :] = dtab[p, aid]
                u_cat[rows, hw * p:hw * p + hw] = utab[p, aid]

    def twice(t):
        return jnp.concatenate([t, t], axis=0)

    def wide(v, at):
        hi = v.astype(BF16).astype(F32)
        return jnp.where(lax.broadcasted_iota(jnp.int32, v.shape, 1) < at, hi, v - hi).astype(BF16)

    def term(v, right):
        k = v.shape[0]
        hi, lo = split(v)
        both_parts = nn(jnp.concatenate([hi, lo], axis=0), right)
        return both_parts[:k] + both_parts[k:]

    def stage1(s, carry):
        aid = ids[s]
        seg_row = seg[pl.ds(s, 1), :]
        seg_col = jnp.broadcast_to(seg_row, (128, n)).T
        for j in range(n // 128):
            same = seg_col == seg_row[:, j * 128:(j + 1) * 128]
            bias[s, :, j * 128:(j + 1) * 128] = jnp.where(same, 0.0, -1e30)
        stack_tables(aid)
        rank = jnp.where(lane < 64, nt(x[s], d_cat[...]), 0.0)
        rank_t[s] = rank.T[0:3 * RANK, :].astype(BF16)
        rank = rank.astype(BF16)

        def project(p, c):
            at = pl.ds(pl.multiple_of(p * hw, hw), hw)
            scale = jnp.where(p == 0, 0.125, 1.0)
            qkv[s, p] = ((nn(x[s], wp[:, at]) + nn(rank, u_cat[:, at])) * scale).astype(BF16)
            return c

        lax.fori_loop(0, 3, project, 0)

        def pair(hp, c):
            at = pl.ds(pl.multiple_of(hp * 128, 128), 128)
            k2 = qkv[s, 1, :, at]
            v2 = jnp.concatenate([qkv[s, 2, :, at], jnp.ones((n, 128), BF16)], axis=1)
            for r in range(2):
                rows = slice(r * (n // 2), (r + 1) * (n // 2))
                q2 = qkv[s, 0, rows, at]
                outs = []
                ln = lane[rows]
                for j in range(2):
                    mine = (ln < HEAD_WIDTH) if j == 0 else (ln >= HEAD_WIDTH)
                    score = nt(jnp.where(mine, q2, jnp.zeros_like(q2)), k2) + bias[s, rows, :]
                    top = jnp.max(score, axis=1, keepdims=True)
                    e = jnp.exp(score - top).astype(BF16)
                    parts_ = nn(e, v2)
                    total = parts_[:, 128:]
                    outs.append(parts_[:, :128] / total)
                    old = lcol[rows, :]
                    lcol[rows, :] = jnp.where(ln == 2 * hp + j, top + jnp.log(total), old)
                heads[s, rows, at] = jnp.where(ln < HEAD_WIDTH, outs[0], outs[1]).astype(BF16)
            return c

        lax.fori_loop(0, pairs, pair, 0)
        lse[s] = lcol[...].T[:lse.shape[1], :]

        @pl.when(s == 0)
        def _():
            load_wo.wait()

        hs = heads[s]
        ro = nt(hs, twice(od[aid]))
        mine_rk[s, 0:RANK, :] = ro.T[0:RANK, :]
        rk_copy(s, 0).start()
        acc[s] = nn(hs, wo[...]) + nn(wide(ro, RANK), twice(ou[aid]))
        exchange(s).start()
        return carry

    lax.fori_loop(0, 2, stage1, 0)

    def stage2(s, carry):
        aid = ids[s]
        exchange(s).wait()

        def norm(i, c):
            rows = pl.ds(pl.multiple_of(i * ROWS, ROWS), ROWS)
            h = x[s, rows, :].astype(F32) + (acc[s, rows, :] + recv[s, rows, :])
            mean = jnp.mean(h, axis=1, keepdims=True)
            h = h - mean
            inv = lax.rsqrt(jnp.mean(h * h, axis=1, keepdims=True) + EPS)
            h = h * inv
            xhat[s, rows, :] = h
            rstd[s, rows, :] = jnp.broadcast_to(inv, (ROWS, 128))
            row[rows, :] = (h * g1[...] + b1[...]).astype(BF16)
            return c

        lax.fori_loop(0, n // ROWS, norm, 0)
        taken(s)
        rank = nt(row[...], ed[aid])
        rank_e[s] = rank.T.astype(BF16)
        rank = rank.astype(BF16)

        def expand(c):
            at = slice(512 * c, 512 * c + 512)
            return nn(row[...], we[:, at]) + nn(rank, eu[aid, :, at])

        before = expand(0)
        for c in range(chunks):
            after = expand(c + 1) if c + 1 < chunks else None
            at = slice(512 * c, 512 * c + 512)
            hid, sl = gelu_parts(before)
            hidden[s, :, at] = hid.astype(BF16)
            slope[s, :, at] = sl.astype(BF16)
            before = after
        rc = nt(hidden[s], twice(cd[aid]))
        mine_rk[s, RANK:2 * RANK, :] = rc.T[0:RANK, :]
        rk_copy(s, 1).start()
        rc = wide(rc, RANK)
        cu2 = twice(cu[aid])
        for c in range(2):
            at = slice(512 * c, 512 * c + 512)
            acc[s, :, at] = nn(hidden[s], wc[:, at]) + nn(rc, cu2[:, at])
        send(s)
        return carry

    load_we.wait()
    load_wc.wait()
    lax.fori_loop(0, 2, stage2, 0)

    def put_out(s):
        return pltpu.make_async_copy(stage_out.at[s], out_hbm.at[s], out_sem.at[s])

    def put_grad(s):
        return pltpu.make_async_copy(stage_out.at[s], grad_hbm.at[s], out_sem.at[s])

    def stage3(s, carry):
        aid = ids[s]
        exchange(s).wait()

        def norm(i, c):
            rows = pl.ds(pl.multiple_of(i * ROWS, ROWS), ROWS)
            normed = xhat[s, rows, :] * g1[...] + b1[...]
            h = normed + (acc[s, rows, :] + recv[s, rows, :])
            mean = jnp.mean(h, axis=1, keepdims=True)
            h = h - mean
            inv = lax.rsqrt(jnp.mean(h * h, axis=1, keepdims=True) + EPS)
            h = h * inv
            stage_out[s, rows, :] = (h * g2[...] + b2[...]).astype(BF16)
            u = cot[s, rows, :].astype(F32) * g2[...]
            back = inv * (
                u - jnp.mean(u, axis=1, keepdims=True) - h * jnp.mean(u * h, axis=1, keepdims=True)
            )
            acc[s, rows, :] = back * first
            row[rows, :] = back.astype(BF16)
            return c

        lax.fori_loop(0, n // ROWS, norm, 0)
        taken(s)
        put_out(s).start()
        brc = nt(row[...], cu[aid])
        brc_t = brc.T.astype(BF16)
        brc = brc.astype(BF16)
        t_cu = term(rank_sum(s, 1, RANK), row[:, half])
        for q in range(4):
            for h in range(2):
                pack_e[s, 8 + 2 * q + h, :, 512:640] = t_cu[8 * h:8 * h + 8, 128 * q:128 * q + 128]
        re_t = rank_e[s]

        def early_parts(c, t, lanes):
            for q in range(2):
                for h in range(2):
                    pack_e[s, 4 * c + 2 * q + h, :, lanes] = t[8 * h:8 * h + 8, 256 * q:256 * q + 256]

        def contract_back(c):
            at = slice(512 * c, 512 * c + 512)
            return nt(row[...], wc[at, :]) + nn(brc, cd[aid, :, at])

        bh = contract_back(0)
        for c in range(chunks):
            after = contract_back(c + 1) if c + 1 < chunks else None
            at = slice(512 * c, 512 * c + 512)
            early_parts(c, nn(brc_t, hidden[s, :, at]), slice(256, 512))
            bb = (bh * slope[s, :, at].astype(F32)).astype(BF16)
            slope[s, :, at] = bb
            early_parts(c, nn(re_t, bb), slice(0, 256))
            bh = after
        br = nt(slope[s], twice(eu[aid]))
        mine_rk[s, 2 * RANK:3 * RANK, :] = br.T[0:RANK, :]
        rk_copy(s, 2).start()
        br = wide(br, RANK)
        ed2 = twice(ed[aid])
        for c in range(2):
            at = slice(512 * c, 512 * c + 512)
            acc[s, :, at] += nt(slope[s], we[at, :]) + nn(br, ed2[:, at])
        send(s)
        return carry

    load_cot.wait()
    lax.fori_loop(0, 2, stage3, 0)

    def early(s, carry):
        inner = (xhat[s, :, half] * g1[:, half] + b1[:, half]).astype(BF16)
        t_ed = term(rank_sum(s, 2, RANK), inner)
        for q in range(4):
            for h in range(2):
                pack_e[s, 2 * q + h, :, 512:640] = t_ed[8 * h:8 * h + 8, 128 * q:128 * q + 128]
        scatter(0, s)
        return carry

    lax.fori_loop(0, 2, early, 0)

    def put_late(s, t, up, down):
        for q in range(2):
            for h in range(2):
                part = slice(8 * h, 8 * h + 8), slice(256 * q, 256 * q + 256)
                if up is not None:
                    pack_l[s, 4 * t + 2 * q + h, :, 0:256] = up[part]
                if down is not None:
                    pack_l[s, 4 * t + 2 * q + h, :, 256:512] = down[part]

    def between(s, hp):
        def at(s_, hp_, f):
            @pl.when(jnp.logical_and(s == s_, hp == hp_))
            def _():
                f()

        def begin():
            combine(0)
            gather_first(0)

        def step(u):
            def f():
                gather_unit(0, u)
                gather_onward(0, u - 1)
            return f

        at(0, 3, begin)
        at(1, 0, step(1))
        at(1, 1, step(2))
        at(1, 3, step(3))

    def wait_picks(k, c):
        pick_copy(k).wait()
        return c

    lax.fori_loop(1, GROUP, wait_picks, 0)

    def stage4(s, carry):
        aid = ids[s]
        exchange(s).wait()

        def norm(i, c):
            rows = pl.ds(pl.multiple_of(i * ROWS, ROWS), ROWS)
            u = (acc[s, rows, :] + recv[s, rows, :]) * g1[...]
            h = xhat[s, rows, :]
            back = rstd[s, rows, 0:1] * (
                u - jnp.mean(u, axis=1, keepdims=True) - h * jnp.mean(u * h, axis=1, keepdims=True)
            )
            acc[s, rows, :] = back * first
            row[rows, :] = back.astype(BF16)
            return c

        lax.fori_loop(0, n // ROWS, norm, 0)
        taken(s)
        hs = heads[s]
        bro = nt(row[...], ou[aid])
        put_late(
            s, 3, nn(bro.T.astype(BF16), hs), term(rank_sum(s, 0, RANK), row[:, half])
        )
        d_heads[...] = (nt(row[...], wo[...]) + nn(bro.astype(BF16), od[aid])).astype(BF16)
        pick = (
            lax.broadcasted_iota(jnp.int32, (RANK, hw), 1) // HEAD_WIDTH
            == lax.broadcasted_iota(jnp.int32, (RANK, hw), 0)
        ).astype(BF16)
        hi, lo = split(d_heads[...].astype(F32) * hs.astype(F32))
        drow[...] = nt(pick, hi) + nt(pick, lo)

        def pair(hp, c):
            at = pl.ds(pl.multiple_of(hp * 128, 128), 128)
            q2 = qkv[s, 0, :, at]
            k2 = qkv[s, 1, :, at]
            v2 = qkv[s, 2, :, at]
            do2 = d_heads[:, at]
            k2t = k2.T
            zero = jnp.zeros_like(k2)
            dk, dv = [], []
            for j in range(2):
                mine = low_half if j == 0 else jnp.logical_not(low_half)
                h = 2 * hp + j
                st = nt(jnp.where(mine, k2, zero), q2) + bias[s]
                pt = jnp.exp(st - lse[s, pl.ds(h, 1), :])
                dpt = nt(jnp.where(mine, v2, zero), do2)
                dst = (pt * (dpt - drow[pl.ds(h, 1), :])).astype(BF16)
                dv.append(nn(pt.astype(BF16), do2))
                dk.append(nn(dst, q2))
                dqt = nn(k2t[j * HEAD_WIDTH:(j + 1) * HEAD_WIDTH, :], dst) * 0.125
                dq_t[pl.ds(pl.multiple_of(h * HEAD_WIDTH, HEAD_WIDTH), HEAD_WIDTH), :] = dqt.astype(BF16)
            to = pl.multiple_of(hp * 128, 128)
            d_qkv[:, pl.ds(hw + to, 128)] = jnp.where(low_half, dk[0], dk[1]).astype(BF16)
            d_qkv[:, pl.ds(2 * hw + to, 128)] = jnp.where(low_half, dv[0], dv[1]).astype(BF16)
            between(s, hp)
            return c

        lax.fori_loop(0, pairs, pair, 0)
        d_qkv[:, 0:hw] = dq_t[...].T
        stack_tables(aid)
        br = nt(d_qkv[...], u_cat[...])
        mine_rk[s, 3 * RANK:6 * RANK, :] = br.T[0:3 * RANK, :]
        rk_copy(s, 3).start()
        br = wide(br, 64)
        for p in range(3):
            put_late(
                s, p, nn(rank_t[s, RANK * p:RANK * p + RANK, :], d_qkv[:, hw * p:hw * p + hw]), None
            )
        t_d = term(rank_sum(s, 3, 3 * RANK), x[s, :, half])
        for p in range(3):
            put_late(s, p, None, t_d[RANK * p:RANK * p + RANK, :])
        scatter(1, s)
        for c in range(2):
            at = slice(512 * c, 512 * c + 512)
            acc[s, :, at] += nt(d_qkv[...], wp[at, :]) + nn(br, d_cat[:, at])
        send(s)
        return carry

    lax.fori_loop(0, 2, stage4, 0)

    gather_onward(0, 3)

    def stage5(s, carry):
        exchange(s).wait()
        put_out(s).wait()

        def add(i, c):
            rows = pl.ds(pl.multiple_of(i * ROWS, ROWS), ROWS)
            stage_out[s, rows, :] = (acc[s, rows, :] + recv[s, rows, :]).astype(BF16)
            return c

        lax.fori_loop(0, n // ROWS, add, 0)
        put_grad(s).start()
        return carry

    lax.fori_loop(0, 2, stage5, 0)
    for u in range(4):
        gather_swap(0, u)
    combine(1)
    gather_first(1)
    for u in (1, 2, 3):
        gather_unit(1, u)
        gather_onward(1, u - 1)
    gather_onward(1, 3)
    for u in range(4):
        gather_swap(1, u)
    gather_end(0)
    gather_end(1)
    put_grad(0).wait()
    put_grad(1).wait()


def place_kernel(*refs):
    src, dst, src_v, dst_v = refs[:8], refs[8:22], refs[22:30], refs[30:42]
    in_sem, out_sem = refs[42:]
    core = lax.axis_index("tensor")
    loads = [pltpu.make_async_copy(a, b, in_sem.at[i]) for i, (a, b) in enumerate(zip(src, src_v))]
    for cp in loads:
        cp.start()
    ends = []

    def store(v, i):
        cp = pltpu.make_async_copy(v, dst[i], out_sem.at[i])
        cp.start()
        ends.append(cp)

    qd, qu, kd, ku, vd, vu, od, ou, ed, eu, cd, cu = range(12)
    up, down, low = (qu, ku, vu, od), (qd, kd, vd, ou), (ed, cu)
    geu, ger, glu, glr, her, hlr = src_v[:6]

    def lanes(side, width, i):
        return pl.ds(pl.multiple_of(side * 512 + width * i, 128), width)

    def rows(n):
        return slice(8 * (n % 2), 8 * (n % 2) + 8)

    loads[0].wait()
    for n in range(GROUP):
        at = slice(256 * (n // 2), 256 * (n // 2) + 256)
        dst_v[eu][:, rows(n), at] = geu[n, :, :, 0:256]
        dst_v[cd][:, rows(n), at] = geu[n, :, :, 256:512]
    store(dst_v[eu], 2 + eu)
    store(dst_v[cd], 2 + cd)
    for i in (1, 4):
        loads[i].wait()
    for n in range(GROUP):
        v = dst_v[low[n // 8]]
        v[:, rows(n), lanes(core, 128, n % 8 // 2)] = ger[n]
        v[:, rows(n), lanes(1 - core, 128, n % 8 // 2)] = her[n]
    store(dst_v[ed], 2 + ed)
    store(dst_v[cu], 2 + cu)
    for i in (2, 3, 5):
        loads[i].wait()
    for t in range(4):
        for n in range(4 * t, 4 * t + 4):
            q = n % 4 // 2
            dst_v[up[t]][:, rows(n), 256 * q:256 * q + 256] = glu[n]
            dst_v[down[t]][:, rows(n), lanes(core, 256, q)] = glr[n]
            dst_v[down[t]][:, rows(n), lanes(1 - core, 256, q)] = hlr[n]
        store(dst_v[up[t]], 2 + up[t])
        store(dst_v[down[t]], 2 + down[t])
    for i in range(2):
        loads[6 + i].wait()
        store(src_v[6 + i], i)
    for cp in ends:
        cp.wait()


def place(out, grad, tables, hw, f):
    s, n, d = out.shape
    hbm = pl.BlockSpec(memory_space=pl.ANY)
    widths = (d, hw, d, hw, d, hw, hw, d, d, f, f, d)
    args = (*tables, out, grad)
    return pl.pallas_call(
        place_kernel,
        out_shape=[jax.ShapeDtypeStruct((s, n, d), BF16)] * 2
        + [jax.ShapeDtypeStruct((8, RANK, w), F32) for w in widths],
        in_specs=[hbm] * 8,
        out_specs=[hbm] * 14,
        scratch_shapes=[pltpu.VMEM(a.shape, a.dtype) for a in args]
        + [pltpu.VMEM((8, RANK, w), F32) for w in widths]
        + [pltpu.SemaphoreType.DMA((8,)), pltpu.SemaphoreType.DMA((14,))],
        compiler_params=pltpu.CompilerParams(vmem_limit_bytes=60 * 1024 * 1024),
    )(*args)


def layer(ids, seg, x, cot, wq, wk, wv, wo, we, wc, g1, b1, g2, b2, *tables):
    s, n, d = x.shape
    hw = wq.shape[1]
    f = we.shape[1]
    hbm = pl.BlockSpec(memory_space=pl.ANY)
    vm = pl.BlockSpec(memory_space=pltpu.VMEM)
    sm = pl.BlockSpec(memory_space=pltpu.SMEM)
    sds = jax.ShapeDtypeStruct
    return pl.pallas_call(
        layer_kernel,
        out_shape=(
            sds((s, n, d), BF16), sds((s, n, d), BF16),
            sds((GROUP, 8, 8, 512), F32), sds((GROUP, 8, 8, 128), F32),
            sds((GROUP, 8, 8, 256), F32), sds((GROUP, 8, 8, 256), F32),
            sds((GROUP, 8, 8, 128), F32), sds((GROUP, 8, 8, 256), F32),
        ),
        in_specs=[sm, vm, hbm, hbm, hbm, hbm, hbm, hbm, hbm, hbm, vm, vm, vm, vm]
        + [hbm] * 6 + [vm] * 6,
        out_specs=(hbm,) * 8,
        scratch_shapes=[
            pltpu.VMEM((s, n, d), BF16),
            pltpu.VMEM((s, n, d), BF16),
            pltpu.VMEM((d, 3 * hw), BF16),
            pltpu.VMEM((hw, d), BF16),
            pltpu.VMEM((d, f), BF16),
            pltpu.VMEM((f, d), BF16),
            pltpu.VMEM((3, 8, RANK, d), BF16),
            pltpu.VMEM((3, 8, RANK, hw), BF16),
            pltpu.VMEM((s, 3, n, hw), BF16),
            pltpu.VMEM((s, n, hw), BF16),
            pltpu.VMEM((s, n, n), F32),
            pltpu.VMEM((s, RANK, n), F32),
            pltpu.VMEM((s, n, d), F32),
            pltpu.VMEM((s, n, 128), F32),
            pltpu.VMEM((s, n, f), BF16),
            pltpu.VMEM((s, n, f), BF16),
            pltpu.VMEM((s, n, d), F32),
            pltpu.VMEM((s, n, d), F32),
            pltpu.VMEM((n, d), BF16),
            pltpu.VMEM((n, hw), BF16),
            pltpu.VMEM((n, 3 * hw), BF16),
            pltpu.VMEM((hw, n), BF16),
            pltpu.VMEM((128, 3 * hw), BF16),
            pltpu.VMEM((128, d), BF16),
            pltpu.VMEM((n, 128), F32),
            pltpu.VMEM((s, 3 * RANK, n), BF16),
            pltpu.VMEM((s, RANK, n), BF16),
            pltpu.VMEM((RANK, n), F32),
            pltpu.VMEM((s, 6 * RANK, n), F32),
            pltpu.VMEM((s, 6 * RANK, n), F32),
            pltpu.VMEM((s, n, d), BF16),
            pltpu.VMEM((s, 8, 128), F32),
            pltpu.VMEM((GROUP, s, 8, 128), F32),
            pltpu.VMEM((s, GROUP, 8, EARLY), F32),
            pltpu.VMEM((s, GROUP, 8, LATE), F32),
            pltpu.VMEM((GROUP, s, 8, EARLY), F32),
            pltpu.VMEM((GROUP, s, 8, LATE), F32),
            pltpu.VMEM((8, 8, 512), F32),
            pltpu.VMEM((8, 8, 128), F32),
            pltpu.VMEM((8, 8, 256), F32),
            pltpu.VMEM((8, 8, 256), F32),
            pltpu.SemaphoreType.DMA((14,)),
            pltpu.SemaphoreType.DMA((2,)),
            pltpu.SemaphoreType.DMA((2,)),
            pltpu.SemaphoreType.DMA((2,)),
            pltpu.SemaphoreType.REGULAR((2,)),
            pltpu.SemaphoreType.DMA((2, 4)),
            pltpu.SemaphoreType.DMA((2, 4)),
            pltpu.SemaphoreType.DMA((GROUP,)),
            pltpu.SemaphoreType.DMA((GROUP,)),
            pltpu.SemaphoreType.DMA((2, 2, GROUP)),
            pltpu.SemaphoreType.DMA((2, 2, GROUP)),
            pltpu.SemaphoreType.DMA((2, 2, 4)),
            pltpu.SemaphoreType.DMA((2, 2, 4)),
            pltpu.SemaphoreType.DMA((2, 2, 4, 4)),
            pltpu.SemaphoreType.DMA((2, 2, 4, 4)),
            pltpu.SemaphoreType.DMA((2, 2)),
            pltpu.SemaphoreType.DMA((2, 4)),
            pltpu.SemaphoreType.DMA((2, 4)),
        ],
        compiler_params=pltpu.CompilerParams(
            collective_id=0, has_side_effects=True, vmem_limit_bytes=63 * 1024 * 1024
        ),
    )(ids, seg, x, cot, wq, wk, wv, wo, we, wc, g1, b1, g2, b2, *tables)


def on_device(
    tokens, cotangent, segment_ids, adapter_ids, query_weight, key_weight, value_weight, output_weight,
    expand_weight, contract_weight, first_gain, first_shift, second_gain, second_shift,
    query_down, query_up, key_down, key_up, value_down, value_up, output_down, output_up,
    expand_down, expand_up, contract_down, contract_up,
):
    seqs, length = segment_ids.shape
    width = tokens.shape[1]
    turn = lambda t: jnp.swapaxes(t, 1, 2)
    line = lambda v: v.reshape(1, -1)
    out, grad, *tables = layer(
        adapter_ids, segment_ids.astype(F32),
        tokens.reshape(seqs, length, width), cotangent.reshape(seqs, length, width),
        query_weight, key_weight, value_weight, output_weight, expand_weight, contract_weight,
        line(first_gain), line(first_shift), line(second_gain), line(second_shift),
        turn(query_down), turn(key_down), turn(value_down), query_up, key_up, value_up,
        turn(output_down), output_up, turn(expand_down), expand_up, turn(contract_down), contract_up,
    )
    out, grad, *tables = place(out, grad, tables, query_weight.shape[1], expand_weight.shape[1])
    count = lax.axis_size("dp")
    if count > GROUP:
        across = [list(range(i, count, GROUP)) for i in range(GROUP)]
        tables = lax.psum(tuple(tables), "dp", axis_index_groups=across)
    qd, qu, kd, ku, vd, vu, od, ou, ed, eu, cd, cu = tables
    return (
        out.reshape(tokens.shape), grad.reshape(tokens.shape),
        turn(qd), qu, turn(kd), ku, turn(vd), vu, turn(od), ou, turn(ed), eu, turn(cd), cu,
    )


def solution(mesh):
    cols = P(None, None, "tensor")
    mid = P(None, "tensor", None)
    return jax.shard_map(
        on_device,
        mesh=mesh,
        in_specs=(
            P("dp", None), P("dp", None), P("dp", None), P("dp"),
            P(None, "tensor"), P(None, "tensor"), P(None, "tensor"), P("tensor", None),
            P(None, "tensor"), P("tensor", None), P(), P(), P(), P(),
            P(), cols, P(), cols, P(), cols, mid, P(), P(), cols, mid, P(),
        ),
        out_specs=(
            P("dp", None), P("dp", None), P(), cols, P(), cols, P(), cols, mid, P(), P(), cols, mid, P(),
        ),
        check_vma=False,
    )
```

```python
import jax
import jax.numpy as jnp
from jax import lax
from jax.experimental import pallas as pl
from jax.experimental.pallas import tpu as pltpu
from jax.sharding import PartitionSpec as P

HEAD_WIDTH = 64
RANK = 16
MESH = pl.DeviceIdType.MESH
F32 = jnp.float32
BF16 = jnp.bfloat16
EPS = 1e-05
ROWS = 128
GROUP = 16
LANES = (256, 384, 128, 384)
GROUPS = range(len(LANES))
SWAPPED = (1, 2, 3)


def nn(a, b):
    return jnp.dot(a, b, preferred_element_type=F32)


def nt(a, b):
    return lax.dot_general(a, b, (((1,), (1,)), ((), ())), preferred_element_type=F32)


def split(v):
    hi = v.astype(BF16)
    return hi, (v - hi.astype(F32)).astype(BF16)


def nn_wide(v, b):
    hi, lo = split(v)
    return nn(hi, b) + nn(lo, b)


def gelu_parts(v):
    z = jnp.abs(v) * 0.7071067811865476
    t = 1.0 / (1.0 + 0.3275911 * z)
    e = jnp.exp(v * v * -0.5)
    tail = t * (
        0.127414796 + t * (-0.142248368 + t * (0.7107068705 + t * (-0.7265760135 + t * 0.5307027145)))
    ) * e
    cdf = jnp.where(v >= 0, 1.0 - tail, tail)
    return v * cdf, cdf + v * (e * 0.3989422804014327)


def layer_kernel(
    ids, seg, x_hbm, cot_hbm, wq, wk, wv, wo_hbm, we_hbm, wc_hbm, g1, b1, g2, b2,
    qd, kd, vd, qu, ku, vu, od_hbm, ou_hbm, ed_hbm, eu_hbm, cd_hbm, cu_hbm,
    out_hbm, grad_hbm, g0, g1_, g2_, g3, h1, h2, h3,
    x, cot, wp, wo, we, wc, dtab, utab, qkv, heads, bias, lse, xhat, rstd, hidden, slope, acc, recv,
    od, ou, ed, eu, cd, cu, row, back_rank, u_cat, d_cat, lcol, rank_t, rank_e, drow, mine_rk, their_rk, stage_out,
    pick_mine, picks, p0, p1, p2, p3, r0, r1, r2, r3, d0, d1, d2, d3,
    load_sem, send_sem, recv_sem, out_sem, credit, rk_send, rk_recv, pick_send, pick_recv,
    rs_send_sem, rs_recv_sem, z_send, z_recv, plane_send, plane_recv, own_sem, swap_send, swap_recv,
):
    dp = lax.axis_index("dp")
    core = lax.axis_index("tensor")
    partner = (dp, 1 - core)
    first = (core == 0).astype(F32)
    me = lax.rem(dp, GROUP)
    base = dp - me
    half = pl.ds(pl.multiple_of(core * 512, 512), 512)

    def load(i, src, dst):
        return pltpu.make_async_copy(src, dst, load_sem.at[i])

    load_x = [load(s, x_hbm.at[s], x.at[s]) for s in range(2)]
    load_d = [load(2 + i, t, dtab.at[i]) for i, t in enumerate((qd, kd, vd))]
    load_u = [load(5 + i, t, utab.at[i]) for i, t in enumerate((qu, ku, vu))]
    load_w = [load(8 + i, t, wp.at[:, pl.ds(512 * i, 512)]) for i, t in enumerate((wq, wk, wv))]
    load_o = [load(11, wo_hbm, wo), load(12, od_hbm, od), load(13, ou_hbm, ou)]
    load_f = [
        load(14, we_hbm, we), load(15, ed_hbm, ed), load(16, eu_hbm, eu),
        load(17, wc_hbm, wc), load(18, cd_hbm, cd), load(19, cu_hbm, cu),
    ]
    load_cot = load(20, cot_hbm, cot)
    for cp in load_x[:1] + load_d + load_w + load_u:
        cp.start()

    def peer(k):
        return (base + lax.bitwise_xor(me, k), core)

    barrier = pltpu.get_barrier_semaphore()
    pl.semaphore_signal(barrier, inc=1, device_id=partner, device_id_type=MESH)

    def greet(k, c):
        pl.semaphore_signal(barrier, inc=1, device_id=peer(k), device_id_type=MESH)
        return c

    lax.fori_loop(1, GROUP, greet, 0)

    def remote(src, dst, ss, rs, to):
        return pltpu.make_async_remote_copy(
            src_ref=src, dst_ref=dst, send_sem=ss, recv_sem=rs, device_id=to, device_id_type=MESH
        )

    def pick_copy(k):
        return remote(pick_mine, picks.at[me], pick_send.at[k], pick_recv.at[k], peer(k))

    table_id = lax.broadcasted_iota(jnp.int32, (8, 128), 0)
    for s in range(2):
        pick_mine[s] = (table_id == ids[s]).astype(F32)
    picks[me] = pick_mine[...]

    def send_pick(k, c):
        pick_copy(k).start()
        return c

    def meet():
        pl.semaphore_wait(barrier, GROUP)
        lax.fori_loop(1, GROUP, send_pick, 0)

    def rk_copy(s, i):
        rows = pl.ds(i * RANK, RANK if i < 3 else 3 * RANK)
        return remote(
            mine_rk.at[s, rows], their_rk.at[s, rows], rk_send.at[s, i], rk_recv.at[s, i], partner
        )

    def rank_sum(s, i, rows):
        rk_copy(s, i).wait()
        at = slice(i * RANK, i * RANK + rows)
        return mine_rk[s, at, :] + their_rk[s, at, :]

    packs, parts, denses = (p0, p1, p2, p3), (r0, r1, r2, r3), (d0, d1, d2, d3)
    gathered, swapped = (g0, g1_, g2_, g3), (None, h1, h2, h3)

    def pack(g, s, col, v):
        for b in range(v.shape[1] // 128):
            cut, ln = divmod(col + 128 * b, LANES[g])
            for h in range(2):
                packs[g][s, 2 * cut + h, :, ln:ln + 128] = v[8 * h:8 * h + 8, 128 * b:128 * b + 128]

    def shard_copy(g, s, k):
        to = lax.bitwise_xor(me, k)
        return remote(
            packs[g].at[s, to], parts[g].at[me, s], rs_send_sem.at[g, s, k], rs_recv_sem.at[g, s, k], peer(k)
        )

    def scatter(g, s):
        parts[g][me, s] = packs[g][s, me]

        def go(k, c):
            shard_copy(g, s, k).start()
            return c

        lax.fori_loop(1, GROUP, go, 0)

    def combine(g):
        def wait(k, c):
            for s in range(2):
                shard_copy(g, s, k).wait()
            return c

        lax.fori_loop(1, GROUP, wait, 0)

        cuts = range(0, LANES[g], 128)

        def add(m, total):
            for s in range(2):
                part = [parts[g][m, s, :, at:at + 128] for at in cuts]
                for a in range(8):
                    weight = jnp.broadcast_to(picks[m, s, a:a + 1, :], (8, 128))
                    total = [
                        t + weight * part[i % len(cuts)] if i // len(cuts) == a else t
                        for i, t in enumerate(total)
                    ]
            return tuple(total)

        total = lax.fori_loop(0, GROUP, add, (jnp.zeros((8, 128), F32),) * (8 * len(cuts)))
        for i, t in enumerate(total):
            a, at = divmod(i, len(cuts))
            denses[g][a, :, 128 * at:128 * at + 128] = t

    def own_copy(g):
        return pltpu.make_async_copy(denses[g], gathered[g].at[me], own_sem.at[g])

    def z_copy(g, u):
        return remote(denses[g], gathered[g].at[me], z_send.at[g, u], z_recv.at[g, u], peer(4 * u))

    def slot(u, k):
        return lax.bitwise_xor(me, 4 * u + k)

    def plane_copy(g, u, way):
        to = gathered[g].at[slot(u, 0)]
        return remote(
            denses[g] if u == 0 else to, to, plane_send.at[g, u, way], plane_recv.at[g, u, way], peer(way + 1)
        )

    def onward_copy(g, u, way):
        at = gathered[g].at[slot(u, way + 1), pl.ds(4 * way, 4)]
        return remote(at, at, plane_send.at[g, u, 2 + way], plane_recv.at[g, u, 2 + way], peer(2 - way))

    def swap_copy(g, u):
        plane = lax.bitwise_xor(me // 4, u)
        return plane >= 2, remote(
            gathered[g].at[pl.ds(4 * plane, 4)], swapped[g].at[pl.ds(4 * lax.rem(plane, 2), 4)],
            swap_send.at[g, u], swap_recv.at[g, u], partner,
        )

    def gather_first(g):
        own_copy(g).start()
        for u in (1, 2, 3):
            z_copy(g, u).start()
        for way in range(2):
            plane_copy(g, 0, way).start()

    def gather_unit(g, u):
        z_copy(g, u).wait_recv()
        for way in range(2):
            plane_copy(g, u, way).start()

    def gather_onward(g, u):
        for way in range(2):
            plane_copy(g, u, way).wait_recv()
            onward_copy(g, u, way).start()

    def gather_swap(g, u):
        if u == 0:
            own_copy(g).wait()
        for way in range(2):
            onward_copy(g, u, way).wait_recv()
        if g in SWAPPED:
            upper, copy = swap_copy(g, u)

            @pl.when(upper)
            def _():
                copy.start()

    def gather_end(g):
        for u in (1, 2, 3):
            z_copy(g, u).wait_send()
        for u in range(4):
            for way in range(2):
                plane_copy(g, u, way).wait_send()
                onward_copy(g, u, way).wait_send()
            if g in SWAPPED:
                upper, copy = swap_copy(g, u)

                @pl.when(upper)
                def _():
                    copy.wait()

    def gather_begin(g):
        combine(g)
        gather_first(g)

    def gather_step(g, u):
        if u < 4:
            gather_unit(g, u)
        gather_onward(g, u - 1)

    def gather_middle(g):
        for u in (1, 2, 3):
            gather_unit(g, u)
        gather_onward(g, 0)

    def gather_late(g):
        for u in (1, 2, 3):
            gather_onward(g, u)

    def gather_close(g):
        for u in range(4):
            gather_swap(g, u)

    def hosted(here, there, f):
        @pl.when(here == there)
        def _():
            f()

    def exchange(s):
        return pltpu.make_async_remote_copy(
            src_ref=acc.at[s], dst_ref=recv.at[s], send_sem=send_sem.at[s], recv_sem=recv_sem.at[s],
            device_id=partner, device_id_type=MESH,
        )

    def taken(s):
        pl.semaphore_signal(credit.at[s], inc=1, device_id=partner, device_id_type=MESH)

    def send(s):
        pl.semaphore_wait(credit.at[s], 1)
        exchange(s).start()

    n = x.shape[1]
    hw = heads.shape[2]
    pairs = hw // 128
    chunks = hidden.shape[2] // 512
    lane = lax.broadcasted_iota(jnp.int32, (n, 128), 1)
    low_half = lane < HEAD_WIDTH

    u_cat[...] = jnp.zeros_like(u_cat)
    d_cat[...] = jnp.zeros_like(d_cat)

    def stack_tables(aid):
        for p in range(3):
            for r in (0, 64):
                rows = slice(r + RANK * p, r + RANK * p + RANK)
                d_cat[rows, :] = dtab[p, aid]
                u_cat[rows, hw * p:hw * p + hw] = utab[p, aid]

    def twice(t):
        return jnp.concatenate([t, t], axis=0)

    def wide(v, at):
        hi = v.astype(BF16).astype(F32)
        return jnp.where(lax.broadcasted_iota(jnp.int32, v.shape, 1) < at, hi, v - hi).astype(BF16)

    def term(v, right):
        k = v.shape[0]
        hi, lo = split(v)
        both_parts = nn(jnp.concatenate([hi, lo], axis=0), right)
        return both_parts[:k] + both_parts[k:]

    def stage1(s, carry):
        aid = ids[s]
        seg_row = seg[pl.ds(s, 1), :].astype(F32)
        seg_col = jnp.broadcast_to(seg_row, (128, n)).T
        for j in range(n // 128):
            same = seg_col == seg_row[:, j * 128:(j + 1) * 128]
            bias[s, :, j * 128:(j + 1) * 128] = jnp.where(same, 0.0, -1e30)

        @pl.when(s == 0)
        def _():
            for cp in load_x[:1] + load_d + load_u:
                cp.wait()
            for cp in load_x[1:] + load_o:
                cp.start()

        @pl.when(s == 1)
        def _():
            load_x[1].wait()

        stack_tables(aid)
        rank = jnp.where(lane < 64, nt(x[s], d_cat[...]), 0.0)
        rank_t[s] = rank.T[0:3 * RANK, :].astype(BF16)
        rank = rank.astype(BF16)

        @pl.when(s == 0)
        def _():
            for cp in load_w:
                cp.wait()
            for cp in load_f + [load_cot]:
                cp.start()

        def project(p, c):
            at = pl.ds(pl.multiple_of(p * hw, hw), hw)
            scale = jnp.where(p == 0, 0.125, 1.0)
            qkv[s, p] = ((nn(x[s], wp[:, at]) + nn(rank, u_cat[:, at])) * scale).astype(BF16)
            return c

        lax.fori_loop(0, 3, project, 0)

        def pair(hp, c):
            at = pl.ds(pl.multiple_of(hp * 128, 128), 128)
            k2 = qkv[s, 1, :, at]
            v2 = jnp.concatenate([qkv[s, 2, :, at], jnp.ones((n, 128), BF16)], axis=1)
            for r in range(2):
                rows = slice(r * (n // 2), (r + 1) * (n // 2))
                q2 = qkv[s, 0, rows, at]
                outs = []
                ln = lane[rows]
                for j in range(2):
                    mine = (ln < HEAD_WIDTH) if j == 0 else (ln >= HEAD_WIDTH)
                    score = nt(jnp.where(mine, q2, jnp.zeros_like(q2)), k2) + bias[s, rows, :]
                    top = jnp.max(score, axis=1, keepdims=True)
                    e = jnp.exp(score - top).astype(BF16)
                    parts_ = nn(e, v2)
                    total = parts_[:, 128:]
                    outs.append(parts_[:, :128] / total)
                    old = lcol[rows, :]
                    lcol[rows, :] = jnp.where(ln == 2 * hp + j, top + jnp.log(total), old)
                heads[s, rows, at] = jnp.where(ln < HEAD_WIDTH, outs[0], outs[1]).astype(BF16)
            return c

        lax.fori_loop(0, pairs, pair, 0)
        lse[s] = lcol[...].T[:lse.shape[1], :]

        @pl.when(s == 0)
        def _():
            for cp in load_o:
                cp.wait()
            meet()

        hs = heads[s]
        ro = nt(hs, twice(od[aid]))
        mine_rk[s, 0:RANK, :] = ro.T[0:RANK, :]
        rk_copy(s, 0).start()
        acc[s] = nn(hs, wo[...]) + nn(wide(ro, RANK), twice(ou[aid]))
        exchange(s).start()
        return carry

    lax.fori_loop(0, 2, stage1, 0)

    def stage2(s, carry):
        aid = ids[s]
        exchange(s).wait()

        def norm(i, c):
            rows = pl.ds(pl.multiple_of(i * ROWS, ROWS), ROWS)
            h = x[s, rows, :].astype(F32) + (acc[s, rows, :] + recv[s, rows, :])
            mean = jnp.mean(h, axis=1, keepdims=True)
            h = h - mean
            inv = lax.rsqrt(jnp.mean(h * h, axis=1, keepdims=True) + EPS)
            h = h * inv
            xhat[s, rows, :] = h
            rstd[s, rows, :] = jnp.broadcast_to(inv, (ROWS, 128))
            row[rows, :] = (h * g1[...] + b1[...]).astype(BF16)
            return c

        lax.fori_loop(0, n // ROWS, norm, 0)
        taken(s)
        rank = nt(row[...], ed[aid])
        rank_e[s] = rank.T.astype(BF16)
        rank = rank.astype(BF16)

        def expand(c):
            at = slice(512 * c, 512 * c + 512)
            return nn(row[...], we[:, at]) + nn(rank, eu[aid, :, at])

        before = expand(0)
        for c in range(chunks):
            after = expand(c + 1) if c + 1 < chunks else None
            at = slice(512 * c, 512 * c + 512)
            hid, sl = gelu_parts(before)
            hidden[s, :, at] = hid.astype(BF16)
            slope[s, :, at] = sl.astype(BF16)
            before = after
        rc = nt(hidden[s], twice(cd[aid]))
        mine_rk[s, RANK:2 * RANK, :] = rc.T[0:RANK, :]
        rk_copy(s, 1).start()
        rc = wide(rc, RANK)
        cu2 = twice(cu[aid])
        for c in range(2):
            at = slice(512 * c, 512 * c + 512)
            acc[s, :, at] = nn(hidden[s], wc[:, at]) + nn(rc, cu2[:, at])
        send(s)
        return carry

    for cp in load_f:
        cp.wait()
    lax.fori_loop(0, 2, stage2, 0)

    def put_out(s):
        return pltpu.make_async_copy(stage_out.at[s], out_hbm.at[s], out_sem.at[s])

    def put_grad(s):
        return pltpu.make_async_copy(stage_out.at[s], grad_hbm.at[s], out_sem.at[s])

    def early(s):
        inner = (xhat[s, :, half] * g1[:, half] + b1[:, half]).astype(BF16)
        pack(1, s, 2048, term(rank_sum(s, 2, RANK), inner))
        scatter(1, s)

    def stage3(s, carry):
        aid = ids[s]
        exchange(s).wait()

        def norm(i, c):
            rows = pl.ds(pl.multiple_of(i * ROWS, ROWS), ROWS)
            normed = xhat[s, rows, :] * g1[...] + b1[...]
            h = normed + (acc[s, rows, :] + recv[s, rows, :])
            mean = jnp.mean(h, axis=1, keepdims=True)
            h = h - mean
            inv = lax.rsqrt(jnp.mean(h * h, axis=1, keepdims=True) + EPS)
            h = h * inv
            stage_out[s, rows, :] = (h * g2[...] + b2[...]).astype(BF16)
            u = cot[s, rows, :].astype(F32) * g2[...]
            back = inv * (
                u - jnp.mean(u, axis=1, keepdims=True) - h * jnp.mean(u * h, axis=1, keepdims=True)
            )
            acc[s, rows, :] = back * first
            row[rows, :] = back.astype(BF16)
            return c

        lax.fori_loop(0, n // ROWS, norm, 0)
        taken(s)
        put_out(s).start()
        brc = nt(row[...], cu[aid])
        brc_t = brc.T.astype(BF16)
        brc = brc.astype(BF16)
        for c in range(chunks):
            pack(0, s, 512 * c, nn(brc_t, hidden[s, :, 512 * c:512 * c + 512]))
        scatter(0, s)
        pack(1, s, 2560, term(rank_sum(s, 1, RANK), row[:, half]))
        re_t = rank_e[s]

        def contract_back(c):
            at = slice(512 * c, 512 * c + 512)
            return nt(row[...], wc[at, :]) + nn(brc, cd[aid, :, at])

        bh = contract_back(0)
        for c in range(chunks):
            after = contract_back(c + 1) if c + 1 < chunks else None
            at = slice(512 * c, 512 * c + 512)
            bb = (bh * slope[s, :, at].astype(F32)).astype(BF16)
            slope[s, :, at] = bb
            pack(1, s, 512 * c, nn(re_t, bb))
            bh = after
            if c == 0:
                hosted(s, 1, lambda: early(0))
        br = nt(slope[s], twice(eu[aid]))
        mine_rk[s, 2 * RANK:3 * RANK, :] = br.T[0:RANK, :]
        rk_copy(s, 2).start()
        br = wide(br, RANK)
        ed2 = twice(ed[aid])
        for c in range(2):
            at = slice(512 * c, 512 * c + 512)
            acc[s, :, at] += nt(slope[s], we[at, :]) + nn(br, ed2[:, at])
        send(s)
        return carry

    def wait_picks(k, c):
        pick_copy(k).wait()
        return c

    lax.fori_loop(1, GROUP, wait_picks, 0)

    load_cot.wait()
    lax.fori_loop(0, 2, stage3, 0)

    early(1)

    plan = {
        (0, 0): lambda: gather_begin(0), (0, 2): lambda: gather_begin(1), (0, 3): lambda: gather_middle(0),
        (1, 0): lambda: gather_middle(1), (1, 1): lambda: gather_late(0),
        (1, 2): lambda: gather_begin(2), (1, 3): lambda: gather_late(1),
    }

    def between(s, hp):
        for (s_, hp_), f in plan.items():
            hosted(4 * s + hp, 4 * s_ + hp_, f)


    def stage4(s, carry):
        aid = ids[s]
        exchange(s).wait()

        def norm(i, c):
            rows = pl.ds(pl.multiple_of(i * ROWS, ROWS), ROWS)
            u = (acc[s, rows, :] + recv[s, rows, :]) * g1[...]
            h = xhat[s, rows, :]
            back = rstd[s, rows, 0:1] * (
                u - jnp.mean(u, axis=1, keepdims=True) - h * jnp.mean(u * h, axis=1, keepdims=True)
            )
            acc[s, rows, :] = back * first
            row[rows, :] = back.astype(BF16)
            return c

        lax.fori_loop(0, n // ROWS, norm, 0)
        taken(s)
        hs = heads[s]
        bro = nt(row[...], ou[aid])
        pack(2, s, 0, nn(bro.T.astype(BF16), hs))
        pack(2, s, 512, term(rank_sum(s, 0, RANK), row[:, half]))
        scatter(2, s)
        hidden[s, :, 3 * hw:] = (nt(row[...], wo[...]) + nn(bro.astype(BF16), od[aid])).astype(BF16)
        pick = (
            lax.broadcasted_iota(jnp.int32, (RANK, hw), 1) // HEAD_WIDTH
            == lax.broadcasted_iota(jnp.int32, (RANK, hw), 0)
        ).astype(BF16)
        hi, lo = split(hidden[s, :, 3 * hw:].astype(F32) * hs.astype(F32))
        drow[...] = nt(pick, hi) + nt(pick, lo)

        def pair(hp, c):
            at = pl.ds(pl.multiple_of(hp * 128, 128), 128)
            q2 = qkv[s, 0, :, at]
            k2 = qkv[s, 1, :, at]
            v2 = qkv[s, 2, :, at]
            do2 = hidden[s, :, pl.ds(pl.multiple_of(3 * hw + hp * 128, 128), 128)]
            k2t = k2.T
            zero = jnp.zeros_like(k2)
            dk, dv = [], []
            for j in range(2):
                mine = low_half if j == 0 else jnp.logical_not(low_half)
                h = 2 * hp + j
                st = nt(jnp.where(mine, k2, zero), q2) + bias[s]
                pt = jnp.exp(st - lse[s, pl.ds(h, 1), :])
                dpt = nt(jnp.where(mine, v2, zero), do2)
                dst = (pt * (dpt - drow[pl.ds(h, 1), :])).astype(BF16)
                dv.append(nn(pt.astype(BF16), do2))
                dk.append(nn(dst, q2))
                dqt = nn(k2t[j * HEAD_WIDTH:(j + 1) * HEAD_WIDTH, :], dst) * 0.125
                slope[s, pl.ds(pl.multiple_of(h * HEAD_WIDTH, HEAD_WIDTH), HEAD_WIDTH), 0:n] = dqt.astype(BF16)
            to = pl.multiple_of(hp * 128, 128)
            hidden[s, :, pl.ds(hw + to, 128)] = jnp.where(low_half, dk[0], dk[1]).astype(BF16)
            hidden[s, :, pl.ds(2 * hw + to, 128)] = jnp.where(low_half, dv[0], dv[1]).astype(BF16)
            between(s, hp)
            return c

        lax.fori_loop(0, pairs, pair, 0)
        hidden[s, :, 0:hw] = slope[s, 0:hw, 0:n].T
        stack_tables(aid)
        br = nt(hidden[s, :, 0:3 * hw], u_cat[...])
        mine_rk[s, 3 * RANK:6 * RANK, :] = br.T[0:3 * RANK, :]
        rk_copy(s, 3).start()
        back_rank[s] = wide(br, 64)
        for p in range(3):
            pack(
                3, s, 512 * p, nn(rank_t[s, RANK * p:RANK * p + RANK, :], hidden[s, :, hw * p:hw * p + hw])
            )
        t_d = term(rank_sum(s, 3, 3 * RANK), x[s, :, half])
        for p in range(3):
            pack(3, s, 1536 + 512 * p, t_d[RANK * p:RANK * p + RANK, :])
        scatter(3, s)
        return carry

    lax.fori_loop(0, 2, stage4, 0)

    def project_back(s, carry):
        stack_tables(ids[s])
        for c in range(2):
            at = slice(512 * c, 512 * c + 512)
            acc[s, :, at] += nt(hidden[s, :, 0:3 * hw], wp[at, :]) + nn(back_rank[s], d_cat[:, at])
        send(s)
        return carry

    lax.fori_loop(0, 2, project_back, 0)
    gather_middle(2)

    def stage5(s):
        exchange(s).wait()
        put_out(s).wait()

        def add(i, c):
            rows = pl.ds(pl.multiple_of(i * ROWS, ROWS), ROWS)
            stage_out[s, rows, :] = (acc[s, rows, :] + recv[s, rows, :]).astype(BF16)
            return c

        lax.fori_loop(0, n // ROWS, add, 0)
        put_grad(s).start()

    gather_begin(3)
    gather_late(2)
    stage5(0)
    gather_step(3, 1)
    stage5(1)
    for g in (0, 1, 2):
        gather_close(g)
    gather_step(3, 2)
    gather_swap(3, 0)
    gather_step(3, 3)
    gather_swap(3, 1)
    gather_step(3, 4)
    gather_swap(3, 2)
    gather_swap(3, 3)
    for g in GROUPS:
        gather_end(g)
    put_grad(0).wait()
    put_grad(1).wait()


def place_kernel(*refs):
    src, dst, src_v, dst_v = refs[:9], refs[9:23], refs[23:32], refs[32:44]
    in_sem, out_sem = refs[44:]
    core = lax.axis_index("tensor")
    loads = [pltpu.make_async_copy(a, b, in_sem.at[i]) for i, (a, b) in enumerate(zip(src, src_v))]
    for cp in loads:
        cp.start()
    ends = []

    def store(v, i):
        cp = pltpu.make_async_copy(v, dst[i], out_sem.at[i])
        cp.start()
        ends.append(cp)

    qd, qu, kd, ku, vd, vu, od, ou, ed, eu, cd, cu = range(12)
    swapped = (None,) + tuple(src_v[4:7])

    def lanes(side, b):
        return pl.ds(pl.multiple_of(side * 512 + 128 * b, 128), 128)

    def fill(g, col, table, count, split_table):
        for b in range(count):
            cut, ln = divmod(col + 128 * b, LANES[g])
            for h in range(2):
                rows = slice(8 * h, 8 * h + 8)
                n, ls = 2 * cut + h, slice(ln, ln + 128)
                v = src_v[g][n, :, :, ls]
                if split_table:
                    dst_v[table][:, rows, lanes(core, b)] = v
                    dst_v[table][:, rows, lanes(1 - core, b)] = swapped[g][n - 8, :, :, ls]
                else:
                    dst_v[table][:, rows, 128 * b:128 * b + 128] = v
        store(dst_v[table], 2 + table)

    loads[0].wait()
    fill(0, 0, cd, 16, False)
    for i in (1, 4):
        loads[i].wait()
    fill(1, 0, eu, 16, False)
    fill(1, 2048, ed, 4, True)
    fill(1, 2560, cu, 4, True)
    for i in (2, 5):
        loads[i].wait()
    fill(2, 0, od, 4, False)
    fill(2, 512, ou, 4, True)
    for i in (3, 6):
        loads[i].wait()
    for p, (up, down) in enumerate(((qu, qd), (ku, kd), (vu, vd))):
        fill(3, 512 * p, up, 4, False)
        fill(3, 1536 + 512 * p, down, 4, True)
    for i in range(2):
        loads[7 + i].wait()
        store(src_v[7 + i], i)
    for cp in ends:
        cp.wait()


def place(out, grad, tables, hw, f):
    s, n, d = out.shape
    hbm = pl.BlockSpec(memory_space=pl.ANY)
    widths = (d, hw, d, hw, d, hw, hw, d, d, f, f, d)
    args = (*tables, out, grad)
    return pl.pallas_call(
        place_kernel,
        out_shape=[jax.ShapeDtypeStruct((s, n, d), BF16)] * 2
        + [jax.ShapeDtypeStruct((8, RANK, w), F32) for w in widths],
        in_specs=[hbm] * 9,
        out_specs=[hbm] * 14,
        scratch_shapes=[pltpu.VMEM(a.shape, a.dtype) for a in args]
        + [pltpu.VMEM((8, RANK, w), F32) for w in widths]
        + [pltpu.SemaphoreType.DMA((9,)), pltpu.SemaphoreType.DMA((14,))],
        compiler_params=pltpu.CompilerParams(vmem_limit_bytes=60 * 1024 * 1024),
    )(*args)


def layer(ids, seg, x, cot, wq, wk, wv, wo, we, wc, g1, b1, g2, b2, *tables):
    s, n, d = x.shape
    hw = wq.shape[1]
    f = we.shape[1]
    hbm = pl.BlockSpec(memory_space=pl.ANY)
    vm = pl.BlockSpec(memory_space=pltpu.VMEM)
    sm = pl.BlockSpec(memory_space=pltpu.SMEM)
    sds = jax.ShapeDtypeStruct
    return pl.pallas_call(
        layer_kernel,
        out_shape=(
            sds((s, n, d), BF16), sds((s, n, d), BF16),
            *(sds((GROUP, 8, 8, w), F32) for w in LANES),
            *(sds((GROUP // 2, 8, 8, LANES[g]), F32) for g in SWAPPED),
        ),
        in_specs=[sm, vm, hbm, hbm, hbm, hbm, hbm, hbm, hbm, hbm, vm, vm, vm, vm]
        + [hbm] * 12,
        out_specs=(hbm,) * 9,
        scratch_shapes=[
            pltpu.VMEM((s, n, d), BF16),
            pltpu.VMEM((s, n, d), BF16),
            pltpu.VMEM((d, 3 * hw), BF16),
            pltpu.VMEM((hw, d), BF16),
            pltpu.VMEM((d, f), BF16),
            pltpu.VMEM((f, d), BF16),
            pltpu.VMEM((3, 8, RANK, d), BF16),
            pltpu.VMEM((3, 8, RANK, hw), BF16),
            pltpu.VMEM((s, 3, n, hw), BF16),
            pltpu.VMEM((s, n, hw), BF16),
            pltpu.VMEM((s, n, n), F32),
            pltpu.VMEM((s, RANK, n), F32),
            pltpu.VMEM((s, n, d), F32),
            pltpu.VMEM((s, n, 128), F32),
            pltpu.VMEM((s, n, f), BF16),
            pltpu.VMEM((s, n, f), BF16),
            pltpu.VMEM((s, n, d), F32),
            pltpu.VMEM((s, n, d), F32),
            *(pltpu.VMEM((8, RANK, w), BF16) for w in (hw, d, d, f, f, d)),
            pltpu.VMEM((n, d), BF16),
            pltpu.VMEM((s, n, 128), BF16),
            pltpu.VMEM((128, 3 * hw), BF16),
            pltpu.VMEM((128, d), BF16),
            pltpu.VMEM((n, 128), F32),
            pltpu.VMEM((s, 3 * RANK, n), BF16),
            pltpu.VMEM((s, RANK, n), BF16),
            pltpu.VMEM((RANK, n), F32),
            pltpu.VMEM((s, 6 * RANK, n), F32),
            pltpu.VMEM((s, 6 * RANK, n), F32),
            pltpu.VMEM((s, n, d), BF16),
            pltpu.VMEM((s, 8, 128), F32),
            pltpu.VMEM((GROUP, s, 8, 128), F32),
            *(pltpu.VMEM((s, GROUP, 8, w), F32) for w in LANES),
            *(pltpu.VMEM((GROUP, s, 8, w), F32) for w in LANES),
            *(pltpu.VMEM((8, 8, w), F32) for w in LANES),
            pltpu.SemaphoreType.DMA((21,)),
            pltpu.SemaphoreType.DMA((2,)),
            pltpu.SemaphoreType.DMA((2,)),
            pltpu.SemaphoreType.DMA((2,)),
            pltpu.SemaphoreType.REGULAR((2,)),
            pltpu.SemaphoreType.DMA((2, 4)),
            pltpu.SemaphoreType.DMA((2, 4)),
            pltpu.SemaphoreType.DMA((GROUP,)),
            pltpu.SemaphoreType.DMA((GROUP,)),
            *(pltpu.SemaphoreType.DMA((len(LANES), 2, GROUP)),) * 2,
            *(pltpu.SemaphoreType.DMA((len(LANES), 4)),) * 2,
            *(pltpu.SemaphoreType.DMA((len(LANES), 4, 4)),) * 2,
            pltpu.SemaphoreType.DMA((len(LANES),)),
            *(pltpu.SemaphoreType.DMA((len(LANES), 4)),) * 2,
        ],
        compiler_params=pltpu.CompilerParams(
            collective_id=0, has_side_effects=True, vmem_limit_bytes=63 * 1024 * 1024
        ),
    )(ids, seg, x, cot, wq, wk, wv, wo, we, wc, g1, b1, g2, b2, *tables)


def on_device(
    tokens, cotangent, segment_ids, adapter_ids, query_weight, key_weight, value_weight, output_weight,
    expand_weight, contract_weight, first_gain, first_shift, second_gain, second_shift,
    query_down, query_up, key_down, key_up, value_down, value_up, output_down, output_up,
    expand_down, expand_up, contract_down, contract_up,
):
    seqs, length = segment_ids.shape
    width = tokens.shape[1]
    turn = lambda t: jnp.swapaxes(t, 1, 2)
    line = lambda v: v.reshape(1, -1)
    out, grad, *tables = layer(
        adapter_ids, segment_ids,
        tokens.reshape(seqs, length, width), cotangent.reshape(seqs, length, width),
        query_weight, key_weight, value_weight, output_weight, expand_weight, contract_weight,
        line(first_gain), line(first_shift), line(second_gain), line(second_shift),
        turn(query_down), turn(key_down), turn(value_down), query_up, key_up, value_up,
        turn(output_down), output_up, turn(expand_down), expand_up, turn(contract_down), contract_up,
    )
    out, grad, *tables = place(out, grad, tables, query_weight.shape[1], expand_weight.shape[1])
    count = lax.axis_size("dp")
    if count > GROUP:
        across = [list(range(i, count, GROUP)) for i in range(GROUP)]
        tables = lax.psum(tuple(tables), "dp", axis_index_groups=across)
    qd, qu, kd, ku, vd, vu, od, ou, ed, eu, cd, cu = tables
    return (
        out.reshape(tokens.shape), grad.reshape(tokens.shape),
        turn(qd), qu, turn(kd), ku, turn(vd), vu, turn(od), ou, turn(ed), eu, turn(cd), cu,
    )


def solution(mesh):
    cols = P(None, None, "tensor")
    mid = P(None, "tensor", None)
    return jax.shard_map(
        on_device,
        mesh=mesh,
        in_specs=(
            P("dp", None), P("dp", None), P("dp", None), P("dp"),
            P(None, "tensor"), P(None, "tensor"), P(None, "tensor"), P("tensor", None),
            P(None, "tensor"), P("tensor", None), P(), P(), P(), P(),
            P(), cols, P(), cols, P(), cols, mid, P(), P(), cols, mid, P(),
        ),
        out_specs=(
            P("dp", None), P("dp", None), P(), cols, P(), cols, P(), cols, mid, P(), P(), cols, mid, P(),
        ),
        check_vma=False,
    )
```

```python
import jax
import jax.numpy as jnp
from jax import lax
from jax.experimental import pallas as pl
from jax.experimental.pallas import tpu as pltpu
from jax.sharding import PartitionSpec as P

HEAD_WIDTH = 64
RANK = 16
MESH = pl.DeviceIdType.MESH
F32 = jnp.float32
BF16 = jnp.bfloat16
EPS = 1e-05
ROWS = 128
GROUP = 16
LANES = (256, 384, 256, 256)
GROUPS = range(len(LANES))
RK = (0, 16, 32, 48, 80, 96)
SWAPPED = (1, 2, 3)


def nn(a, b):
    return jnp.dot(a, b, preferred_element_type=F32)


def nt(a, b):
    return lax.dot_general(a, b, (((1,), (1,)), ((), ())), preferred_element_type=F32)


def split(v):
    hi = v.astype(BF16)
    return hi, (v - hi.astype(F32)).astype(BF16)


def nn_wide(v, b):
    hi, lo = split(v)
    return nn(hi, b) + nn(lo, b)


def gelu_parts(v):
    t = 1.0 / (1.0 + 0.23164188 * jnp.abs(v))
    e = jnp.exp2(v * v * -0.7213475204444817)
    tail = t * (
        0.127414796 + t * (-0.142248368 + t * (0.7107068705 + t * (-0.7265760135 + t * 0.5307027145)))
    ) * e
    cdf = jnp.where(v >= 0, 1.0 - tail, tail)
    return v * cdf, cdf + v * (e * 0.3989422804014327)


def layer_kernel(
    ids, seg, x_hbm, cot_hbm, wq, wk, wv, wo_hbm, we_hbm, wc_hbm, g1, b1, g2, b2,
    qd, kd, vd, qu, ku, vu, od_hbm, ou_hbm, ed_hbm, eu_hbm, cd_hbm, cu_hbm,
    out_hbm, grad_hbm, g0, g1_, g2_, g3, h1, h2, h3,
    x, cot, wp, wo, ff, dtab, utab, qkv, heads, bias, lse, xhat, rstd, hidden, slope, acc, recv,
    od, ou, ed, eu, cd, cu, row, back_rank, u_cat, d_cat, lcol, rank_t, rank_e, drow, mine_rk, their_rk, stage_out,
    pick_mine, picks, p0, p1, p2, p3, r0, r1, r2, r3, d0, d1, d2, d3,
    load_sem, send_sem, recv_sem, out_sem, credit, rk_send, rk_recv, pick_send, pick_recv,
    rs_send_sem, rs_recv_sem, z_send, z_recv, plane_send, plane_recv, own_sem, swap_send, swap_recv,
):
    dp = lax.axis_index("dp")
    core = lax.axis_index("tensor")
    partner = (dp, 1 - core)
    first = (core == 0).astype(F32)
    me = lax.rem(dp, GROUP)
    base = dp - me
    half = pl.ds(pl.multiple_of(core * 512, 512), 512)

    wc, we = ff.at[0], ff.at[1]
    d = x.shape[2]

    def load(i, src, dst):
        return pltpu.make_async_copy(src, dst, load_sem.at[i])

    load_x = [load(s, x_hbm.at[s], x.at[s]) for s in range(2)]
    load_d = [load(2 + i, t, dtab.at[i]) for i, t in enumerate((qd, kd, vd))]
    load_u = [load(5 + i, t, utab.at[i]) for i, t in enumerate((qu, ku, vu))]
    load_w = [load(8 + i, t, wp.at[:, pl.ds(512 * i, 512)]) for i, t in enumerate((wq, wk, wv))]
    load_o = [load(11, wo_hbm, wo), load(12, od_hbm, od), load(13, ou_hbm, ou)]
    load_f = [
        load(14, we_hbm.at[:, pl.ds(0, d)], we.at[pl.ds(0, d)]),
        load(15, we_hbm.at[:, pl.ds(d, d)], we.at[pl.ds(d, d)]),
        load(16, ed_hbm, ed), load(17, eu_hbm, eu),
        load(18, wc_hbm, wc), load(19, cd_hbm, cd), load(20, cu_hbm, cu),
    ]
    load_cot = load(21, cot_hbm, cot)
    for cp in load_x[:1] + load_d + load_w + load_u:
        cp.start()

    def peer(k):
        return (base + lax.bitwise_xor(me, k), core)

    barrier = pltpu.get_barrier_semaphore()
    pl.semaphore_signal(barrier, inc=1, device_id=partner, device_id_type=MESH)

    def greet(k, c):
        pl.semaphore_signal(barrier, inc=1, device_id=peer(k), device_id_type=MESH)
        return c

    lax.fori_loop(1, GROUP, greet, 0)

    def remote(src, dst, ss, rs, to):
        return pltpu.make_async_remote_copy(
            src_ref=src, dst_ref=dst, send_sem=ss, recv_sem=rs, device_id=to, device_id_type=MESH
        )

    def pick_copy(k):
        return remote(pick_mine, picks.at[me], pick_send.at[k], pick_recv.at[k], peer(k))

    table_id = lax.broadcasted_iota(jnp.int32, (8, 128), 0)
    for s in range(2):
        pick_mine[s] = (table_id == ids[s]).astype(F32)
    picks[me] = pick_mine[...]

    def send_pick(k, c):
        pick_copy(k).start()
        return c

    def meet():
        pl.semaphore_wait(barrier, GROUP)
        lax.fori_loop(1, GROUP, send_pick, 0)

    def rk_copy(s, i):
        rows = pl.ds(RK[i], RK[i + 1] - RK[i])
        return remote(
            mine_rk.at[s, rows], their_rk.at[s, rows], rk_send.at[s, i], rk_recv.at[s, i], partner
        )

    def rank_sum(s, i):
        rk_copy(s, i).wait()
        at = slice(RK[i], RK[i + 1])
        return mine_rk[s, at, :] + their_rk[s, at, :]

    packs, parts, denses = (p0, p1, p2, p3), (r0, r1, r2, r3), (d0, d1, d2, d3)
    gathered, swapped = (g0, g1_, g2_, g3), (None, h1, h2, h3)

    def pack(g, s, col, v):
        for b in range(v.shape[1] // 128):
            cut, ln = divmod(col + 128 * b, LANES[g])
            for h in range(2):
                packs[g][s, 2 * cut + h, :, ln:ln + 128] = v[8 * h:8 * h + 8, 128 * b:128 * b + 128]

    def shard_copy(g, s, k):
        to = lax.bitwise_xor(me, k)
        return remote(
            packs[g].at[s, to], parts[g].at[me, s], rs_send_sem.at[g, s, k], rs_recv_sem.at[g, s, k], peer(k)
        )

    def scatter(g, s):
        parts[g][me, s] = packs[g][s, me]

        def go(k, c):
            shard_copy(g, s, k).start()
            return c

        lax.fori_loop(1, GROUP, go, 0)

    def combine(g):
        def wait(k, c):
            for s in range(2):
                shard_copy(g, s, k).wait()
            return c

        lax.fori_loop(1, GROUP, wait, 0)

        cuts = range(0, LANES[g], 128)

        def add(m, total):
            for s in range(2):
                part = [parts[g][m, s, :, at:at + 128] for at in cuts]
                for a in range(8):
                    weight = jnp.broadcast_to(picks[m, s, a:a + 1, :], (8, 128))
                    total = [
                        t + weight * part[i % len(cuts)] if i // len(cuts) == a else t
                        for i, t in enumerate(total)
                    ]
            return tuple(total)

        total = lax.fori_loop(0, GROUP, add, (jnp.zeros((8, 128), F32),) * (8 * len(cuts)))
        for i, t in enumerate(total):
            a, at = divmod(i, len(cuts))
            denses[g][a, :, 128 * at:128 * at + 128] = t

    def own_copy(g):
        return pltpu.make_async_copy(denses[g], gathered[g].at[me], own_sem.at[g])

    def z_copy(g, u):
        return remote(denses[g], gathered[g].at[me], z_send.at[g, u], z_recv.at[g, u], peer(4 * u))

    def slot(u, k):
        return lax.bitwise_xor(me, 4 * u + k)

    def plane_copy(g, u, way):
        to = gathered[g].at[slot(u, 0)]
        return remote(
            denses[g] if u == 0 else to, to, plane_send.at[g, u, way], plane_recv.at[g, u, way], peer(way + 1)
        )

    def onward_copy(g, u, way):
        at = gathered[g].at[slot(u, way + 1), pl.ds(4 * way, 4)]
        return remote(at, at, plane_send.at[g, u, 2 + way], plane_recv.at[g, u, 2 + way], peer(2 - way))

    def swap_copy(g, u):
        plane = lax.bitwise_xor(me // 4, u)
        return plane >= 2, remote(
            gathered[g].at[pl.ds(4 * plane, 4)], swapped[g].at[pl.ds(4 * lax.rem(plane, 2), 4)],
            swap_send.at[g, u], swap_recv.at[g, u], partner,
        )

    def gather_first(g):
        own_copy(g).start()
        for u in (1, 2, 3):
            z_copy(g, u).start()
        for way in range(2):
            plane_copy(g, 0, way).start()

    def gather_unit(g, u):
        z_copy(g, u).wait_recv()
        for way in range(2):
            plane_copy(g, u, way).start()

    def gather_onward(g, u):
        for way in range(2):
            plane_copy(g, u, way).wait_recv()
            onward_copy(g, u, way).start()

    def gather_swap(g, u):
        if u == 0:
            own_copy(g).wait()
        for way in range(2):
            onward_copy(g, u, way).wait_recv()
        if g in SWAPPED:
            upper, copy = swap_copy(g, u)

            @pl.when(upper)
            def _():
                copy.start()

    def gather_end(g):
        for u in (1, 2, 3):
            z_copy(g, u).wait_send()
        for u in range(4):
            for way in range(2):
                plane_copy(g, u, way).wait_send()
                onward_copy(g, u, way).wait_send()
            if g in SWAPPED:
                upper, copy = swap_copy(g, u)

                @pl.when(upper)
                def _():
                    copy.wait()

    def gather_begin(g):
        combine(g)
        gather_first(g)

    def gather_step(g, u):
        if u < 4:
            gather_unit(g, u)
        gather_onward(g, u - 1)

    def gather_middle(g):
        for u in (1, 2, 3):
            gather_unit(g, u)
        gather_onward(g, 0)

    def gather_late(g):
        for u in (1, 2, 3):
            gather_onward(g, u)

    def gather_close(g):
        for u in range(4):
            gather_swap(g, u)

    def hosted(here, there, f):
        @pl.when(here == there)
        def _():
            f()

    def exchange(s):
        return pltpu.make_async_remote_copy(
            src_ref=acc.at[s], dst_ref=recv.at[s], send_sem=send_sem.at[s], recv_sem=recv_sem.at[s],
            device_id=partner, device_id_type=MESH,
        )

    def taken(s):
        pl.semaphore_signal(credit.at[s], inc=1, device_id=partner, device_id_type=MESH)

    def send(s):
        pl.semaphore_wait(credit.at[s], 1)
        exchange(s).start()

    n = x.shape[1]
    hw = heads.shape[2]
    pairs = hw // 128
    chunks = hidden.shape[2] // 512
    lane = lax.broadcasted_iota(jnp.int32, (n, 128), 1)
    low_half = lane < HEAD_WIDTH

    u_cat[...] = jnp.zeros_like(u_cat)
    d_cat[...] = jnp.zeros_like(d_cat)

    def stack_tables(aid):
        for p in range(3):
            for r in (0, 64):
                rows = slice(r + RANK * p, r + RANK * p + RANK)
                d_cat[rows, :] = dtab[p, aid]
                u_cat[rows, hw * p:hw * p + hw] = utab[p, aid]

    def twice(t):
        return jnp.concatenate([t, t], axis=0)

    def wide(v, at):
        hi = v.astype(BF16).astype(F32)
        return jnp.where(lax.broadcasted_iota(jnp.int32, v.shape, 1) < at, hi, v - hi).astype(BF16)

    def term(v, right):
        k = v.shape[0]
        hi, lo = split(v)
        both_parts = nn(jnp.concatenate([hi, lo], axis=0), right)
        return both_parts[:k] + both_parts[k:]

    def stage1(s, carry):
        aid = ids[s]
        seg_row = seg[pl.ds(s, 1), :].astype(F32)
        seg_col = jnp.broadcast_to(seg_row, (128, n)).T
        for j in range(n // 128):
            same = seg_col == seg_row[:, j * 128:(j + 1) * 128]
            bias[s, :, j * 128:(j + 1) * 128] = jnp.where(same, 0.0, -1e30)

        @pl.when(s == 0)
        def _():
            for cp in load_x[:1] + load_d + load_u:
                cp.wait()
            for cp in load_x[1:] + load_o:
                cp.start()

        @pl.when(s == 1)
        def _():
            load_x[1].wait()

        stack_tables(aid)
        rank = jnp.where(lane < 64, nt(x[s], d_cat[...]), 0.0)
        rank_t[s] = rank.T[0:3 * RANK, :].astype(BF16)
        rank = rank.astype(BF16)

        @pl.when(s == 0)
        def _():
            for cp in load_f + [load_cot]:
                cp.start()

        def project(p, c):
            at = pl.ds(pl.multiple_of(p * hw, hw), hw)
            for i in range(3):
                hosted(3 * s + p, i, lambda: load_w[i].wait())
            scale = jnp.where(p == 0, 0.125, 1.0)
            qkv[s, p] = ((nn(x[s], wp[:, at]) + nn(rank, u_cat[:, at])) * scale).astype(BF16)
            return c

        lax.fori_loop(0, 3, project, 0)

        def pair(hp, c):
            at = pl.ds(pl.multiple_of(hp * 128, 128), 128)
            k2 = qkv[s, 1, :, at]
            v2 = jnp.concatenate([qkv[s, 2, :, at], jnp.ones((n, 128), BF16)], axis=1)
            for r in range(2):
                rows = slice(r * (n // 2), (r + 1) * (n // 2))
                q2 = qkv[s, 0, rows, at]
                outs = []
                ln = lane[rows]
                for j in range(2):
                    mine = (ln < HEAD_WIDTH) if j == 0 else (ln >= HEAD_WIDTH)
                    score = nt(jnp.where(mine, q2, jnp.zeros_like(q2)), k2) + bias[s, rows, :]
                    top = jnp.max(score, axis=1, keepdims=True)
                    e = jnp.exp(score - top).astype(BF16)
                    parts_ = nn(e, v2)
                    total = parts_[:, 128:]
                    outs.append(parts_[:, :128] / total)
                    old = lcol[rows, :]
                    lcol[rows, :] = jnp.where(ln == 2 * hp + j, top + jnp.log(total), old)
                heads[s, rows, at] = jnp.where(ln < HEAD_WIDTH, outs[0], outs[1]).astype(BF16)
            return c

        lax.fori_loop(0, pairs, pair, 0)
        lse[s] = lcol[...].T[:lse.shape[1], :]

        @pl.when(s == 0)
        def _():
            for cp in load_o:
                cp.wait()
            meet()

        hs = heads[s]
        ro = nt(hs, twice(od[aid]))
        mine_rk[s, 0:RANK, :] = ro.T[0:RANK, :]
        rk_copy(s, 0).start()
        acc[s] = nn(hs, wo[...]) + nn(wide(ro, RANK), twice(ou[aid]))
        exchange(s).start()
        return carry

    lax.fori_loop(0, 2, stage1, 0)

    def stage2(s, carry):
        aid = ids[s]
        exchange(s).wait()

        def norm(i, c):
            rows = pl.ds(pl.multiple_of(i * ROWS, ROWS), ROWS)
            h = x[s, rows, :].astype(F32) + (acc[s, rows, :] + recv[s, rows, :])
            mean = jnp.mean(h, axis=1, keepdims=True)
            h = h - mean
            inv = lax.rsqrt(jnp.mean(h * h, axis=1, keepdims=True) + EPS)
            h = h * inv
            xhat[s, rows, :] = h
            rstd[s, rows, :] = jnp.broadcast_to(inv, (ROWS, 128))
            row[rows, :] = (h * g1[...] + b1[...]).astype(BF16)
            return c

        lax.fori_loop(0, n // ROWS, norm, 0)
        taken(s)
        rank = nt(row[...], ed[aid])
        rank_e[s] = rank.T.astype(BF16)
        rank = rank.astype(BF16)

        def expand(c):
            at = slice(512 * c, 512 * c + 512)
            top, left = divmod(512 * c, d)
            return nn(row[...], we[d * top:d * top + d, left:left + 512]) + nn(rank, eu[aid, :, at])

        before = expand(0)
        for c in range(chunks):
            after = expand(c + 1) if c + 1 < chunks else None
            at = slice(512 * c, 512 * c + 512)
            hid, sl = gelu_parts(before)
            hidden[s, :, at] = hid.astype(BF16)
            slope[s, :, at] = sl.astype(BF16)
            before = after
        rc = nt(hidden[s], twice(cd[aid]))
        mine_rk[s, RANK:2 * RANK, :] = rc.T[0:RANK, :]
        rk_copy(s, 1).start()
        rc = wide(rc, RANK)
        cu2 = twice(cu[aid])
        for c in range(2):
            at = slice(512 * c, 512 * c + 512)
            acc[s, :, at] = nn(hidden[s], wc[:, at]) + nn(rc, cu2[:, at])
        send(s)
        return carry

    for cp in load_f:
        cp.wait()
    lax.fori_loop(0, 2, stage2, 0)

    def put_out(s):
        return pltpu.make_async_copy(stage_out.at[s], out_hbm.at[s], out_sem.at[s])

    def put_grad(s):
        return pltpu.make_async_copy(stage_out.at[s], grad_hbm.at[s], out_sem.at[s])

    def early(s):
        inner = (xhat[s, :, half] * g1[:, half] + b1[:, half]).astype(BF16)
        pack(1, s, 2048, term(rank_sum(s, 2), inner))
        scatter(1, s)

    def stage3(s, carry):
        aid = ids[s]
        exchange(s).wait()

        def norm(i, c):
            rows = pl.ds(pl.multiple_of(i * ROWS, ROWS), ROWS)
            normed = xhat[s, rows, :] * g1[...] + b1[...]
            h = normed + (acc[s, rows, :] + recv[s, rows, :])
            mean = jnp.mean(h, axis=1, keepdims=True)
            h = h - mean
            inv = lax.rsqrt(jnp.mean(h * h, axis=1, keepdims=True) + EPS)
            h = h * inv
            stage_out[s, rows, :] = (h * g2[...] + b2[...]).astype(BF16)
            u = cot[s, rows, :].astype(F32) * g2[...]
            back = inv * (
                u - jnp.mean(u, axis=1, keepdims=True) - h * jnp.mean(u * h, axis=1, keepdims=True)
            )
            acc[s, rows, :] = back * first
            row[rows, :] = back.astype(BF16)
            return c

        lax.fori_loop(0, n // ROWS, norm, 0)
        taken(s)
        put_out(s).start()
        brc = nt(row[...], cu[aid])
        brc_t = brc.T.astype(BF16)
        brc = brc.astype(BF16)
        for c in range(chunks):
            pack(0, s, 512 * c, nn(brc_t, hidden[s, :, 512 * c:512 * c + 512]))
        scatter(0, s)
        pack(1, s, 2560, term(rank_sum(s, 1), row[:, half]))
        re_t = rank_e[s]

        def contract_back(c):
            at = slice(512 * c, 512 * c + 512)
            return nt(row[...], wc[at, :]) + nn(brc, cd[aid, :, at])

        bh = contract_back(0)
        for c in range(chunks):
            after = contract_back(c + 1) if c + 1 < chunks else None
            at = slice(512 * c, 512 * c + 512)
            bb = (bh * slope[s, :, at].astype(F32)).astype(BF16)
            slope[s, :, at] = bb
            pack(1, s, 512 * c, nn(re_t, bb))
            bh = after
            if c == 0:
                hosted(s, 1, lambda: early(0))
        br = nt(slope[s], twice(eu[aid]))
        mine_rk[s, 2 * RANK:3 * RANK, :] = br.T[0:RANK, :]
        rk_copy(s, 2).start()
        br = wide(br, RANK)
        ed2 = twice(ed[aid])
        for c in range(2):
            at = slice(512 * c, 512 * c + 512)
            low = slice(d + 512 * c, d + 512 * c + 512)
            acc[s, :, at] += (
                nt(slope[s, :, 0:d], we[at, :]) + nt(slope[s, :, d:], we[low, :]) + nn(br, ed2[:, at])
            )
        send(s)
        return carry

    def wait_picks(k, c):
        pick_copy(k).wait()
        return c

    lax.fori_loop(1, GROUP, wait_picks, 0)

    load_cot.wait()
    lax.fori_loop(0, 2, stage3, 0)

    early(1)

    def finish(g, s):
        if g == 2:
            pack(2, s, 1536, term(rank_sum(s, 4), x[s, :, half]))
        else:
            t_d = term(rank_sum(s, 3), x[s, :, half])
            pack(3, s, 1024, t_d[0:RANK, :])
            pack(3, s, 1536, t_d[RANK:2 * RANK, :])
        scatter(g, s)

    def stage4(s, carry):
        aid = ids[s]
        exchange(s).wait()

        def norm(i, c):
            rows = pl.ds(pl.multiple_of(i * ROWS, ROWS), ROWS)
            u = (acc[s, rows, :] + recv[s, rows, :]) * g1[...]
            h = xhat[s, rows, :]
            back = rstd[s, rows, 0:1] * (
                u - jnp.mean(u, axis=1, keepdims=True) - h * jnp.mean(u * h, axis=1, keepdims=True)
            )
            acc[s, rows, :] = back * first
            row[rows, :] = back.astype(BF16)
            return c

        lax.fori_loop(0, n // ROWS, norm, 0)
        taken(s)
        hs = heads[s]
        bro = nt(row[...], ou[aid])
        pack(2, s, 0, nn(bro.T.astype(BF16), hs))
        pack(2, s, 1024, term(rank_sum(s, 0), row[:, half]))
        hosted(s, 0, lambda: gather_begin(0))
        hosted(s, 1, lambda: finish(2, 0))
        hosted(s, 1, lambda: gather_middle(0))
        hidden[s, :, 3 * hw:] = (nt(row[...], wo[...]) + nn(bro.astype(BF16), od[aid])).astype(BF16)
        pick = (
            lax.broadcasted_iota(jnp.int32, (RANK, hw), 1) // HEAD_WIDTH
            == lax.broadcasted_iota(jnp.int32, (RANK, hw), 0)
        ).astype(BF16)
        hi, lo = split(hidden[s, :, 3 * hw:].astype(F32) * hs.astype(F32))
        drow[s] = nt(pick, hi) + nt(pick, lo)

        def pair(hp, c):
            at = pl.ds(pl.multiple_of(hp * 128, 128), 128)
            q2 = qkv[s, 0, :, at]
            k2 = qkv[s, 1, :, at]
            do2 = hidden[s, :, pl.ds(pl.multiple_of(3 * hw + hp * 128, 128), 128)]
            dv = []
            for j in range(2):
                mine = low_half if j == 0 else jnp.logical_not(low_half)
                st = nt(jnp.where(mine, k2, jnp.zeros_like(k2)), q2) + bias[s]
                pt = jnp.exp(st - lse[s, pl.ds(2 * hp + j, 1), :]).astype(BF16)
                ff[s, pl.ds(pl.multiple_of(hp * n, n), n), j * n:j * n + n] = pt
                dv.append(nn(pt, do2))
            to = pl.ds(pl.multiple_of(2 * hw + hp * 128, 128), 128)
            hidden[s, :, to] = jnp.where(low_half, dv[0], dv[1]).astype(BF16)
            return c

        lax.fori_loop(0, pairs, pair, 0)
        stack_tables(aid)
        d_v = hidden[s, :, 2 * hw:3 * hw]
        br = nt(d_v, u_cat[:, 2 * hw:3 * hw])
        mine_rk[s, RK[4]:RK[5], :] = br.T[2 * RANK:3 * RANK, :]
        rk_copy(s, 4).start()
        back_rank[s] = wide(br, 64)
        pack(2, s, 512, nn(rank_t[s, 2 * RANK:3 * RANK, :], d_v))
        hosted(s, 0, lambda: gather_begin(1))
        hosted(s, 1, lambda: gather_late(0))
        return carry

    lax.fori_loop(0, 2, stage4, 0)

    def stage4b(s, carry):
        aid = ids[s]

        def pair(hp, c):
            at = pl.ds(pl.multiple_of(hp * 128, 128), 128)
            q2 = qkv[s, 0, :, at]
            k2 = qkv[s, 1, :, at]
            v2 = qkv[s, 2, :, at]
            do2 = hidden[s, :, pl.ds(pl.multiple_of(3 * hw + hp * 128, 128), 128)]
            k2t = k2.T
            dk = []
            for j in range(2):
                mine = low_half if j == 0 else jnp.logical_not(low_half)
                h = 2 * hp + j
                pt = ff[s, pl.ds(pl.multiple_of(hp * n, n), n), j * n:j * n + n].astype(F32)
                dpt = nt(jnp.where(mine, v2, jnp.zeros_like(v2)), do2)
                dst = (pt * (dpt - drow[s, pl.ds(h, 1), :])).astype(BF16)
                dk.append(nn(dst, q2))
                dqt = nn(k2t[j * HEAD_WIDTH:(j + 1) * HEAD_WIDTH, :], dst) * 0.125
                slope[s, pl.ds(pl.multiple_of(h * HEAD_WIDTH, HEAD_WIDTH), HEAD_WIDTH), 0:n] = dqt.astype(BF16)
            to = pl.ds(pl.multiple_of(hw + hp * 128, 128), 128)
            hidden[s, :, to] = jnp.where(low_half, dk[0], dk[1]).astype(BF16)
            for (s_, hp_), f in plan.items():
                hosted(4 * s + hp, 4 * s_ + hp_, f)
            return c

        lax.fori_loop(0, pairs, pair, 0)
        hidden[s, :, 0:hw] = slope[s, 0:hw, 0:n].T
        stack_tables(aid)
        br = nt(hidden[s, :, 0:2 * hw], u_cat[:, 0:2 * hw])
        mine_rk[s, RK[3]:RK[4], :] = br.T[0:2 * RANK, :]
        rk_copy(s, 3).start()
        back_rank[s] += wide(br, 64)
        for p in range(2):
            pack(
                3, s, 512 * p, nn(rank_t[s, RANK * p:RANK * p + RANK, :], hidden[s, :, hw * p:hw * p + hw])
            )
        hosted(s, 0, lambda: gather_begin(2))
        return carry

    plan = {(0, 0): lambda: finish(2, 1), (0, 1): lambda: gather_middle(1), (1, 0): lambda: finish(3, 0), (1, 2): lambda: gather_late(1)}
    lax.fori_loop(0, 2, stage4b, 0)

    def project_back(s, carry):
        stack_tables(ids[s])
        for c in range(2):
            at = slice(512 * c, 512 * c + 512)
            acc[s, :, at] += nt(hidden[s, :, 0:3 * hw], wp[at, :]) + nn(back_rank[s], d_cat[:, at])
        send(s)
        return carry

    def back_step(s, carry):
        project_back(s, carry)
        hosted(s, 0, lambda: finish(3, 1))
        hosted(s, 0, lambda: gather_middle(2))
        return carry

    lax.fori_loop(0, 2, back_step, 0)

    def stage5(s):
        exchange(s).wait()
        put_out(s).wait()

        def add(i, c):
            rows = pl.ds(pl.multiple_of(i * ROWS, ROWS), ROWS)
            stage_out[s, rows, :] = (acc[s, rows, :] + recv[s, rows, :]).astype(BF16)
            return c

        lax.fori_loop(0, n // ROWS, add, 0)
        put_grad(s).start()

    gather_begin(3)
    gather_late(2)
    stage5(0)
    gather_onward(3, 0)
    gather_unit(3, 1)
    stage5(1)
    for g in (0, 1, 2):
        gather_close(g)
    gather_step(3, 2)
    gather_swap(3, 0)
    gather_step(3, 3)
    gather_swap(3, 1)
    gather_step(3, 4)
    gather_swap(3, 2)
    gather_swap(3, 3)
    for g in GROUPS:
        gather_end(g)
    put_grad(0).wait()
    put_grad(1).wait()


def place_kernel(*refs):
    src, dst, src_v, dst_v = refs[:9], refs[9:23], refs[23:32], refs[32:44]
    in_sem, out_sem = refs[44:]
    core = lax.axis_index("tensor")
    loads = [pltpu.make_async_copy(a, b, in_sem.at[i]) for i, (a, b) in enumerate(zip(src, src_v))]
    for cp in loads:
        cp.start()
    ends = []

    def store(v, i):
        cp = pltpu.make_async_copy(v, dst[i], out_sem.at[i])
        cp.start()
        ends.append(cp)

    qd, qu, kd, ku, vd, vu, od, ou, ed, eu, cd, cu = range(12)
    swapped = (None,) + tuple(src_v[4:7])

    def lanes(side, b):
        return pl.ds(pl.multiple_of(side * 512 + 128 * b, 128), 128)

    def fill(g, col, table, count, split_table):
        for b in range(count):
            cut, ln = divmod(col + 128 * b, LANES[g])
            for h in range(2):
                rows = slice(8 * h, 8 * h + 8)
                n, ls = 2 * cut + h, slice(ln, ln + 128)
                v = src_v[g][n, :, :, ls]
                if split_table:
                    dst_v[table][:, rows, lanes(core, b)] = v
                    dst_v[table][:, rows, lanes(1 - core, b)] = swapped[g][n - 8, :, :, ls]
                else:
                    dst_v[table][:, rows, 128 * b:128 * b + 128] = v
        store(dst_v[table], 2 + table)

    loads[0].wait()
    fill(0, 0, cd, 16, False)
    for i in (1, 4):
        loads[i].wait()
    fill(1, 0, eu, 16, False)
    fill(1, 2048, ed, 4, True)
    fill(1, 2560, cu, 4, True)
    for i in (2, 5):
        loads[i].wait()
    fill(2, 0, od, 4, False)
    fill(2, 512, vu, 4, False)
    fill(2, 1024, ou, 4, True)
    fill(2, 1536, vd, 4, True)
    for i in (3, 6):
        loads[i].wait()
    fill(3, 0, qu, 4, False)
    fill(3, 512, ku, 4, False)
    fill(3, 1024, qd, 4, True)
    fill(3, 1536, kd, 4, True)
    for i in range(2):
        loads[7 + i].wait()
        store(src_v[7 + i], i)
    for cp in ends:
        cp.wait()


def place(out, grad, tables, hw, f):
    s, n, d = out.shape
    hbm = pl.BlockSpec(memory_space=pl.ANY)
    widths = (d, hw, d, hw, d, hw, hw, d, d, f, f, d)
    args = (*tables, out, grad)
    return pl.pallas_call(
        place_kernel,
        out_shape=[jax.ShapeDtypeStruct((s, n, d), BF16)] * 2
        + [jax.ShapeDtypeStruct((8, RANK, w), F32) for w in widths],
        in_specs=[hbm] * 9,
        out_specs=[hbm] * 14,
        scratch_shapes=[pltpu.VMEM(a.shape, a.dtype) for a in args]
        + [pltpu.VMEM((8, RANK, w), F32) for w in widths]
        + [pltpu.SemaphoreType.DMA((9,)), pltpu.SemaphoreType.DMA((14,))],
        compiler_params=pltpu.CompilerParams(vmem_limit_bytes=60 * 1024 * 1024),
    )(*args)


def layer(ids, seg, x, cot, wq, wk, wv, wo, we, wc, g1, b1, g2, b2, *tables):
    s, n, d = x.shape
    hw = wq.shape[1]
    f = we.shape[1]
    hbm = pl.BlockSpec(memory_space=pl.ANY)
    vm = pl.BlockSpec(memory_space=pltpu.VMEM)
    sm = pl.BlockSpec(memory_space=pltpu.SMEM)
    sds = jax.ShapeDtypeStruct
    return pl.pallas_call(
        layer_kernel,
        out_shape=(
            sds((s, n, d), BF16), sds((s, n, d), BF16),
            *(sds((GROUP, 8, 8, w), F32) for w in LANES),
            *(sds((GROUP // 2, 8, 8, LANES[g]), F32) for g in SWAPPED),
        ),
        in_specs=[sm, vm, hbm, hbm, hbm, hbm, hbm, hbm, hbm, hbm, vm, vm, vm, vm]
        + [hbm] * 12,
        out_specs=(hbm,) * 9,
        scratch_shapes=[
            pltpu.VMEM((s, n, d), BF16),
            pltpu.VMEM((s, n, d), BF16),
            pltpu.VMEM((d, 3 * hw), BF16),
            pltpu.VMEM((hw, d), BF16),
            pltpu.VMEM((2, f, d), BF16),
            pltpu.VMEM((3, 8, RANK, d), BF16),
            pltpu.VMEM((3, 8, RANK, hw), BF16),
            pltpu.VMEM((s, 3, n, hw), BF16),
            pltpu.VMEM((s, n, hw), BF16),
            pltpu.VMEM((s, n, n), F32),
            pltpu.VMEM((s, RANK, n), F32),
            pltpu.VMEM((s, n, d), F32),
            pltpu.VMEM((s, n, 128), F32),
            pltpu.VMEM((s, n, f), BF16),
            pltpu.VMEM((s, n, f), BF16),
            pltpu.VMEM((s, n, d), F32),
            pltpu.VMEM((s, n, d), F32),
            *(pltpu.VMEM((8, RANK, w), BF16) for w in (hw, d, d, f, f, d)),
            pltpu.VMEM((n, d), BF16),
            pltpu.VMEM((s, n, 128), BF16),
            pltpu.VMEM((128, 3 * hw), BF16),
            pltpu.VMEM((128, d), BF16),
            pltpu.VMEM((n, 128), F32),
            pltpu.VMEM((s, 3 * RANK, n), BF16),
            pltpu.VMEM((s, RANK, n), BF16),
            pltpu.VMEM((s, RANK, n), F32),
            pltpu.VMEM((s, 6 * RANK, n), F32),
            pltpu.VMEM((s, 6 * RANK, n), F32),
            pltpu.VMEM((s, n, d), BF16),
            pltpu.VMEM((s, 8, 128), F32),
            pltpu.VMEM((GROUP, s, 8, 128), F32),
            *(pltpu.VMEM((s, GROUP, 8, w), F32) for w in LANES),
            *(pltpu.VMEM((GROUP, s, 8, w), F32) for w in LANES),
            *(pltpu.VMEM((8, 8, w), F32) for w in LANES),
            pltpu.SemaphoreType.DMA((22,)),
            pltpu.SemaphoreType.DMA((2,)),
            pltpu.SemaphoreType.DMA((2,)),
            pltpu.SemaphoreType.DMA((2,)),
            pltpu.SemaphoreType.REGULAR((2,)),
            *(pltpu.SemaphoreType.DMA((2, 5)),) * 2,
            pltpu.SemaphoreType.DMA((GROUP,)),
            pltpu.SemaphoreType.DMA((GROUP,)),
            *(pltpu.SemaphoreType.DMA((len(LANES), 2, GROUP)),) * 2,
            *(pltpu.SemaphoreType.DMA((len(LANES), 4)),) * 2,
            *(pltpu.SemaphoreType.DMA((len(LANES), 4, 4)),) * 2,
            pltpu.SemaphoreType.DMA((len(LANES),)),
            *(pltpu.SemaphoreType.DMA((len(LANES), 4)),) * 2,
        ],
        compiler_params=pltpu.CompilerParams(
            collective_id=0, has_side_effects=True, vmem_limit_bytes=63 * 1024 * 1024
        ),
    )(ids, seg, x, cot, wq, wk, wv, wo, we, wc, g1, b1, g2, b2, *tables)


def on_device(
    tokens, cotangent, segment_ids, adapter_ids, query_weight, key_weight, value_weight, output_weight,
    expand_weight, contract_weight, first_gain, first_shift, second_gain, second_shift,
    query_down, query_up, key_down, key_up, value_down, value_up, output_down, output_up,
    expand_down, expand_up, contract_down, contract_up,
):
    seqs, length = segment_ids.shape
    width = tokens.shape[1]
    turn = lambda t: jnp.swapaxes(t, 1, 2)
    line = lambda v: v.reshape(1, -1)
    out, grad, *tables = layer(
        adapter_ids, segment_ids,
        tokens.reshape(seqs, length, width), cotangent.reshape(seqs, length, width),
        query_weight, key_weight, value_weight, output_weight, expand_weight, contract_weight,
        line(first_gain), line(first_shift), line(second_gain), line(second_shift),
        turn(query_down), turn(key_down), turn(value_down), query_up, key_up, value_up,
        turn(output_down), output_up, turn(expand_down), expand_up, turn(contract_down), contract_up,
    )
    out, grad, *tables = place(out, grad, tables, query_weight.shape[1], expand_weight.shape[1])
    count = lax.axis_size("dp")
    if count > GROUP:
        across = [list(range(i, count, GROUP)) for i in range(GROUP)]
        tables = lax.psum(tuple(tables), "dp", axis_index_groups=across)
    qd, qu, kd, ku, vd, vu, od, ou, ed, eu, cd, cu = tables
    return (
        out.reshape(tokens.shape), grad.reshape(tokens.shape),
        turn(qd), qu, turn(kd), ku, turn(vd), vu, turn(od), ou, turn(ed), eu, turn(cd), cu,
    )


def solution(mesh):
    cols = P(None, None, "tensor")
    mid = P(None, "tensor", None)
    return jax.shard_map(
        on_device,
        mesh=mesh,
        in_specs=(
            P("dp", None), P("dp", None), P("dp", None), P("dp"),
            P(None, "tensor"), P(None, "tensor"), P(None, "tensor"), P("tensor", None),
            P(None, "tensor"), P("tensor", None), P(), P(), P(), P(),
            P(), cols, P(), cols, P(), cols, mid, P(), P(), cols, mid, P(),
        ),
        out_specs=(
            P("dp", None), P("dp", None), P(), cols, P(), cols, P(), cols, mid, P(), P(), cols, mid, P(),
        ),
        check_vma=False,
    )
```

```python
import jax
import jax.numpy as jnp
from jax import lax
from jax.experimental import pallas as pl
from jax.experimental.pallas import tpu as pltpu
from jax.sharding import PartitionSpec as P

HEAD_WIDTH = 64
RANK = 16
MESH = pl.DeviceIdType.MESH
F32 = jnp.float32
BF16 = jnp.bfloat16
EPS = 1e-05
ROWS = 256
GROUP = 16
LANES = (256, 384, 256, 256)
GROUPS = range(len(LANES))
RK = (0, 16, 32, 48, 80, 96)
SWAPPED = (1, 2, 3)


def nn(a, b):
    return jnp.dot(a, b, preferred_element_type=F32)


def nt(a, b):
    return lax.dot_general(a, b, (((1,), (1,)), ((), ())), preferred_element_type=F32)


def split(v):
    hi = v.astype(BF16)
    return hi, (v - hi.astype(F32)).astype(BF16)


def nn_wide(v, b):
    hi, lo = split(v)
    return nn(hi, b) + nn(lo, b)


def gelu_parts(v):
    t = 1.0 / (1.0 + 0.23164188 * jnp.abs(v))
    e = jnp.exp2(v * v * -0.7213475204444817)
    tail = t * (
        0.127414796 + t * (-0.142248368 + t * (0.7107068705 + t * (-0.7265760135 + t * 0.5307027145)))
    ) * e
    cdf = jnp.where(v >= 0, 1.0 - tail, tail)
    return v * cdf, cdf + v * (e * 0.3989422804014327)


def layer_kernel(
    ids, seg, x_hbm, cot_hbm, wq, wk, wv, wo_hbm, we_hbm, wc_hbm, g1, b1, g2, b2,
    qd, kd, vd, qu, ku, vu, od_hbm, ou_hbm, ed_hbm, eu_hbm, cd_hbm, cu_hbm,
    out_hbm, grad_hbm, g0, g1_, g2_, g3, h1, h2, h3,
    x, cot, wp, wo, ff, dtab, utab, qkv, heads, bias, lse, xhat, rstd, hidden, slope, acc, recv,
    od, ou, ed, eu, cd, cu, row, back_rank, u_cat, d_cat, lcol, rank_t, rank_e, drow, mine_rk, their_rk, stage_out,
    pick_mine, picks, p0, p1, p2, p3, r0, r1, r2, r3, d0, d1, d2, d3,
    load_sem, send_sem, recv_sem, out_sem, credit, rk_send, rk_recv, pick_send, pick_recv,
    rs_send_sem, rs_recv_sem, z_send, z_recv, plane_send, plane_recv, own_sem, swap_send, swap_recv,
):
    dp = lax.axis_index("dp")
    core = lax.axis_index("tensor")
    partner = (dp, 1 - core)
    first = (core == 0).astype(F32)
    me = lax.rem(dp, GROUP)
    base = dp - me
    half = pl.ds(pl.multiple_of(core * 512, 512), 512)

    wc, we = ff.at[0], ff.at[1]
    d = x.shape[2]

    def load(i, src, dst):
        return pltpu.make_async_copy(src, dst, load_sem.at[i])

    load_x = [load(s, x_hbm.at[s], x.at[s]) for s in range(2)]
    load_d = [load(2 + i, t, dtab.at[i]) for i, t in enumerate((qd, kd, vd))]
    load_u = [load(5 + i, t, utab.at[i]) for i, t in enumerate((qu, ku, vu))]
    load_w = [load(8 + i, t, wp.at[:, pl.ds(512 * i, 512)]) for i, t in enumerate((wq, wk, wv))]
    load_o = [load(11, wo_hbm, wo), load(12, od_hbm, od), load(13, ou_hbm, ou)]
    load_f = [
        load(14, we_hbm.at[:, pl.ds(0, d)], we.at[pl.ds(0, d)]),
        load(15, we_hbm.at[:, pl.ds(d, d)], we.at[pl.ds(d, d)]),
        load(16, ed_hbm, ed), load(17, eu_hbm, eu),
        load(18, wc_hbm, wc), load(19, cd_hbm, cd), load(20, cu_hbm, cu),
    ]
    load_cot = load(21, cot_hbm, cot)
    for cp in load_x[:1] + load_d + load_w + load_u:
        cp.start()

    def peer(k):
        return (base + lax.bitwise_xor(me, k), core)

    barrier = pltpu.get_barrier_semaphore()
    pl.semaphore_signal(barrier, inc=1, device_id=partner, device_id_type=MESH)

    def greet(k, c):
        pl.semaphore_signal(barrier, inc=1, device_id=peer(k), device_id_type=MESH)
        return c

    lax.fori_loop(1, GROUP, greet, 0)

    def remote(src, dst, ss, rs, to):
        return pltpu.make_async_remote_copy(
            src_ref=src, dst_ref=dst, send_sem=ss, recv_sem=rs, device_id=to, device_id_type=MESH
        )

    def pick_copy(k):
        return remote(pick_mine, picks.at[me], pick_send.at[k], pick_recv.at[k], peer(k))

    table_id = lax.broadcasted_iota(jnp.int32, (8, 128), 0)
    for s in range(2):
        pick_mine[s] = (table_id == ids[s]).astype(F32)
    picks[me] = pick_mine[...]

    def send_pick(k, c):
        pick_copy(k).start()
        return c

    def meet():
        pl.semaphore_wait(barrier, GROUP)
        lax.fori_loop(1, GROUP, send_pick, 0)

    def rk_copy(s, i):
        rows = pl.ds(RK[i], RK[i + 1] - RK[i])
        return remote(
            mine_rk.at[s, rows], their_rk.at[s, rows], rk_send.at[s, i], rk_recv.at[s, i], partner
        )

    def rank_sum(s, i):
        rk_copy(s, i).wait()
        at = slice(RK[i], RK[i + 1])
        return mine_rk[s, at, :] + their_rk[s, at, :]

    packs, parts, denses = (p0, p1, p2, p3), (r0, r1, r2, r3), (d0, d1, d2, d3)
    gathered, swapped = (g0, g1_, g2_, g3), (None, h1, h2, h3)

    def pack(g, s, col, v):
        for b in range(v.shape[1] // 128):
            cut, ln = divmod(col + 128 * b, LANES[g])
            for h in range(2):
                packs[g][s, 2 * cut + h, :, ln:ln + 128] = v[8 * h:8 * h + 8, 128 * b:128 * b + 128]

    def shard_copy(g, s, k):
        to = lax.bitwise_xor(me, k)
        return remote(
            packs[g].at[s, to], parts[g].at[me, s], rs_send_sem.at[g, s, k], rs_recv_sem.at[g, s, k], peer(k)
        )

    def scatter(g, s):
        parts[g][me, s] = packs[g][s, me]

        def go(k, c):
            shard_copy(g, s, k).start()
            return c

        lax.fori_loop(1, GROUP, go, 0)

    def combine(g):
        def wait(k, c):
            for s in range(2):
                shard_copy(g, s, k).wait()
            return c

        lax.fori_loop(1, GROUP, wait, 0)

        cuts = range(0, LANES[g], 128)

        def add(m, total):
            for s in range(2):
                part = [parts[g][m, s, :, at:at + 128] for at in cuts]
                for a in range(8):
                    weight = jnp.broadcast_to(picks[m, s, a:a + 1, :], (8, 128))
                    total = [
                        t + weight * part[i % len(cuts)] if i // len(cuts) == a else t
                        for i, t in enumerate(total)
                    ]
            return tuple(total)

        total = lax.fori_loop(0, GROUP, add, (jnp.zeros((8, 128), F32),) * (8 * len(cuts)))
        for i, t in enumerate(total):
            a, at = divmod(i, len(cuts))
            denses[g][a, :, 128 * at:128 * at + 128] = t

    def own_copy(g):
        return pltpu.make_async_copy(denses[g], gathered[g].at[me], own_sem.at[g])

    def z_copy(g, u):
        return remote(denses[g], gathered[g].at[me], z_send.at[g, u], z_recv.at[g, u], peer(4 * u))

    def slot(u, k):
        return lax.bitwise_xor(me, 4 * u + k)

    def plane_copy(g, u, way):
        to = gathered[g].at[slot(u, 0)]
        return remote(
            denses[g] if u == 0 else to, to, plane_send.at[g, u, way], plane_recv.at[g, u, way], peer(way + 1)
        )

    def onward_copy(g, u, way):
        at = gathered[g].at[slot(u, way + 1), pl.ds(4 * way, 4)]
        return remote(at, at, plane_send.at[g, u, 2 + way], plane_recv.at[g, u, 2 + way], peer(2 - way))

    def swap_copy(g, u):
        plane = lax.bitwise_xor(me // 4, u)
        return plane >= 2, remote(
            gathered[g].at[pl.ds(4 * plane, 4)], swapped[g].at[pl.ds(4 * lax.rem(plane, 2), 4)],
            swap_send.at[g, u], swap_recv.at[g, u], partner,
        )

    def gather_first(g):
        own_copy(g).start()
        for u in (1, 2, 3):
            z_copy(g, u).start()
        for way in range(2):
            plane_copy(g, 0, way).start()

    def gather_unit(g, u):
        z_copy(g, u).wait_recv()
        for way in range(2):
            plane_copy(g, u, way).start()

    def gather_onward(g, u):
        for way in range(2):
            plane_copy(g, u, way).wait_recv()
            onward_copy(g, u, way).start()

    def gather_swap(g, u):
        if u == 0:
            own_copy(g).wait()
        for way in range(2):
            onward_copy(g, u, way).wait_recv()
        if g in SWAPPED:
            upper, copy = swap_copy(g, u)

            @pl.when(upper)
            def _():
                copy.start()

    def gather_end(g):
        for u in (1, 2, 3):
            z_copy(g, u).wait_send()
        for u in range(4):
            for way in range(2):
                plane_copy(g, u, way).wait_send()
                onward_copy(g, u, way).wait_send()
            if g in SWAPPED:
                upper, copy = swap_copy(g, u)

                @pl.when(upper)
                def _():
                    copy.wait()

    def gather_begin(g):
        combine(g)
        gather_first(g)

    def gather_step(g, u):
        if u < 4:
            gather_unit(g, u)
        gather_onward(g, u - 1)

    def gather_middle(g):
        for u in (1, 2, 3):
            gather_unit(g, u)
        gather_onward(g, 0)

    def gather_late(g):
        for u in (1, 2, 3):
            gather_onward(g, u)

    def gather_close(g):
        for u in range(4):
            gather_swap(g, u)

    def hosted(here, there, f):
        @pl.when(here == there)
        def _():
            f()

    def exchange(s):
        return pltpu.make_async_remote_copy(
            src_ref=acc.at[s], dst_ref=recv.at[s], send_sem=send_sem.at[s], recv_sem=recv_sem.at[s],
            device_id=partner, device_id_type=MESH,
        )

    def taken(s):
        pl.semaphore_signal(credit.at[s], inc=1, device_id=partner, device_id_type=MESH)

    def send(s):
        pl.semaphore_wait(credit.at[s], 1)
        exchange(s).start()

    n = x.shape[1]
    hw = heads.shape[2]
    pairs = hw // 128
    chunks = hidden.shape[2] // 512
    lane = lax.broadcasted_iota(jnp.int32, (n, 128), 1)
    low_half = lane < HEAD_WIDTH

    u_cat[...] = jnp.zeros_like(u_cat)
    d_cat[...] = jnp.zeros_like(d_cat)

    def stack_tables(aid):
        for p in range(3):
            for r in (0, 64):
                rows = slice(r + RANK * p, r + RANK * p + RANK)
                d_cat[rows, :] = dtab[p, aid]
                u_cat[rows, hw * p:hw * p + hw] = utab[p, aid]

    def twice(t):
        return jnp.concatenate([t, t], axis=0)

    def wide(v, at):
        hi = v.astype(BF16).astype(F32)
        return jnp.where(lax.broadcasted_iota(jnp.int32, v.shape, 1) < at, hi, v - hi).astype(BF16)

    def term(v, right):
        k = v.shape[0]
        hi, lo = split(v)
        both_parts = nn(jnp.concatenate([hi, lo], axis=0), right)
        return both_parts[:k] + both_parts[k:]

    def stage1(s, carry):
        aid = ids[s]
        seg_row = seg[pl.ds(s, 1), :].astype(F32)
        seg_col = jnp.broadcast_to(seg_row, (128, n)).T
        for j in range(n // 128):
            same = seg_col == seg_row[:, j * 128:(j + 1) * 128]
            bias[s, :, j * 128:(j + 1) * 128] = jnp.where(same, 0.0, -1e30)

        @pl.when(s == 0)
        def _():
            for cp in load_x[:1] + load_d + load_u:
                cp.wait()
            for cp in load_x[1:] + load_o:
                cp.start()

        @pl.when(s == 1)
        def _():
            load_x[1].wait()

        stack_tables(aid)
        rank = jnp.where(lane < 64, nt(x[s], d_cat[...]), 0.0)
        rank_t[s] = rank.T[0:3 * RANK, :].astype(BF16)
        rank = rank.astype(BF16)

        @pl.when(s == 0)
        def _():
            for cp in load_f + [load_cot]:
                cp.start()

        def project(p, c):
            at = pl.ds(pl.multiple_of(p * hw, hw), hw)
            for i in range(3):
                hosted(3 * s + p, i, lambda: load_w[i].wait())
            scale = jnp.where(p == 0, 0.125, 1.0)
            qkv[s, p] = ((nn(x[s], wp[:, at]) + nn(rank, u_cat[:, at])) * scale).astype(BF16)
            return c

        lax.fori_loop(0, 3, project, 0)

        def pair(hp, c):
            at = pl.ds(pl.multiple_of(hp * 128, 128), 128)
            k2 = qkv[s, 1, :, at]
            v2 = jnp.concatenate([qkv[s, 2, :, at], jnp.ones((n, 128), BF16)], axis=1)
            for r in range(2):
                rows = slice(r * (n // 2), (r + 1) * (n // 2))
                q2 = qkv[s, 0, rows, at]
                outs = []
                ln = lane[rows]
                for j in range(2):
                    mine = (ln < HEAD_WIDTH) if j == 0 else (ln >= HEAD_WIDTH)
                    score = nt(jnp.where(mine, q2, jnp.zeros_like(q2)), k2) + bias[s, rows, :]
                    top = jnp.max(score, axis=1, keepdims=True)
                    e = jnp.exp(score - top).astype(BF16)
                    parts_ = nn(e, v2)
                    total = parts_[:, 128:]
                    outs.append(parts_[:, :128] / total)
                    old = lcol[rows, :]
                    lcol[rows, :] = jnp.where(ln == 2 * hp + j, top + jnp.log(total), old)
                heads[s, rows, at] = jnp.where(ln < HEAD_WIDTH, outs[0], outs[1]).astype(BF16)
            return c

        lax.fori_loop(0, pairs, pair, 0)
        lse[s] = lcol[...].T[:lse.shape[1], :]

        @pl.when(s == 0)
        def _():
            for cp in load_o:
                cp.wait()
            meet()

        hs = heads[s]
        ro = nt(hs, twice(od[aid]))
        mine_rk[s, 0:RANK, :] = ro.T[0:RANK, :]
        rk_copy(s, 0).start()
        acc[s] = nn(hs, wo[...]) + nn(wide(ro, RANK), twice(ou[aid]))
        exchange(s).start()
        return carry

    lax.fori_loop(0, 2, stage1, 0)

    def stage2(s, carry):
        aid = ids[s]
        exchange(s).wait()

        def norm(i, c):
            rows = pl.ds(pl.multiple_of(i * ROWS, ROWS), ROWS)
            h = x[s, rows, :].astype(F32) + (acc[s, rows, :] + recv[s, rows, :])
            mean = jnp.mean(h, axis=1, keepdims=True)
            h = h - mean
            inv = lax.rsqrt(jnp.mean(h * h, axis=1, keepdims=True) + EPS)
            h = h * inv
            xhat[s, rows, :] = h
            rstd[s, rows, :] = jnp.broadcast_to(inv, (ROWS, 128))
            row[rows, :] = (h * g1[...] + b1[...]).astype(BF16)
            return c

        lax.fori_loop(0, n // ROWS, norm, 0)
        taken(s)
        rank = nt(row[...], ed[aid])
        rank_e[s] = rank.T.astype(BF16)
        rank = rank.astype(BF16)

        def expand(c):
            at = slice(512 * c, 512 * c + 512)
            top, left = divmod(512 * c, d)
            return nn(row[...], we[d * top:d * top + d, left:left + 512]) + nn(rank, eu[aid, :, at])

        before = expand(0)
        for c in range(chunks):
            after = expand(c + 1) if c + 1 < chunks else None
            at = slice(512 * c, 512 * c + 512)
            hid, sl = gelu_parts(before)
            hidden[s, :, at] = hid.astype(BF16)
            slope[s, :, at] = sl.astype(BF16)
            before = after
        rc = nt(hidden[s], twice(cd[aid]))
        mine_rk[s, RANK:2 * RANK, :] = rc.T[0:RANK, :]
        rk_copy(s, 1).start()
        rc = wide(rc, RANK)
        cu2 = twice(cu[aid])
        for c in range(2):
            at = slice(512 * c, 512 * c + 512)
            acc[s, :, at] = nn(hidden[s], wc[:, at]) + nn(rc, cu2[:, at])
        send(s)
        return carry

    for cp in load_f:
        cp.wait()
    lax.fori_loop(0, 2, stage2, 0)

    def put_out(s):
        return pltpu.make_async_copy(stage_out.at[s], out_hbm.at[s], out_sem.at[s])

    def put_grad(s):
        return pltpu.make_async_copy(stage_out.at[s], grad_hbm.at[s], out_sem.at[s])

    def early(s):
        inner = (xhat[s, :, half] * g1[:, half] + b1[:, half]).astype(BF16)
        pack(1, s, 2048, term(rank_sum(s, 2), inner))
        scatter(1, s)

    def stage3(s, carry):
        aid = ids[s]
        exchange(s).wait()

        def norm(i, c):
            rows = pl.ds(pl.multiple_of(i * ROWS, ROWS), ROWS)
            normed = xhat[s, rows, :] * g1[...] + b1[...]
            h = normed + (acc[s, rows, :] + recv[s, rows, :])
            mean = jnp.mean(h, axis=1, keepdims=True)
            h = h - mean
            inv = lax.rsqrt(jnp.mean(h * h, axis=1, keepdims=True) + EPS)
            h = h * inv
            stage_out[s, rows, :] = (h * g2[...] + b2[...]).astype(BF16)
            u = cot[s, rows, :].astype(F32) * g2[...]
            back = inv * (
                u - jnp.mean(u, axis=1, keepdims=True) - h * jnp.mean(u * h, axis=1, keepdims=True)
            )
            acc[s, rows, :] = back * first
            row[rows, :] = back.astype(BF16)
            return c

        lax.fori_loop(0, n // ROWS, norm, 0)
        taken(s)
        put_out(s).start()
        brc = nt(row[...], cu[aid])
        brc_t = brc.T.astype(BF16)
        brc = brc.astype(BF16)
        for c in range(chunks):
            pack(0, s, 512 * c, nn(brc_t, hidden[s, :, 512 * c:512 * c + 512]))
        scatter(0, s)
        pack(1, s, 2560, term(rank_sum(s, 1), row[:, half]))
        re_t = rank_e[s]

        def contract_back(c):
            at = slice(512 * c, 512 * c + 512)
            return nt(row[...], wc[at, :]) + nn(brc, cd[aid, :, at])

        bh = contract_back(0)
        for c in range(chunks):
            after = contract_back(c + 1) if c + 1 < chunks else None
            at = slice(512 * c, 512 * c + 512)
            bb = (bh * slope[s, :, at].astype(F32)).astype(BF16)
            slope[s, :, at] = bb
            pack(1, s, 512 * c, nn(re_t, bb))
            bh = after
            if c == 0:
                hosted(s, 1, lambda: early(0))
        br = nt(slope[s], twice(eu[aid]))
        mine_rk[s, 2 * RANK:3 * RANK, :] = br.T[0:RANK, :]
        rk_copy(s, 2).start()
        br = wide(br, RANK)
        ed2 = twice(ed[aid])
        for c in range(2):
            at = slice(512 * c, 512 * c + 512)
            low = slice(d + 512 * c, d + 512 * c + 512)
            acc[s, :, at] += (
                nt(slope[s, :, 0:d], we[at, :]) + nt(slope[s, :, d:], we[low, :]) + nn(br, ed2[:, at])
            )
        send(s)
        return carry

    def wait_picks(k, c):
        pick_copy(k).wait()
        return c

    lax.fori_loop(1, GROUP, wait_picks, 0)

    load_cot.wait()
    lax.fori_loop(0, 2, stage3, 0)

    early(1)

    def finish(g, s):
        if g == 2:
            pack(2, s, 1536, term(rank_sum(s, 4), x[s, :, half]))
        else:
            t_d = term(rank_sum(s, 3), x[s, :, half])
            pack(3, s, 1024, t_d[0:RANK, :])
            pack(3, s, 1536, t_d[RANK:2 * RANK, :])
        scatter(g, s)

    def stage4(s, carry):
        aid = ids[s]
        exchange(s).wait()

        def norm(i, c):
            rows = pl.ds(pl.multiple_of(i * ROWS, ROWS), ROWS)
            u = (acc[s, rows, :] + recv[s, rows, :]) * g1[...]
            h = xhat[s, rows, :]
            back = rstd[s, rows, 0:1] * (
                u - jnp.mean(u, axis=1, keepdims=True) - h * jnp.mean(u * h, axis=1, keepdims=True)
            )
            acc[s, rows, :] = back * first
            row[rows, :] = back.astype(BF16)
            return c

        lax.fori_loop(0, n // ROWS, norm, 0)
        taken(s)
        hs = heads[s]
        bro = nt(row[...], ou[aid])
        pack(2, s, 0, nn(bro.T.astype(BF16), hs))
        pack(2, s, 1024, term(rank_sum(s, 0), row[:, half]))
        hosted(s, 0, lambda: gather_begin(0))
        hosted(s, 1, lambda: finish(2, 0))
        hosted(s, 1, lambda: gather_middle(0))
        hidden[s, :, 3 * hw:] = (nt(row[...], wo[...]) + nn(bro.astype(BF16), od[aid])).astype(BF16)
        pick = (
            lax.broadcasted_iota(jnp.int32, (RANK, hw), 1) // HEAD_WIDTH
            == lax.broadcasted_iota(jnp.int32, (RANK, hw), 0)
        ).astype(BF16)
        hi, lo = split(hidden[s, :, 3 * hw:].astype(F32) * hs.astype(F32))
        drow[s] = nt(pick, hi) + nt(pick, lo)

        def pair(hp, c):
            at = pl.ds(pl.multiple_of(hp * 128, 128), 128)
            q2 = qkv[s, 0, :, at]
            k2 = qkv[s, 1, :, at]
            do2 = hidden[s, :, pl.ds(pl.multiple_of(3 * hw + hp * 128, 128), 128)]
            dv = []
            for j in range(2):
                mine = low_half if j == 0 else jnp.logical_not(low_half)
                st = nt(jnp.where(mine, k2, jnp.zeros_like(k2)), q2) + bias[s]
                pt = jnp.exp(st - lse[s, pl.ds(2 * hp + j, 1), :]).astype(BF16)
                ff[s, pl.ds(pl.multiple_of(hp * n, n), n), j * n:j * n + n] = pt
                dv.append(nn(pt, do2))
            to = pl.ds(pl.multiple_of(2 * hw + hp * 128, 128), 128)
            hidden[s, :, to] = jnp.where(low_half, dv[0], dv[1]).astype(BF16)
            return c

        lax.fori_loop(0, pairs, pair, 0)
        stack_tables(aid)
        d_v = hidden[s, :, 2 * hw:3 * hw]
        br = nt(d_v, u_cat[:, 2 * hw:3 * hw])
        mine_rk[s, RK[4]:RK[5], :] = br.T[2 * RANK:3 * RANK, :]
        rk_copy(s, 4).start()
        back_rank[s] = wide(br, 64)
        pack(2, s, 512, nn(rank_t[s, 2 * RANK:3 * RANK, :], d_v))
        hosted(s, 0, lambda: gather_begin(1))
        hosted(s, 1, lambda: gather_late(0))
        return carry

    lax.fori_loop(0, 2, stage4, 0)

    def stage4b(s, carry):
        aid = ids[s]

        def pair(hp, c):
            at = pl.ds(pl.multiple_of(hp * 128, 128), 128)
            q2 = qkv[s, 0, :, at]
            k2 = qkv[s, 1, :, at]
            v2 = qkv[s, 2, :, at]
            do2 = hidden[s, :, pl.ds(pl.multiple_of(3 * hw + hp * 128, 128), 128)]
            k2t = k2.T
            dk = []
            for j in range(2):
                mine = low_half if j == 0 else jnp.logical_not(low_half)
                h = 2 * hp + j
                pt = ff[s, pl.ds(pl.multiple_of(hp * n, n), n), j * n:j * n + n].astype(F32)
                dpt = nt(jnp.where(mine, v2, jnp.zeros_like(v2)), do2)
                dst = (pt * (dpt - drow[s, pl.ds(h, 1), :])).astype(BF16)
                dk.append(nn(dst, q2))
                dqt = nn(k2t[j * HEAD_WIDTH:(j + 1) * HEAD_WIDTH, :], dst) * 0.125
                slope[s, pl.ds(pl.multiple_of(h * HEAD_WIDTH, HEAD_WIDTH), HEAD_WIDTH), 0:n] = dqt.astype(BF16)
            to = pl.ds(pl.multiple_of(hw + hp * 128, 128), 128)
            hidden[s, :, to] = jnp.where(low_half, dk[0], dk[1]).astype(BF16)
            for (s_, hp_), f in plan.items():
                hosted(4 * s + hp, 4 * s_ + hp_, f)
            return c

        lax.fori_loop(0, pairs, pair, 0)
        hidden[s, :, 0:hw] = slope[s, 0:hw, 0:n].T
        stack_tables(aid)
        br = nt(hidden[s, :, 0:2 * hw], u_cat[:, 0:2 * hw])
        mine_rk[s, RK[3]:RK[4], :] = br.T[0:2 * RANK, :]
        rk_copy(s, 3).start()
        back_rank[s] += wide(br, 64)
        for p in range(2):
            pack(
                3, s, 512 * p, nn(rank_t[s, RANK * p:RANK * p + RANK, :], hidden[s, :, hw * p:hw * p + hw])
            )
        hosted(s, 0, lambda: gather_begin(2))
        return carry

    plan = {(0, 0): lambda: finish(2, 1), (0, 1): lambda: gather_middle(1), (1, 0): lambda: finish(3, 0), (1, 2): lambda: gather_late(1)}
    lax.fori_loop(0, 2, stage4b, 0)

    def project_back(s, carry):
        stack_tables(ids[s])
        for c in range(2):
            at = slice(512 * c, 512 * c + 512)
            acc[s, :, at] += nt(hidden[s, :, 0:3 * hw], wp[at, :]) + nn(back_rank[s], d_cat[:, at])
        send(s)
        return carry

    def back_step(s, carry):
        project_back(s, carry)
        hosted(s, 0, lambda: finish(3, 1))
        hosted(s, 0, lambda: gather_middle(2))
        return carry

    lax.fori_loop(0, 2, back_step, 0)

    def stage5(s):
        exchange(s).wait()
        put_out(s).wait()

        def add(i, c):
            rows = pl.ds(pl.multiple_of(i * ROWS, ROWS), ROWS)
            stage_out[s, rows, :] = (acc[s, rows, :] + recv[s, rows, :]).astype(BF16)
            return c

        lax.fori_loop(0, n // ROWS, add, 0)
        put_grad(s).start()

    gather_begin(3)
    gather_late(2)
    stage5(0)
    gather_onward(3, 0)
    gather_unit(3, 1)
    stage5(1)
    for g in (0, 1, 2):
        gather_close(g)
    gather_step(3, 2)
    gather_swap(3, 0)
    gather_step(3, 3)
    gather_swap(3, 1)
    gather_step(3, 4)
    gather_swap(3, 2)
    gather_swap(3, 3)
    for g in GROUPS:
        gather_end(g)
    put_grad(0).wait()
    put_grad(1).wait()


def place_kernel(*refs):
    src, dst, src_v, dst_v = refs[:9], refs[9:23], refs[23:32], refs[32:44]
    in_sem, out_sem = refs[44:]
    core = lax.axis_index("tensor")
    loads = [pltpu.make_async_copy(a, b, in_sem.at[i]) for i, (a, b) in enumerate(zip(src, src_v))]
    for cp in loads:
        cp.start()
    ends = []

    def store(v, i):
        cp = pltpu.make_async_copy(v, dst[i], out_sem.at[i])
        cp.start()
        ends.append(cp)

    qd, qu, kd, ku, vd, vu, od, ou, ed, eu, cd, cu = range(12)
    swapped = (None,) + tuple(src_v[4:7])

    def lanes(side, b):
        return pl.ds(pl.multiple_of(side * 512 + 128 * b, 128), 128)

    def fill(g, col, table, count, split_table):
        for b in range(count):
            cut, ln = divmod(col + 128 * b, LANES[g])
            for h in range(2):
                rows = slice(8 * h, 8 * h + 8)
                n, ls = 2 * cut + h, slice(ln, ln + 128)
                v = src_v[g][n, :, :, ls]
                if split_table:
                    dst_v[table][:, rows, lanes(core, b)] = v
                    dst_v[table][:, rows, lanes(1 - core, b)] = swapped[g][n - 8, :, :, ls]
                else:
                    dst_v[table][:, rows, 128 * b:128 * b + 128] = v
        store(dst_v[table], 2 + table)

    loads[0].wait()
    fill(0, 0, cd, 16, False)
    for i in (1, 4):
        loads[i].wait()
    fill(1, 0, eu, 16, False)
    fill(1, 2048, ed, 4, True)
    fill(1, 2560, cu, 4, True)
    for i in (2, 5):
        loads[i].wait()
    fill(2, 0, od, 4, False)
    fill(2, 512, vu, 4, False)
    fill(2, 1024, ou, 4, True)
    fill(2, 1536, vd, 4, True)
    for i in (3, 6):
        loads[i].wait()
    fill(3, 0, qu, 4, False)
    fill(3, 512, ku, 4, False)
    fill(3, 1024, qd, 4, True)
    fill(3, 1536, kd, 4, True)
    for i in range(2):
        loads[7 + i].wait()
        store(src_v[7 + i], i)
    for cp in ends:
        cp.wait()


def place(out, grad, tables, hw, f):
    s, n, d = out.shape
    hbm = pl.BlockSpec(memory_space=pl.ANY)
    widths = (d, hw, d, hw, d, hw, hw, d, d, f, f, d)
    args = (*tables, out, grad)
    return pl.pallas_call(
        place_kernel,
        out_shape=[jax.ShapeDtypeStruct((s, n, d), BF16)] * 2
        + [jax.ShapeDtypeStruct((8, RANK, w), F32) for w in widths],
        in_specs=[hbm] * 9,
        out_specs=[hbm] * 14,
        scratch_shapes=[pltpu.VMEM(a.shape, a.dtype) for a in args]
        + [pltpu.VMEM((8, RANK, w), F32) for w in widths]
        + [pltpu.SemaphoreType.DMA((9,)), pltpu.SemaphoreType.DMA((14,))],
        compiler_params=pltpu.CompilerParams(vmem_limit_bytes=60 * 1024 * 1024),
    )(*args)


def layer(ids, seg, x, cot, wq, wk, wv, wo, we, wc, g1, b1, g2, b2, *tables):
    s, n, d = x.shape
    hw = wq.shape[1]
    f = we.shape[1]
    hbm = pl.BlockSpec(memory_space=pl.ANY)
    vm = pl.BlockSpec(memory_space=pltpu.VMEM)
    sm = pl.BlockSpec(memory_space=pltpu.SMEM)
    sds = jax.ShapeDtypeStruct
    return pl.pallas_call(
        layer_kernel,
        out_shape=(
            sds((s, n, d), BF16), sds((s, n, d), BF16),
            *(sds((GROUP, 8, 8, w), F32) for w in LANES),
            *(sds((GROUP // 2, 8, 8, LANES[g]), F32) for g in SWAPPED),
        ),
        in_specs=[sm, vm, hbm, hbm, hbm, hbm, hbm, hbm, hbm, hbm, vm, vm, vm, vm]
        + [hbm] * 12,
        out_specs=(hbm,) * 9,
        scratch_shapes=[
            pltpu.VMEM((s, n, d), BF16),
            pltpu.VMEM((s, n, d), BF16),
            pltpu.VMEM((d, 3 * hw), BF16),
            pltpu.VMEM((hw, d), BF16),
            pltpu.VMEM((2, f, d), BF16),
            pltpu.VMEM((3, 8, RANK, d), BF16),
            pltpu.VMEM((3, 8, RANK, hw), BF16),
            pltpu.VMEM((s, 3, n, hw), BF16),
            pltpu.VMEM((s, n, hw), BF16),
            pltpu.VMEM((s, n, n), F32),
            pltpu.VMEM((s, RANK, n), F32),
            pltpu.VMEM((s, n, d), F32),
            pltpu.VMEM((s, n, 128), F32),
            pltpu.VMEM((s, n, f), BF16),
            pltpu.VMEM((s, n, f), BF16),
            pltpu.VMEM((s, n, d), F32),
            pltpu.VMEM((s, n, d), F32),
            *(pltpu.VMEM((8, RANK, w), BF16) for w in (hw, d, d, f, f, d)),
            pltpu.VMEM((n, d), BF16),
            pltpu.VMEM((s, n, 128), BF16),
            pltpu.VMEM((128, 3 * hw), BF16),
            pltpu.VMEM((128, d), BF16),
            pltpu.VMEM((n, 128), F32),
            pltpu.VMEM((s, 3 * RANK, n), BF16),
            pltpu.VMEM((s, RANK, n), BF16),
            pltpu.VMEM((s, RANK, n), F32),
            pltpu.VMEM((s, 6 * RANK, n), F32),
            pltpu.VMEM((s, 6 * RANK, n), F32),
            pltpu.VMEM((s, n, d), BF16),
            pltpu.VMEM((s, 8, 128), F32),
            pltpu.VMEM((GROUP, s, 8, 128), F32),
            *(pltpu.VMEM((s, GROUP, 8, w), F32) for w in LANES),
            *(pltpu.VMEM((GROUP, s, 8, w), F32) for w in LANES),
            *(pltpu.VMEM((8, 8, w), F32) for w in LANES),
            pltpu.SemaphoreType.DMA((22,)),
            pltpu.SemaphoreType.DMA((2,)),
            pltpu.SemaphoreType.DMA((2,)),
            pltpu.SemaphoreType.DMA((2,)),
            pltpu.SemaphoreType.REGULAR((2,)),
            *(pltpu.SemaphoreType.DMA((2, 5)),) * 2,
            pltpu.SemaphoreType.DMA((GROUP,)),
            pltpu.SemaphoreType.DMA((GROUP,)),
            *(pltpu.SemaphoreType.DMA((len(LANES), 2, GROUP)),) * 2,
            *(pltpu.SemaphoreType.DMA((len(LANES), 4)),) * 2,
            *(pltpu.SemaphoreType.DMA((len(LANES), 4, 4)),) * 2,
            pltpu.SemaphoreType.DMA((len(LANES),)),
            *(pltpu.SemaphoreType.DMA((len(LANES), 4)),) * 2,
        ],
        compiler_params=pltpu.CompilerParams(
            collective_id=0, has_side_effects=True, vmem_limit_bytes=63 * 1024 * 1024
        ),
    )(ids, seg, x, cot, wq, wk, wv, wo, we, wc, g1, b1, g2, b2, *tables)


def on_device(
    tokens, cotangent, segment_ids, adapter_ids, query_weight, key_weight, value_weight, output_weight,
    expand_weight, contract_weight, first_gain, first_shift, second_gain, second_shift,
    query_down, query_up, key_down, key_up, value_down, value_up, output_down, output_up,
    expand_down, expand_up, contract_down, contract_up,
):
    seqs, length = segment_ids.shape
    width = tokens.shape[1]
    turn = lambda t: jnp.swapaxes(t, 1, 2)
    line = lambda v: v.reshape(1, -1)
    out, grad, *tables = layer(
        adapter_ids, segment_ids,
        tokens.reshape(seqs, length, width), cotangent.reshape(seqs, length, width),
        query_weight, key_weight, value_weight, output_weight, expand_weight, contract_weight,
        line(first_gain), line(first_shift), line(second_gain), line(second_shift),
        turn(query_down), turn(key_down), turn(value_down), query_up, key_up, value_up,
        turn(output_down), output_up, turn(expand_down), expand_up, turn(contract_down), contract_up,
    )
    out, grad, *tables = place(out, grad, tables, query_weight.shape[1], expand_weight.shape[1])
    count = lax.axis_size("dp")
    if count > GROUP:
        across = [list(range(i, count, GROUP)) for i in range(GROUP)]
        tables = lax.psum(tuple(tables), "dp", axis_index_groups=across)
    qd, qu, kd, ku, vd, vu, od, ou, ed, eu, cd, cu = tables
    return (
        out.reshape(tokens.shape), grad.reshape(tokens.shape),
        turn(qd), qu, turn(kd), ku, turn(vd), vu, turn(od), ou, turn(ed), eu, turn(cd), cu,
    )


def solution(mesh):
    cols = P(None, None, "tensor")
    mid = P(None, "tensor", None)
    return jax.shard_map(
        on_device,
        mesh=mesh,
        in_specs=(
            P("dp", None), P("dp", None), P("dp", None), P("dp"),
            P(None, "tensor"), P(None, "tensor"), P(None, "tensor"), P("tensor", None),
            P(None, "tensor"), P("tensor", None), P(), P(), P(), P(),
            P(), cols, P(), cols, P(), cols, mid, P(), P(), cols, mid, P(),
        ),
        out_specs=(
            P("dp", None), P("dp", None), P(), cols, P(), cols, P(), cols, mid, P(), P(), cols, mid, P(),
        ),
        check_vma=False,
    )
```
